128 devices in a mesh: row: 8 (over x, core), col: 16 (over z, y).
Axes of the slice: x: 4, y: 4, z: 4, core: 2. Of those that a mesh axis runs over, the one named last changes fastest.
Arguments:
- surface_head: float32 [512, 4096], P('row', 'col'), may hold values from -6 to 6
- conduct_x: float32 [512, 4096], P('row', 'col'), may hold values from 0.01 to 0.1
- conduct_y: float32 [512, 4096], P('row', 'col'), may hold values from 0.01 to 0.1
- porosity: float32 [512, 4096], P('row', 'col'), may hold values from 0.45 to 1
- rainfall: float32 [512, 4096], P('row', 'col'), may hold values from 0.005 to 0.1
- pipe_head: float32 [32, 32768], P(None, ('row', 'col')), may hold values from -6 to 6
- pipe_class: int32 [32768], P(('row', 'col')), may hold values from 0 to 3
- pipe_up: int32 [32768], P(('row', 'col')), may hold values from 0 to 4095
- pipe_down: int32 [32768], P(('row', 'col')), may hold values from 0 to 4095
- pipe_matrices: float32 [4, 32, 32], replicated
- link_cell: int32 [128, 128, 64], P(('row', 'col')), may hold values from -1 to 16383, as said below
- link_node: int32 [128, 128, 64], P(None, ('row', 'col')), may hold values from -1 to 8191, as said below
- link_coef: float32 [128, 128, 64], P(None, ('row', 'col')), may hold values from 0.05 to 0.4
Outputs:
- surface_out: float32 [512, 4096], P('row', 'col')
- pipe_out: float32 [32, 32768], P(None, ('row', 'col'))
The draws below stay inside these ranges and needn't reach their ends.
Inputs may be any that keep to these rules, and one draw needn't show every extreme that they name: `link_cell`: for each source tile and pipe owner the live slots come first; each is a cell of the source tile counted row by row; the other slots are -1. In every draw some tile sends 64 live slots to some owner. `link_node`: -1 exactly where link_cell is -1 at the same source tile, owner and slot; else a node of the owner's pipes, numbered node * 256 + pipe.
All inputs are finite; a program needn't handle non-finite values.
Results may differ from the reference program's by a relative error of at most 0.00015.
Values sent between devices are 32-bit elements; how exact they have to be, the bound alone decides.
No kernel may reach another device: no remote copies, remote signals or barrier semaphores. Data moves between devices by JAX's collectives and lax.ppermute only.
A program may use at most 64 MiB of HBM per device.

```python
import math
import jax
import jax.numpy as jnp
from jax import lax

CX = 64
CY = 256
P_DEV = 256
CAP = 64
NODES = 32
CLASSES = 4
SWEEPS = 4
STEPS = 3
TILE_COLS = 16
TILES = 128
NX = 512
NY = 4096
GROUP_PIPES = 4096
PIPES = 32768


def link_counts(key):
    base = jax.random.fold_in(key, 11)
    heavy_key = jax.random.fold_in(base, 1)
    light_key = jax.random.fold_in(base, 2)
    source_tile = jnp.arange(TILES, dtype=jnp.int32)[:, None]
    target_tile = jnp.arange(TILES, dtype=jnp.int32)[None, :]
    heavy_load = jax.random.randint(heavy_key, (TILES, TILES), CAP // 2, CAP + 1)
    light_load = jax.random.randint(light_key, (TILES, TILES), 0, CAP // 2 + 1)
    counts = jnp.where(target_tile % 4 == 0, heavy_load, light_load)
    counts = jnp.where((source_tile * 5 + target_tile) % 7 == 0, CAP, counts)
    return counts


def live_slots(key):
    slot_index = jnp.arange(CAP, dtype=jnp.int32)
    return slot_index[None, None, :] < link_counts(key)[:, :, None]


def draw_link_cell(key, part):
    live = live_slots(key)
    values = jax.random.randint(jax.random.fold_in(key, 12), (TILES, TILES, CAP), 0, CX * CY)
    values = values.at[0, 0, 0].set(CX * CY - 1)
    return jnp.where(live, values, -1).astype(jnp.int32)


def draw_link_node(key, part):
    live = live_slots(key)
    values = jax.random.randint(jax.random.fold_in(key, 13), (TILES, TILES, CAP), 0, NODES * P_DEV)
    values = values.at[0, 0, 0].set(NODES * P_DEV - 1)
    return jnp.where(live, values, -1).astype(jnp.int32)


def draw_pipe_matrices(key, part):
    position = jnp.arange(NODES, dtype=jnp.float32)
    distance = jnp.abs(position[:, None] - position[None, :])
    diagonal = jax.random.uniform(jax.random.fold_in(key, 21), (CLASSES, NODES, NODES), jnp.float32, 0.4, 0.6)
    factor = jax.random.uniform(jax.random.fold_in(key, 22), (CLASSES, NODES, NODES), jnp.float32, 0.3, 1.0)
    off_diagonal = factor * 0.1 * jnp.power(0.55, jnp.maximum(distance - 1.0, 0.0))
    return jnp.where(distance == 0.0, diagonal, off_diagonal).astype(jnp.float32)


def set_ends(drawn, stream_key, low, high):
    spot = [jax.random.randint(jax.random.fold_in(stream_key, axis), (), 0, length) for axis, length in enumerate(drawn.shape)]
    longest = drawn.shape.index(max(drawn.shape))
    next_to = spot[:longest] + [(spot[longest] + 1) % drawn.shape[longest]] + spot[longest + 1:]
    return drawn.at[tuple(spot)].set(low).at[tuple(next_to)].set(high)


def steps_of(rng, dims, split, low, largest):
    def one(dim, shards_of):
        heights = jax.random.uniform(jax.random.fold_in(jax.random.fold_in(rng, 6), dim), (shards_of,), jnp.float32, low / len(split), largest / len(split))
        return jnp.repeat(jnp.exp(heights), dims[dim] // shards_of).reshape((-1,) + (1,) * (len(dims) - dim - 1))

    loudness = one(*split[0])
    for cut in split[1:]:
        loudness = loudness * one(*cut)
    return loudness


def scatter_about(key, dims, width, most, pieces=(), held_as=jnp.bfloat16):
    result = jax.random.normal(key, dims, jnp.float32) * width
    if len(pieces) > 0:
        result = steps_of(key, dims, pieces, -0.22, 0.18) * result
    return jnp.clip(result, min=-most, max=most).astype(held_as)


def setup_inputs(seed: int = 0) -> dict:
    keys = jax.random.split(jax.random.key(seed), 14)
    return {
        "surface_head": scatter_about(keys[0], (NX, NY), 1.0, 6.0, ((0, 8), (1, 16)), jnp.float32),
        "conduct_x": jnp.clip(0.01 + 0.09 * jax.random.uniform(keys[1], (NX, NY), jnp.float32) ** steps_of(keys[1], (NX, NY), ((0, 8), (1, 16)), -0.2, 0.2), 0.01, 0.1),
        "conduct_y": jnp.clip(0.01 + 0.09 * jax.random.uniform(keys[2], (NX, NY), jnp.float32) ** steps_of(keys[2], (NX, NY), ((0, 8), (1, 16)), -0.2, 0.2), 0.01, 0.1),
        "porosity": jnp.clip(0.45 + 0.55 * jax.random.uniform(keys[3], (NX, NY), jnp.float32) ** steps_of(keys[3], (NX, NY), ((0, 8), (1, 16)), -0.2, 0.2), 0.45, 1.0),
        "rainfall": jnp.clip(jnp.exp(math.log(0.1) - 2.9957323 * jax.random.uniform(keys[4], (NX, NY), jnp.float32) ** steps_of(keys[4], (NX, NY), ((0, 8), (1, 16)), -0.2, 0.2)), 0.005, 0.1),
        "pipe_head": scatter_about(keys[5], (NODES, PIPES), 1.0, 6.0, ((1, 128),), jnp.float32),
        "pipe_class": set_ends(jax.random.randint(keys[6], (PIPES,), 0, CLASSES), jax.random.fold_in(keys[6], 1), 0, CLASSES - 1).astype(jnp.int32),
        "pipe_up": set_ends(jax.random.randint(keys[7], (PIPES,), 0, GROUP_PIPES), jax.random.fold_in(keys[7], 1), 0, GROUP_PIPES - 1).astype(jnp.int32),
        "pipe_down": set_ends(jax.random.randint(keys[8], (PIPES,), 0, GROUP_PIPES), jax.random.fold_in(keys[8], 1), 0, GROUP_PIPES - 1).astype(jnp.int32),
        "pipe_matrices": draw_pipe_matrices(jax.random.fold_in(keys[13], 71), 0),
        "link_cell": draw_link_cell(jax.random.fold_in(keys[13], 71), 0),
        "link_node": draw_link_node(jax.random.fold_in(keys[13], 71), 0),
        "link_coef": jnp.clip(0.05 + 0.35 * jax.random.uniform(keys[12], (TILES, TILES, CAP), jnp.float32) ** steps_of(keys[12], (TILES, TILES, CAP), ((1, 128),), -0.2, 0.2), 0.05, 0.4),
    }


boundary_gain = 0.5


def sweep_once(center, north, south, west, east, north_gain, south_gain, west_gain, east_gain, inverse, source):
    change = north_gain * (north - center) + south_gain * (south - center) + west_gain * (west - center) + east_gain * (east - center)
    return center + change * inverse + source


def reference(surface_head, conduct_x, conduct_y, porosity, rainfall, pipe_head, pipe_class, pipe_up, pipe_down, pipe_matrices, link_cell, link_node, link_coef):
    inverse = 1.0 / porosity
    north_gain = jnp.pad(conduct_x, ((1, 0), (0, 0)))[:-1, :]
    west_gain = jnp.pad(conduct_y, ((0, 0), (1, 0)))[:, :-1]
    tile_index = jnp.arange(TILES, dtype=jnp.int32)
    cell_live = link_cell >= 0
    cell_safe = jnp.where(cell_live, link_cell, 0).astype(jnp.int32)
    grid_row = (tile_index // TILE_COLS)[:, None, None] * CX + cell_safe // CY
    grid_col = (tile_index % TILE_COLS)[:, None, None] * CY + cell_safe % CY
    node_live = link_node >= 0
    node_safe = jnp.where(node_live, link_node, 0).astype(jnp.int32)
    pipe_row = node_safe // P_DEV
    pipe_col = tile_index[None, :, None] * P_DEV + node_safe % P_DEV
    group_base = (jnp.arange(PIPES, dtype=jnp.int32) // GROUP_PIPES) * GROUP_PIPES
    upper_pipe = group_base + pipe_up
    lower_pipe = group_base + pipe_down
    surface = surface_head
    pipe_state = pipe_head
    for coupling_step in range(STEPS):
        for sweep_index in range(SWEEPS):
            padded = jnp.pad(surface, 1)
            surface = sweep_once(surface, padded[:-2, 1:-1], padded[2:, 1:-1], padded[1:-1, :-2], padded[1:-1, 2:],
                                 north_gain, conduct_x, west_gain, conduct_y, inverse, rainfall)
        sent_heads = jnp.where(cell_live, surface[grid_row, grid_col], 0.0)
        manhole_flow = jnp.where(node_live, link_coef * (sent_heads - pipe_state[pipe_row, pipe_col]), 0.0)
        inflow = jnp.zeros_like(pipe_state).at[pipe_row, pipe_col].add(manhole_flow)
        surface = surface.at[grid_row, grid_col].add(-(manhole_flow * inverse[grid_row, grid_col]))
        balance = pipe_state + inflow
        balance = balance.at[0].add(boundary_gain * pipe_state[-1, upper_pipe])
        balance = balance.at[-1].add(boundary_gain * pipe_state[0, lower_pipe])
        updated = jnp.zeros_like(pipe_state)
        for class_index in range(CLASSES):
            product = jnp.dot(pipe_matrices[class_index], balance, precision=lax.Precision.HIGHEST,
                              preferred_element_type=jnp.float32)
            updated = jnp.where(pipe_class[None, :] == class_index, product, updated)
        pipe_state = updated
    return surface, pipe_state
```

```python
import functools

import jax
import jax.numpy as jnp
from jax import lax
from jax.experimental import pallas as pl
from jax.experimental.pallas import tpu as pltpu
from jax.sharding import PartitionSpec as P

CLASSES = 4
SWEEPS = 4
STEPS = 3
F32 = jnp.float32
BF16 = jnp.bfloat16

boundary_gain = 0.5

HALO_ROWS = 4
HALO_COLS = 12
ZONE = 8


def iota(shape, dim):
    return lax.broadcasted_iota(jnp.int32, shape, dim)


def packed(x):
    return jnp.concatenate([x[:64], x[64:]], axis=1)


def low_halves(block):
    lane = iota((64, 128), 1)
    return jnp.where(lane < 64, block[:64], pltpu.roll(block[64:], 64, 1))


def high_halves(block):
    lane = iota((64, 128), 1)
    return jnp.where(lane < 64, pltpu.roll(block[:64], 64, 1), block[64:])


def paired(low, high):
    lane = iota((64, 128), 1)
    top = jnp.where(lane < 64, low, pltpu.roll(high, 64, 1))
    bottom = jnp.where(lane < 64, pltpu.roll(low, 64, 1), high)
    return jnp.concatenate([top, bottom], axis=0)


def beside(values):
    lane = iota((128, 128), 1)
    both = paired(values, values)
    return jnp.where(lane < 64, pltpu.roll(both, 1, 0), pltpu.roll(both, 127, 0))


def gathered(table_ref, rows, high, low):
    low = jnp.bitwise_and(low, 127)

    found = jnp.zeros(high.shape, F32)
    for row in range(rows):
        line = jnp.broadcast_to(table_ref[row : row + 1, :], high.shape)
        found = jnp.where(high == row, jnp.take_along_axis(line, low, axis=1), found)
    return found


def summed(high_ref, low_ref, value_ref, high_size, low_size):
    rows = high_ref.shape[0]

    def step(index, total):
        start = pl.multiple_of(index * 8, 8)
        high = high_ref[pl.ds(start, 8), :]
        low = low_ref[pl.ds(start, 8), :]
        value = value_ref[pl.ds(start, 8), :]
        coarse = value.astype(BF16).astype(F32)
        fine = value - coarse
        row_hot, coarse_hot, fine_hot = [], [], []
        for j in range(8):
            row_hot.append(
                jnp.where(iota((high_size, 128), 0) == high[j : j + 1], 1.0, 0.0).astype(BF16)
            )
            same = iota((low_size, 128), 0) == low[j : j + 1]
            coarse_hot.append(jnp.where(same, coarse[j : j + 1], 0.0).astype(BF16))
            fine_hot.append(jnp.where(same, fine[j : j + 1], 0.0).astype(BF16))
        row_hot = jnp.concatenate(row_hot, axis=1)
        value_hot = jnp.concatenate(
            [jnp.concatenate(coarse_hot, axis=1), jnp.concatenate(fine_hot, axis=1)], axis=0
        )
        return total + lax.dot_general(
            row_hot, value_hot, (((1,), (1,)), ((), ())), preferred_element_type=F32
        )

    total = lax.fori_loop(0, rows // 8, step, jnp.zeros((high_size, 2 * low_size), F32))
    return total


def cell_place(cell):
    high = jnp.where(
        cell >= 0, jnp.bitwise_and(cell >> 7, 1) * 64 + (cell >> 8), -1
    )
    return high, jnp.bitwise_and(cell, 127)


def node_place(node):
    high = jnp.where(
        node >= 0, jnp.bitwise_and(node >> 7, 1) * 32 + (node >> 8), -1
    )
    return high, jnp.bitwise_and(node, 127)


def pipe_table(state):
    return jnp.concatenate([state[:, :128], state[:, 128:]], axis=0)


def pack_rows_kernel(place_ref, surface, cond_x, cond_y, porosity, rainfall, pipes, out):
    row = place_ref[0]
    fields = [surface[...], cond_x[...], cond_y[...], 1.0 / porosity[...], rainfall[...]]
    ends = pipe_table(pipes[...])
    ends = [ends[0:1], ends[32:33], ends[31:32], ends[63:64]]
    for target in range(8):
        upward = target < row
        for index, field in enumerate(fields):
            strip = jnp.where(upward, field[:4], field[60:])
            out[target, pl.ds(index * 8, 4), :] = strip[:, :128]
            out[target, pl.ds(index * 8 + 4, 4), :] = strip[:, 128:]
        out[target, pl.ds(40, 8), :] = jnp.broadcast_to(ends[target % 4], (8, 128))


def neighbours(place_ref):
    row = place_ref[0]
    above, below = jnp.maximum(row - 1, 0), jnp.minimum(row + 1, 7)
    return above, below, row > 0, row < 7


def pack_cols_kernel(
    place_ref, got, surface, cond_x, cond_y, porosity, rainfall, link_cell, fields_out, out
):
    above, below, has_above, has_below = neighbours(place_ref)
    fields = [surface[...], cond_x[...], cond_y[...], 1.0 / porosity[...], rainfall[...]]
    lane = iota((72, 128), 1)
    message = jnp.zeros((72, 128), F32)
    for index, field in enumerate(fields):
        over = got[above, pl.ds(index * 8, 8), :]
        under = got[below, pl.ds(index * 8, 8), :]
        over = jnp.where(has_above, over, 0.0)
        under = jnp.where(has_below, under, 0.0)
        tall = [
            jnp.concatenate([field[:, half * 128 : half * 128 + 128],
                             under[half * 4 : half * 4 + 4], over[half * 4 : half * 4 + 4]], axis=0)
            for half in range(2)
        ]
        fields_out[index, :, 0:128] = tall[0]
        fields_out[index, :, 128:256] = tall[1]
        edges = jnp.where(
            lane < HALO_COLS, tall[0], jnp.where(lane >= 128 - HALO_COLS, tall[1], 0.0)
        )
        if index:
            edges = pltpu.roll(edges, index * 2 * HALO_COLS, 1)
        message = message + edges
    out[0:72, :] = message
    out[72:136, :] = packed(link_cell[...]).astype(F32)


def swept(state, gains):
    def once(_, w):
        return (
            gains[0] * w
            + gains[1] * pltpu.roll(w, 1, 0)
            + gains[2] * pltpu.roll(w, 71, 0)
            + gains[3] * pltpu.roll(w, 1, 1)
            + gains[4] * pltpu.roll(w, 383, 1)
            + gains[5]
        )

    for i in range(SWEEPS):
        state = once(i, state)
    return state


def build_message(out, heads, nodes, got, ends_at):
    out[:, 0:128] = paired(heads, nodes)
    out[:, 128:256] = beside(nodes)
    for source in range(8):
        out[pl.ds(source * 16, 16), 256:384] = jnp.broadcast_to(
            got[source, pl.ds(ends_at, 1), :], (16, 128)
        )


def zone_heads(edge, zone_place, edge_ref, zone_ref):
    lane = iota((64, 128), 1)
    edge_ref[...] = jnp.where(lane < ZONE, edge, pltpu.roll(edge, 2 * ZONE, 1))
    lane8 = iota((8, 128), 1)
    table = jnp.zeros((8, 128), F32)
    for s in range(8):
        line = edge_ref[pl.ds(s, 8, stride=8), :]
        if s:
            line = pltpu.roll(line, s * 16, 1)
        table = jnp.where((lane8 >> 4) == s, line, table)
    zone_ref[...] = table
    zone_row, zone_col = zone_place
    high = jnp.where(zone_row >= 0, zone_row >> 3, -1)
    low = jnp.bitwise_and(zone_row, 7) * 16 + zone_col
    return gathered(zone_ref, 8, high, low)


def sweep_and_gather(
    state, gains, cell_place_, node_place_, zone_place, table, surface_out, heads_out, zone_out,
    nodes_out, cell_table, edge_ref, zone_ref,
):
    state = swept(state, gains)
    surface_out[...] = state[:64]
    cell_table[0:64, :] = state[:64, 0:128]
    cell_table[64:128, :] = state[:64, 128:256]
    heads = gathered(cell_table, 128, *cell_place_)
    heads_out[...] = heads
    if zone_place is not None:
        zone_out[...] = zone_heads(state[:64, 256:384], zone_place, edge_ref, zone_ref)
    nodes = gathered(table, 64, *node_place_)
    nodes_out[...] = nodes
    return heads, nodes


def first_sweep_kernel(
    fields, from_west, from_east, got, link_cell, link_node, link_coef, pipes,
    gains_out, inverse_out, zone_row_out, zone_col_out, surface_out, heads_out, zone_out, nodes_out,
    table_out, out, cell_table, edge_ref, zone_ref,
):
    lane = iota((72, 128), 1)
    wide = []
    for index in range(5):
        west, east = from_west[0:72, :], from_east[0:72, :]
        if index:
            west = pltpu.roll(west, 128 - index * 2 * HALO_COLS, 1)
            east = pltpu.roll(east, 128 - index * 2 * HALO_COLS, 1)
        edge = jnp.where(
            lane < HALO_COLS, east, jnp.where(lane >= 128 - HALO_COLS, west, 0.0)
        )
        wide.append(jnp.concatenate([fields[index], edge], axis=1))
    state, cond_x, cond_y, inverse, rainfall = wide
    north = pltpu.roll(cond_x, 1, 0)
    west = pltpu.roll(cond_y, 1, 1)
    gains = [
        1.0 - (north + cond_x + west + cond_y) * inverse,
        north * inverse, cond_x * inverse, west * inverse, cond_y * inverse, rainfall,
    ]
    for index, gain in enumerate(gains):
        gains_out[index] = gain
    inverse_out[...] = inverse[:64]
    west_cell = from_west[72:136, :].astype(jnp.int32)
    east_cell = from_east[72:136, :].astype(jnp.int32)
    cells = paired(west_cell, east_cell)
    col = jnp.bitwise_and(cells, 255)
    is_west = iota((128, 128), 1) < 64
    inside = jnp.where(is_west, jnp.where(col >= 256 - ZONE, 1, 0), jnp.where(col < ZONE, 1, 0))
    zone_row = jnp.where((cells >= 0) & (inside == 1), cells >> 8, -1)
    zone_col = jnp.where(is_west, col - (256 - 2 * ZONE), col)
    zone_row_out[...] = zone_row
    zone_col_out[...] = zone_col
    table_out[...] = pipe_table(pipes[...])
    heads, nodes = sweep_and_gather(
        state, gains, cell_place(packed(link_cell[...])), node_place(packed(link_node[...])),
        (zone_row, zone_col), table_out, surface_out, heads_out, zone_out, nodes_out,
        cell_table, edge_ref, zone_ref,
    )
    build_message(out, heads, nodes, got, 40)
    coef = packed(link_coef[...])
    out[:, 384:512] = paired(coef, coef)
    out[:, 512:640] = beside(coef)


def sweep_kernel(
    place_ref, surface, got, gains_ref, link_cell, link_node, zone_row, zone_col, table,
    surface_out, heads_out, zone_out, nodes_out, out, cell_table, edge_ref, zone_ref,
):
    above, below, has_above, has_below = neighbours(place_ref)
    over = jnp.where(has_above, got[above, pl.ds(0, 16), :], 0.0)
    under = jnp.where(has_below, got[below, pl.ds(0, 16), :], 0.0)
    columns = []
    for block in range(3):
        columns.append(
            jnp.concatenate(
                [surface[:, block * 128 : block * 128 + 128],
                 under[block * 4 : block * 4 + 4], over[block * 4 : block * 4 + 4]], axis=0
            )
        )
    state = jnp.concatenate(columns, axis=1)
    gains = [gains_ref[index] for index in range(6)]
    heads, nodes = sweep_and_gather(
        state, gains, cell_place(packed(link_cell[...])), node_place(packed(link_node[...])),
        (zone_row[...], zone_col[...]), table, surface_out, heads_out, zone_out, nodes_out,
        cell_table, edge_ref, zone_ref,
    )
    build_message(out, heads, nodes, got, 12)


def update_kernel(
    first, last,
    place_ref, got, surface, inverse, heads, zone, nodes, link_cell, link_node, link_coef,
    zone_row, zone_col, table, meets, classes, matrices, *rest,
):
    rest = list(rest)
    if first:
        own_coef = low_halves(got[:, 384:512])
        zone_coef = got[:, 512:640]
    else:
        own_coef = rest.pop(0)[...]
        zone_coef = rest.pop(0)[...]
    if last:
        surface_out, pipes_out = rest[:2]
        rest = rest[2:]
    else:
        surface_out, table_out, out = rest[:3]
        rest = rest[3:]
        if first:
            rest[0][...] = own_coef
            rest[1][...] = zone_coef
            rest = rest[2:]
    high_ref, low_ref, value_ref, zone_value_ref = rest
    row = place_ref[0]
    block = got[:, 0:128]
    high, low = cell_place(packed(link_cell[...]))
    high_ref[...] = high
    low_ref[...] = low
    value_ref[...] = jnp.where(high >= 0, own_coef * (heads[...] - high_halves(block)), 0.0)
    lost = summed(high_ref, low_ref, value_ref, 128, 128)
    lost = lost[:, :128] + lost[:, 128:]
    left = surface[:, 0:128] - inverse[:, 0:128] * lost[:64]
    right = surface[:, 128:256] - inverse[:, 128:256] * lost[64:]
    surface_out[:, 0:128] = left
    surface_out[:, 128:256] = right
    if not last:
        zone_value_ref[...] = jnp.where(
            zone_row[...] >= 0, zone_coef * (zone[...] - got[:, 128:256]), 0.0
        )
        lost = summed(zone_row, zone_col, zone_value_ref, 64, 64)
        lost = lost[:, :64] + lost[:, 64:]
        lost = jnp.concatenate([lost, jnp.zeros((64, 64), F32)], axis=1)
        lane = iota((64, 128), 1)
        lost = jnp.where(
            lane < ZONE, lost,
            jnp.where(lane >= 128 - ZONE, pltpu.roll(lost, 128 - 2 * ZONE, 1), 0.0),
        )
        edge = surface[:, 256:384] - inverse[:, 256:384] * lost
        surface_out[:, 256:384] = edge
    high, low = node_place(packed(link_node[...]))
    high_ref[...] = high
    low_ref[...] = low
    value_ref[...] = jnp.where(
        high >= 0, packed(link_coef[...]) * (low_halves(block) - nodes[...]), 0.0
    )
    inflow = summed(high_ref, low_ref, value_ref, 64, 128)
    balance = table[...] + (inflow[:, :128] + inflow[:, 128:])
    meet = meets[...]
    meet_row = iota((8, 128), 0)
    meet_high = jnp.bitwise_and(meet >> 7, 1) * 16 + (meet >> 8)
    meet_high = jnp.where(meet_row < 2, meet_high + 32, meet_high)
    met = gathered(got.at[:, 256:384], 64, meet_high, meet) * boundary_gain
    node_row = iota((32, 128), 0)
    parts = []
    for half in range(2):
        part = balance[half * 32 : half * 32 + 32]
        part = part + jnp.where(
            node_row == 0, met[half : half + 1],
            jnp.where(node_row == 31, met[2 + half : 3 + half], 0.0),
        )
        products = jnp.dot(
            matrices[...], part, precision=lax.Precision.HIGHEST, preferred_element_type=F32
        )
        kind = classes[half : half + 1, :]
        updated = jnp.zeros((32, 128), F32)
        for index in range(CLASSES):
            updated = jnp.where(kind == index, products[index * 32 : index * 32 + 32], updated)
        parts.append(updated)
    if last:
        pipes_out[:, 0:128] = parts[0]
        pipes_out[:, 128:256] = parts[1]
        return
    table_out[0:32, :] = parts[0]
    table_out[32:64, :] = parts[1]
    ends = [parts[0][0:1], parts[1][0:1], parts[0][31:32], parts[1][31:32]]
    blocks = [left, right, edge]
    for target in range(8):
        upward = target < row
        for index, field in enumerate(blocks):
            out[target, pl.ds(index * 4, 4), :] = jnp.where(upward, field[:4], field[60:])
        out[target, pl.ds(12, 4), :] = jnp.broadcast_to(ends[target % 4], (4, 128))


def shape(*dims, dtype=F32):
    return jax.ShapeDtypeStruct(dims, dtype)


def call(kernel, inputs, outputs, scratch=(), scalars=1):
    smem = pl.BlockSpec(memory_space=pltpu.SMEM)
    vmem = pl.BlockSpec(memory_space=pltpu.VMEM)
    return pl.pallas_call(
        kernel,
        out_shape=outputs,
        in_specs=[smem] * scalars + [vmem] * (len(inputs) - scalars),
        out_specs=[vmem] * len(outputs),
        scratch_shapes=list(scratch),
        compiler_params=pltpu.CompilerParams(vmem_limit_bytes=32 << 20),
    )(*inputs)


def along(block, axis, distance):
    devices = range(lax.axis_size(axis))
    route = [(i, i + distance) for i in devices if i + distance in devices]
    return lax.ppermute(block, axis, route)


def body(
    surface_head, conduct_x, conduct_y, porosity, rainfall, pipe_head, pipe_class, pipe_up,
    pipe_down, pipe_matrices, link_cell, link_node, link_coef,
):
    place = lax.axis_index("row").astype(jnp.int32).reshape(1)
    link_cell = link_cell[0]
    link_node = link_node[:, 0, :]
    link_coef = link_coef[:, 0, :]
    meets = jnp.concatenate(
        [pipe_up.reshape(2, 128), pipe_down.reshape(2, 128), jnp.zeros((4, 128), jnp.int32)], axis=0
    )
    classes = pipe_class.reshape(2, 128)
    matrices = pipe_matrices.reshape(CLASSES * 32, 32)
    fields = (surface_head, conduct_x, conduct_y, porosity, rainfall)

    (sent,) = call(pack_rows_kernel, (place, *fields, pipe_head), [shape(8, 48, 128)])
    got = lax.all_to_all(sent, "row", split_axis=0, concat_axis=0, tiled=True)
    tall, sent = call(
        pack_cols_kernel, (place, got, *fields, link_cell), [shape(5, 72, 256), shape(136, 128)]
    )
    from_west = along(sent, "col", 1)
    from_east = along(sent, "col", -1)
    gather_scratch = [pltpu.VMEM((128, 128), F32), pltpu.VMEM((64, 128), F32), pltpu.VMEM((8, 128), F32)]
    sum_scratch = [
        pltpu.VMEM((64, 128), jnp.int32), pltpu.VMEM((64, 128), jnp.int32),
        pltpu.VMEM((64, 128), F32), pltpu.VMEM((128, 128), F32),
    ]
    swept_shapes = [shape(64, 384), shape(64, 128), shape(128, 128), shape(64, 128)]
    gains, inverse, zone_row, zone_col, surface, heads, zone, nodes, table, sent = call(
        first_sweep_kernel,
        (tall, from_west, from_east, got, link_cell, link_node, link_coef, pipe_head),
        [shape(6, 72, 384), shape(64, 384), shape(128, 128, dtype=jnp.int32),
         shape(128, 128, dtype=jnp.int32), *swept_shapes, shape(64, 128), shape(128, 640)],
        gather_scratch, scalars=0,
    )
    coefs = ()
    for step in range(STEPS):
        if step:
            surface, heads, zone, nodes, sent = call(
                sweep_kernel,
                (place, surface, got, gains, link_cell, link_node, zone_row, zone_col, table),
                [*swept_shapes, shape(128, 384)], gather_scratch,
            )
        got = lax.all_to_all(sent, ("row", "col"), split_axis=0, concat_axis=0, tiled=True)
        last = step == STEPS - 1
        outputs = [shape(64, 256), shape(32, 256)] if last else [
            shape(64, 384), shape(64, 128), shape(8, 16, 128)
        ]
        if not step:
            outputs += [shape(64, 128), shape(128, 128)]
        done = call(
            functools.partial(update_kernel, step == 0, last),
            (place, got, surface, inverse, heads, zone, nodes, link_cell, link_node, link_coef,
             zone_row, zone_col, table, meets, classes, matrices, *coefs),
            outputs, sum_scratch,
        )
        if last:
            return tuple(done)
        surface, table, sent = done[:3]
        if not step:
            coefs = tuple(done[3:])
        got = lax.all_to_all(sent, "row", split_axis=0, concat_axis=0, tiled=True)


def solution(mesh):
    placed = (
        P("row", "col"),
        P("row", "col"),
        P("row", "col"),
        P("row", "col"),
        P("row", "col"),
        P(None, ("row", "col")),
        P(("row", "col")),
        P(("row", "col")),
        P(("row", "col")),
        P(),
        P(("row", "col"), None, None),
        P(None, ("row", "col"), None),
        P(None, ("row", "col"), None),
    )
    return jax.shard_map(
        body,
        mesh=mesh,
        in_specs=placed,
        out_specs=(P("row", "col"), P(None, ("row", "col"))),
        check_vma=False,
    )
```

```python
import functools

import jax
import jax.numpy as jnp
from jax import lax
from jax.experimental import pallas as pl
from jax.experimental.pallas import tpu as pltpu
from jax.sharding import PartitionSpec as P

CLASSES = 4
SWEEPS = 4
STEPS = 3
F32 = jnp.float32
BF16 = jnp.bfloat16

boundary_gain = 0.5

HALO_ROWS = 4
HALO_COLS = 12
ZONE = 8
ENDS = (0, 32, 31, 63)


def iota(shape, dim):
    return lax.broadcasted_iota(jnp.int32, shape, dim)


def packed(x):
    return jnp.concatenate([x[:64], x[64:]], axis=1)


def low_halves(block):
    lane = iota((64, 128), 1)
    return jnp.where(lane < 64, block[:64], pltpu.roll(block[64:], 64, 1))


def high_halves(block):
    lane = iota((64, 128), 1)
    return jnp.where(lane < 64, pltpu.roll(block[:64], 64, 1), block[64:])


def paired(low, high):
    lane = iota((64, 128), 1)
    top = jnp.where(lane < 64, low, pltpu.roll(high, 64, 1))
    bottom = jnp.where(lane < 64, pltpu.roll(low, 64, 1), high)
    return jnp.concatenate([top, bottom], axis=0)


def beside(values):
    lane = iota((128, 128), 1)
    both = paired(values, values)
    return jnp.where(lane < 64, pltpu.roll(both, 1, 0), pltpu.roll(both, 127, 0))


def gathered(table_ref, rows, high, low):
    low = jnp.bitwise_and(low, 127)

    found = jnp.zeros(high.shape, F32)
    for row in range(rows):
        line = jnp.broadcast_to(table_ref[row : row + 1, :], high.shape)
        found = jnp.where(high == row, jnp.take_along_axis(line, low, axis=1), found)
    return found


def summed(high_ref, low_ref, value_ref, high_size, low_size):
    rows = high_ref.shape[0]

    def step(index, total):
        start = pl.multiple_of(index * 8, 8)
        high = high_ref[pl.ds(start, 8), :]
        low = low_ref[pl.ds(start, 8), :]
        value = value_ref[pl.ds(start, 8), :]
        coarse = value.astype(BF16).astype(F32)
        fine = value - coarse
        row_hot, coarse_hot, fine_hot = [], [], []
        for j in range(8):
            row_hot.append(
                jnp.where(iota((high_size, 128), 0) == high[j : j + 1], 1.0, 0.0).astype(BF16)
            )
            same = iota((low_size, 128), 0) == low[j : j + 1]
            coarse_hot.append(jnp.where(same, coarse[j : j + 1], 0.0).astype(BF16))
            fine_hot.append(jnp.where(same, fine[j : j + 1], 0.0).astype(BF16))
        row_hot = jnp.concatenate(row_hot, axis=1)
        value_hot = jnp.concatenate(
            [jnp.concatenate(coarse_hot, axis=1), jnp.concatenate(fine_hot, axis=1)], axis=0
        )
        return total + lax.dot_general(
            row_hot, value_hot, (((1,), (1,)), ((), ())), preferred_element_type=F32
        )

    total = lax.fori_loop(0, rows // 8, step, jnp.zeros((high_size, 2 * low_size), F32))
    return total


def cell_place(cell):
    high = jnp.where(
        cell >= 0, jnp.bitwise_and(cell >> 7, 1) * 64 + (cell >> 8), -1
    )
    return high, jnp.bitwise_and(cell, 127)


def node_place(node):
    high = jnp.where(
        node >= 0, jnp.bitwise_and(node >> 7, 1) * 32 + (node >> 8), -1
    )
    return high, jnp.bitwise_and(node, 127)


def pipe_table(state):
    return jnp.concatenate([state[:, :128], state[:, 128:]], axis=0)


def strips(blocks, start):
    return jnp.concatenate([block[start : start + HALO_ROWS] for block in blocks], axis=0)


def start_kernel(surface, cond_x, cond_y, porosity, rainfall, fields, up, down, arrived):
    copies = [
        pltpu.make_async_copy(source, fields.at[index], arrived.at[index])
        for index, source in enumerate((surface, cond_x, cond_y, porosity, rainfall))
    ]
    for copy in copies:
        copy.start()
    for copy in copies:
        copy.wait()
    fields[3] = 1.0 / fields[3]
    for index in range(5):
        halves = [fields[index, :, 0:128], fields[index, :, 128:256]]
        up[pl.ds(index * 8, 8), :] = strips(halves, 0)
        down[pl.ds(index * 8, 8), :] = strips(halves, 60)


def tall_block(place_ref, block, above, below, start):
    over = jnp.where(place_ref[0] > 0, above[start : start + 4, :], 0.0)
    under = jnp.where(place_ref[0] < 7, below[start : start + 4, :], 0.0)
    return jnp.concatenate([block, under, over], axis=0)


def pack_cols_kernel(place_ref, above, below, fields, link_cell, tall_out, out):
    lane = iota((72, 128), 1)
    message = jnp.zeros((72, 128), F32)
    for index in range(5):
        tall = [
            tall_block(
                place_ref, fields[index, :, half * 128 : half * 128 + 128], above, below,
                index * 8 + half * 4,
            )
            for half in range(2)
        ]
        tall_out[index, :, 0:128] = tall[0]
        tall_out[index, :, 128:256] = tall[1]
        edges = jnp.where(
            lane < HALO_COLS, tall[0], jnp.where(lane >= 128 - HALO_COLS, tall[1], 0.0)
        )
        if index:
            edges = pltpu.roll(edges, index * 2 * HALO_COLS, 1)
        message = message + edges
    out[0:72, :] = message
    out[72:136, :] = packed(link_cell[...]).astype(F32)


def owner_start_kernel(
    pipes, link_node, link_coef, table, nodes, node_high, node_low, coef
):
    table[...] = pipe_table(pipes[...])
    high, low = node_place(packed(link_node[...]))
    node_high[...] = high
    node_low[...] = low
    coef[...] = packed(link_coef[...])
    nodes[...] = gathered(table, 64, high, low)


def swept(state, gains):
    def once(_, w):
        return (
            gains[0] * w
            + gains[1] * pltpu.roll(w, 1, 0)
            + gains[2] * pltpu.roll(w, 71, 0)
            + gains[3] * pltpu.roll(w, 1, 1)
            + gains[4] * pltpu.roll(w, 383, 1)
            + gains[5]
        )

    for i in range(SWEEPS):
        state = once(i, state)
    return state


def build_message(out, heads, nodes, table):
    out[:, 0:128] = paired(heads, nodes)
    out[:, 128:256] = beside(nodes)
    for index, row in enumerate(ENDS):
        block = jnp.broadcast_to(table[row : row + 1, :], (128, 128))
        out[:, 256 + index * 128 : 384 + index * 128] = block


def zone_heads(edge, zone_place, edge_ref, zone_ref):
    lane = iota((64, 128), 1)
    edge_ref[...] = jnp.where(lane < ZONE, edge, pltpu.roll(edge, 2 * ZONE, 1))
    lane8 = iota((8, 128), 1)
    table = jnp.zeros((8, 128), F32)
    for s in range(8):
        line = edge_ref[pl.ds(s, 8, stride=8), :]
        if s:
            line = pltpu.roll(line, s * 16, 1)
        table = jnp.where((lane8 >> 4) == s, line, table)
    zone_ref[...] = table
    zone_row, zone_col = zone_place
    high = jnp.where(zone_row >= 0, zone_row >> 3, -1)
    low = jnp.bitwise_and(zone_row, 7) * 16 + zone_col
    return gathered(zone_ref, 8, high, low)


def sweep_and_gather(
    state, gains, cell_high, cell_low, zone_place, surface_out, heads_out, zone_out, cell_table,
    edge_ref, zone_ref,
):
    state = swept(state, gains)
    surface_out[...] = state[:64]
    cell_table[0:64, :] = state[:64, 0:128]
    cell_table[64:128, :] = state[:64, 128:256]
    heads = gathered(cell_table, 128, cell_high, cell_low)
    heads_out[...] = heads
    if zone_place is not None:
        zone_out[...] = zone_heads(state[:64, 256:384], zone_place, edge_ref, zone_ref)
    return heads


def first_sweep_kernel(
    place_ref, tall, from_west, from_east, link_cell, table, nodes, coef,
    gains_out, inverse_out, cell_high, cell_low, zone_row_out, zone_col_out, surface_out, heads_out,
    zone_out, out, cell_table, edge_ref, zone_ref,
):
    lane = iota((72, 128), 1)
    wide = []
    for index in range(5):
        west = jnp.where(place_ref[1] > 0, from_west[0:72, :], 0.0)
        east = jnp.where(place_ref[1] < 15, from_east[0:72, :], 0.0)
        if index:
            west = pltpu.roll(west, 128 - index * 2 * HALO_COLS, 1)
            east = pltpu.roll(east, 128 - index * 2 * HALO_COLS, 1)
        edge = jnp.where(
            lane < HALO_COLS, east, jnp.where(lane >= 128 - HALO_COLS, west, 0.0)
        )
        wide.append(jnp.concatenate([tall[index], edge], axis=1))
    state, cond_x, cond_y, inverse, rainfall = wide
    north = pltpu.roll(cond_x, 1, 0)
    west = pltpu.roll(cond_y, 1, 1)
    gains = [
        1.0 - (north + cond_x + west + cond_y) * inverse,
        north * inverse, cond_x * inverse, west * inverse, cond_y * inverse, rainfall,
    ]
    for index, gain in enumerate(gains):
        gains_out[index] = gain
    inverse_out[...] = inverse[:64]
    cells = paired(from_west[72:136, :], from_east[72:136, :]).astype(jnp.int32)
    col = jnp.bitwise_and(cells, 255)
    is_west = iota((128, 128), 1) < 64
    zone_col = jnp.where(is_west, col - (256 - 2 * ZONE), col)
    inside = (zone_col >= 0) & (zone_col < 2 * ZONE)
    inside = inside & (jnp.where(is_west, zone_col, zone_col + ZONE) >= ZONE)
    zone_row = jnp.where((cells >= 0) & inside & (jnp.where(is_west, 0, zone_col) < ZONE), cells >> 8, -1)
    zone_row_out[...] = zone_row
    zone_col_out[...] = zone_col
    high, low = cell_place(packed(link_cell[...]))
    cell_high[...] = high
    cell_low[...] = low
    heads = sweep_and_gather(
        state, gains, high, low, (zone_row, zone_col), surface_out, heads_out, zone_out,
        cell_table, edge_ref, zone_ref,
    )
    build_message(out, heads, nodes[...], table)
    out[:, 768:896] = paired(coef[...], coef[...])
    out[:, 896:1024] = beside(coef[...])


def sweep_kernel(
    last, place_ref, surface, above, below, gains_ref, cell_high, cell_low, zone_row, zone_col,
    table, nodes, surface_out, heads_out, zone_out, out, cell_table, edge_ref, zone_ref,
):
    state = jnp.concatenate(
        [
            tall_block(
                place_ref, surface[:, block * 128 : block * 128 + 128], above, below, block * 4
            )
            for block in range(3)
        ],
        axis=1,
    )
    gains = [gains_ref[index] for index in range(6)]
    zone_place = None if last else (zone_row[...], zone_col[...])
    heads = sweep_and_gather(
        state, gains, cell_high[...], cell_low[...], zone_place, surface_out, heads_out, zone_out,
        cell_table, edge_ref, zone_ref,
    )
    build_message(out, heads, nodes[...], table)


def tile_kernel(
    first, last, got, surface, inverse, heads, zone, cell_high, cell_low, zone_row, zone_col, *rest
):
    rest = list(rest)
    if first:
        own_coef = low_halves(got[:, 768:896])
        zone_coef = got[:, 896:1024]
    else:
        own_coef = rest.pop(0)[...]
        zone_coef = rest.pop(0)[...]
    surface_out = rest.pop(0)
    if not last:
        up, down = rest.pop(0), rest.pop(0)
    if first:
        rest.pop(0)[...] = own_coef
        rest.pop(0)[...] = zone_coef
    value_ref, zone_value_ref = rest
    value_ref[...] = jnp.where(
        cell_high[...] >= 0, own_coef * (heads[...] - high_halves(got[:, 0:128])), 0.0
    )
    lost = summed(cell_high, cell_low, value_ref, 128, 128)
    lost = lost[:, :128] + lost[:, 128:]
    left = surface[:, 0:128] - inverse[:, 0:128] * lost[:64]
    right = surface[:, 128:256] - inverse[:, 128:256] * lost[64:]
    surface_out[:, 0:128] = left
    surface_out[:, 128:256] = right
    if last:
        return
    zone_value_ref[...] = jnp.where(
        zone_row[...] >= 0, zone_coef * (zone[...] - got[:, 128:256]), 0.0
    )
    lost = summed(zone_row, zone_col, zone_value_ref, 64, 64)
    lost = lost[:, :64] + lost[:, 64:]
    lost = jnp.concatenate([lost, jnp.zeros((64, 64), F32)], axis=1)
    lane = iota((64, 128), 1)
    lost = jnp.where(
        lane < ZONE, lost,
        jnp.where(lane >= 128 - ZONE, pltpu.roll(lost, 128 - 2 * ZONE, 1), 0.0),
    )
    edge = surface[:, 256:384] - inverse[:, 256:384] * lost
    surface_out[:, 256:384] = edge
    up[...] = strips([left, right, edge], 0)
    down[...] = strips([left, right, edge], 60)


def owner_kernel(
    last, place_ref, got, nodes, node_high, node_low, coef, table, meets, classes, matrices, *rest
):
    if last:
        pipes_out, value_ref, ends_ref = rest
    else:
        table_out, nodes_out, value_ref, ends_ref = rest
    value_ref[...] = jnp.where(
        node_high[...] >= 0, coef[...] * (low_halves(got[:, 0:128]) - nodes[...]), 0.0
    )
    inflow = summed(node_high, node_low, value_ref, 64, 128)
    balance = table[...] + (inflow[:, :128] + inflow[:, 128:])
    start = pl.multiple_of(place_ref[0] * 16, 16)
    for index in range(4):
        ends_ref[index * 16 : index * 16 + 16, :] = got[
            pl.ds(start, 16), 256 + index * 128 : 384 + index * 128
        ]
    meet = meets[...]
    meet_high = jnp.bitwise_and(meet >> 7, 1) * 16 + (meet >> 8)
    meet_high = jnp.where(iota((8, 128), 0) < 2, meet_high + 32, meet_high)
    met = gathered(ends_ref, 64, meet_high, meet) * boundary_gain
    node_row = iota((32, 128), 0)
    parts = []
    for half in range(2):
        part = balance[half * 32 : half * 32 + 32]
        part = part + jnp.where(
            node_row == 0, met[half : half + 1],
            jnp.where(node_row == 31, met[2 + half : 3 + half], 0.0),
        )
        products = jnp.dot(
            matrices[...], part, precision=lax.Precision.HIGHEST, preferred_element_type=F32
        )
        kind = classes[half : half + 1, :]
        updated = jnp.zeros((32, 128), F32)
        for index in range(CLASSES):
            updated = jnp.where(kind == index, products[index * 32 : index * 32 + 32], updated)
        parts.append(updated)
    if last:
        pipes_out[:, 0:128] = parts[0]
        pipes_out[:, 128:256] = parts[1]
        return
    table_out[0:32, :] = parts[0]
    table_out[32:64, :] = parts[1]
    nodes_out[...] = gathered(table_out, 64, node_high[...], node_low[...])


def shape(*dims, dtype=F32):
    return jax.ShapeDtypeStruct(dims, dtype)


def call(kernel, inputs, outputs, scratch=(), scalars=0, space=pltpu.VMEM, flops=10**9):
    smem = pl.BlockSpec(memory_space=pltpu.SMEM)
    vmem = pl.BlockSpec(memory_space=pltpu.VMEM)
    return pl.pallas_call(
        kernel,
        out_shape=outputs,
        in_specs=[smem] * scalars + [pl.BlockSpec(memory_space=space)] * (len(inputs) - scalars),
        out_specs=[vmem] * len(outputs),
        scratch_shapes=list(scratch),
        compiler_params=pltpu.CompilerParams(vmem_limit_bytes=32 << 20),
        cost_estimate=pl.CostEstimate(flops=flops, bytes_accessed=1 << 20, transcendentals=0),
    )(*inputs)


def ring(block, axis, distance):
    size = lax.axis_size(axis)
    return lax.ppermute(block, axis, [(i, (i + distance) % size) for i in range(size)])


def body(
    surface_head, conduct_x, conduct_y, porosity, rainfall, pipe_head, pipe_class, pipe_up,
    pipe_down, pipe_matrices, link_cell, link_node, link_coef,
):
    place = jnp.stack([lax.axis_index("row"), lax.axis_index("col")]).astype(jnp.int32)
    link_cell = link_cell[0]
    link_node = link_node[:, 0, :]
    link_coef = link_coef[:, 0, :]
    meets = jnp.concatenate(
        [pipe_up.reshape(2, 128), pipe_down.reshape(2, 128), jnp.zeros((4, 128), jnp.int32)], axis=0
    )
    classes = pipe_class.reshape(2, 128)
    matrices = pipe_matrices.reshape(CLASSES * 32, 32)
    ints = functools.partial(shape, dtype=jnp.int32)

    fields, up, down = call(
        start_kernel, (surface_head, conduct_x, conduct_y, porosity, rainfall),
        [shape(5, 64, 256), shape(40, 128), shape(40, 128)],
        [pltpu.SemaphoreType.DMA((5,))], space=pltpu.HBM,
    )
    above, below = ring(down, "row", 1), ring(up, "row", -1)
    tall, sent = call(
        pack_cols_kernel, (place, above, below, fields, link_cell),
        [shape(5, 72, 256), shape(136, 128)], scalars=1,
    )
    from_west, from_east = ring(sent, "col", 1), ring(sent, "col", -1)
    table, nodes, node_high, node_low, coef = call(
        owner_start_kernel, (pipe_head, link_node, link_coef),
        [shape(64, 128), shape(64, 128), ints(64, 128), ints(64, 128), shape(64, 128)],
    )
    gather_scratch = [
        pltpu.VMEM((128, 128), F32), pltpu.VMEM((64, 128), F32), pltpu.VMEM((8, 128), F32)
    ]
    swept_shapes = [shape(64, 384), shape(64, 128), shape(128, 128)]
    (gains, inverse, cell_high, cell_low, zone_row, zone_col, surface, heads, zone, sent) = call(
        first_sweep_kernel,
        (place, tall, from_west, from_east, link_cell, table, nodes, coef),
        [shape(6, 72, 384), shape(64, 384), ints(64, 128), ints(64, 128), ints(128, 128),
         ints(128, 128), *swept_shapes, shape(128, 1024)],
        gather_scratch, scalars=1,
    )
    sent, meets, classes, matrices = lax.optimization_barrier((sent, meets, classes, matrices))
    coefs = ()
    for step in range(STEPS):
        first, last = step == 0, step == STEPS - 1
        if step:
            surface, heads, zone, sent = call(
                functools.partial(sweep_kernel, last),
                (place, surface, above, below, gains, cell_high, cell_low, zone_row, zone_col,
                 table, nodes),
                [*swept_shapes, shape(128, 768)], gather_scratch, scalars=1,
            )
        got = lax.all_to_all(sent, ("row", "col"), split_axis=0, concat_axis=0, tiled=True)
        outputs = [shape(64, 256)] if last else [shape(64, 384), shape(12, 128), shape(12, 128)]
        if first:
            outputs += [shape(64, 128), shape(128, 128)]
        tile = call(
            functools.partial(tile_kernel, first, last),
            (got, surface, inverse, heads, zone, cell_high, cell_low, zone_row, zone_col, *coefs),
            outputs, [pltpu.VMEM((64, 128), F32), pltpu.VMEM((128, 128), F32)],
        )
        if not last:
            above, below = ring(tile[2], "row", 1), ring(tile[1], "row", -1)
        owner = call(
            functools.partial(owner_kernel, last),
            (place, got, nodes, node_high, node_low, coef, table, meets, classes, matrices),
            [shape(32, 256)] if last else [shape(64, 128), shape(64, 128)],
            [pltpu.VMEM((64, 128), F32), pltpu.VMEM((64, 128), F32)], scalars=1,
        )
        if last:
            return tile[0], owner[0]
        surface = tile[0]
        table, nodes = owner
        if first:
            coefs = tuple(tile[3:])


def solution(mesh):
    placed = (
        P("row", "col"),
        P("row", "col"),
        P("row", "col"),
        P("row", "col"),
        P("row", "col"),
        P(None, ("row", "col")),
        P(("row", "col")),
        P(("row", "col")),
        P(("row", "col")),
        P(),
        P(("row", "col"), None, None),
        P(None, ("row", "col"), None),
        P(None, ("row", "col"), None),
    )
    return jax.shard_map(
        body,
        mesh=mesh,
        in_specs=placed,
        out_specs=(P("row", "col"), P(None, ("row", "col"))),
        check_vma=False,
    )
```

```python
import functools

import jax
import jax.numpy as jnp
from jax import lax
from jax.experimental import pallas as pl
from jax.experimental.pallas import tpu as pltpu
from jax.sharding import PartitionSpec as P

CLASSES = 4
SWEEPS = 4
STEPS = 3
F32 = jnp.float32
BF16 = jnp.bfloat16

boundary_gain = 0.5

HALO_ROWS = 4
HALO_COLS = 12
ZONE = 8
ENDS = (0, 32, 31, 63)


def iota(shape, dim):
    return lax.broadcasted_iota(jnp.int32, shape, dim)


def packed(x):
    return jnp.concatenate([x[:64], x[64:]], axis=1)


def low_halves(block):
    lane = iota((64, 128), 1)
    return jnp.where(lane < 64, block[:64], pltpu.roll(block[64:], 64, 1))


def high_halves(block):
    lane = iota((64, 128), 1)
    return jnp.where(lane < 64, pltpu.roll(block[:64], 64, 1), block[64:])


def paired(low, high):
    lane = iota((64, 128), 1)
    top = jnp.where(lane < 64, low, pltpu.roll(high, 64, 1))
    bottom = jnp.where(lane < 64, pltpu.roll(low, 64, 1), high)
    return jnp.concatenate([top, bottom], axis=0)


def beside(values):
    lane = iota((128, 128), 1)
    both = paired(values, values)
    return jnp.where(lane < 64, pltpu.roll(both, 1, 0), pltpu.roll(both, 127, 0))


def gathered(table_ref, rows, high, low):
    low = jnp.bitwise_and(low, 127)
    tiles = []
    for start in range(0, high.shape[0], 8):
        tile_high, tile_low = high[start : start + 8], low[start : start + 8]
        found = jnp.zeros((8, 128), F32)
        for row in range(rows):
            line = jnp.broadcast_to(table_ref[row : row + 1, :], (8, 128))
            values = jnp.take_along_axis(line, tile_low, axis=1)
            found = jnp.where(tile_high == row, values, found)
        tiles.append(found)
    return jnp.concatenate(tiles, axis=0) if len(tiles) > 1 else tiles[0]


def repeated(line, size):
    block = jnp.broadcast_to(line, (16, 128)).astype(BF16)
    return jnp.concatenate([block] * (size // 16), axis=0) if size > 16 else block


def summed(high_ref, low_ref, value_ref, high_size, low_size):
    high_iota = iota((high_size, 128), 0).astype(F32).astype(BF16)
    low_iota = iota((low_size, 128), 0).astype(F32).astype(BF16)
    high_zero = jnp.zeros((high_size, 128), BF16)
    low_zero = jnp.zeros((low_size, 128), BF16)
    low_one = jnp.ones((low_size, 128), BF16)
    total = jnp.zeros((2 * high_size, low_size), F32)
    for start in range(0, high_ref.shape[0], 8):
        high = high_ref[start : start + 8, :].astype(F32)
        low = low_ref[start : start + 8, :].astype(F32)
        value = value_ref[start : start + 8, :]
        coarse = value.astype(BF16).astype(F32)
        fine = value - coarse
        coarse_hot, fine_hot, low_hot = [], [], []
        for j in range(8):
            same = repeated(high[j : j + 1], high_size) == high_iota
            coarse_hot.append(jnp.where(same, repeated(coarse[j : j + 1], high_size), high_zero))
            fine_hot.append(jnp.where(same, repeated(fine[j : j + 1], high_size), high_zero))
            same = repeated(low[j : j + 1], low_size) == low_iota
            low_hot.append(jnp.where(same, low_one, low_zero))
        value_hot = jnp.concatenate(
            [jnp.concatenate(coarse_hot, axis=1), jnp.concatenate(fine_hot, axis=1)], axis=0
        )
        total = total + lax.dot_general(
            value_hot, jnp.concatenate(low_hot, axis=1), (((1,), (1,)), ((), ())),
            preferred_element_type=F32,
        )
    return total[:high_size] + total[high_size:]


def cell_place(cell):
    high = jnp.where(
        cell >= 0, jnp.bitwise_and(cell >> 7, 1) * 64 + (cell >> 8), -1
    )
    return high, jnp.bitwise_and(cell, 127)


def node_place(node):
    high = jnp.where(
        node >= 0, jnp.bitwise_and(node >> 7, 1) * 32 + (node >> 8), -1
    )
    return high, jnp.bitwise_and(node, 127)


def pipe_table(state):
    return jnp.concatenate([state[:, :128], state[:, 128:]], axis=0)


def strips(blocks, start):
    return jnp.concatenate([block[start : start + HALO_ROWS] for block in blocks], axis=0)


def start_kernel(surface, cond_x, cond_y, porosity, rainfall, fields, up, down, arrived):
    copies = [
        pltpu.make_async_copy(source, fields.at[index], arrived.at[index])
        for index, source in enumerate((surface, cond_x, cond_y, porosity, rainfall))
    ]
    for copy in copies:
        copy.start()
    for copy in copies:
        copy.wait()
    fields[3] = 1.0 / fields[3]
    for index in range(5):
        halves = [fields[index, :, 0:128], fields[index, :, 128:256]]
        up[pl.ds(index * 8, 8), :] = strips(halves, 0)
        down[pl.ds(index * 8, 8), :] = strips(halves, 60)


def tall_block(place_ref, block, above, below, start):
    over = jnp.where(place_ref[0] > 0, above[start : start + 4, :], 0.0)
    under = jnp.where(place_ref[0] < 7, below[start : start + 4, :], 0.0)
    return jnp.concatenate([block, under, over], axis=0)


def pack_cols_kernel(place_ref, above, below, fields, link_cell, tall_out, out):
    lane = iota((72, 128), 1)
    message = jnp.zeros((72, 128), F32)
    for index in range(5):
        tall = [
            tall_block(
                place_ref, fields[index, :, half * 128 : half * 128 + 128], above, below,
                index * 8 + half * 4,
            )
            for half in range(2)
        ]
        tall_out[index, :, 0:128] = tall[0]
        tall_out[index, :, 128:256] = tall[1]
        edges = jnp.where(
            lane < HALO_COLS, tall[0], jnp.where(lane >= 128 - HALO_COLS, tall[1], 0.0)
        )
        if index:
            edges = pltpu.roll(edges, index * 2 * HALO_COLS, 1)
        message = message + edges
    out[0:72, :] = message
    out[72:136, :] = packed(link_cell[...]).astype(F32)


def owner_start_kernel(
    pipes, link_node, link_coef, table, nodes, node_high, node_low, coef
):
    table[...] = pipe_table(pipes[...])
    high, low = node_place(packed(link_node[...]))
    node_high[...] = high
    node_low[...] = low
    coef[...] = packed(link_coef[...])
    nodes[...] = gathered(table, 64, high, low)


def swept(state, gains):
    def once(_, w):
        return (
            gains[0] * w
            + gains[1] * pltpu.roll(w, 1, 0)
            + gains[2] * pltpu.roll(w, 71, 0)
            + gains[3] * pltpu.roll(w, 1, 1)
            + gains[4] * pltpu.roll(w, 383, 1)
            + gains[5]
        )

    for i in range(SWEEPS):
        state = once(i, state)
    return state


def build_message(out, heads, nodes, table):
    out[:, 0:128] = paired(heads, nodes)
    out[:, 128:256] = beside(nodes)
    for index, row in enumerate(ENDS):
        block = jnp.broadcast_to(table[row : row + 1, :], (128, 128))
        out[:, 256 + index * 128 : 384 + index * 128] = block


def zone_heads(edge, zone_place, edge_ref, zone_ref):
    lane = iota((64, 128), 1)
    edge_ref[...] = jnp.where(lane < ZONE, edge, pltpu.roll(edge, 2 * ZONE, 1))
    lane8 = iota((8, 128), 1)
    table = jnp.zeros((8, 128), F32)
    for s in range(8):
        line = edge_ref[pl.ds(s, 8, stride=8), :]
        if s:
            line = pltpu.roll(line, s * 16, 1)
        table = jnp.where((lane8 >> 4) == s, line, table)
    zone_ref[...] = table
    zone_row, zone_col = zone_place
    high = jnp.where(zone_row >= 0, zone_row >> 3, -1)
    low = jnp.bitwise_and(zone_row, 7) * 16 + zone_col
    return gathered(zone_ref, 8, high, low)


def sweep_and_gather(
    state, gains, cell_high, cell_low, zone_place, surface_out, heads_out, zone_out, cell_table,
    edge_ref, zone_ref,
):
    state = swept(state, gains)
    surface_out[...] = state[:64]
    cell_table[0:64, :] = state[:64, 0:128]
    cell_table[64:128, :] = state[:64, 128:256]
    heads = gathered(cell_table, 128, cell_high, cell_low)
    heads_out[...] = heads
    if zone_place is not None:
        zone_out[...] = zone_heads(state[:64, 256:384], zone_place, edge_ref, zone_ref)
    return heads


def first_sweep_kernel(
    place_ref, tall, from_west, from_east, link_cell, table, nodes, coef,
    gains_out, inverse_out, cell_high, cell_low, zone_row_out, zone_col_out, surface_out, heads_out,
    zone_out, out, cell_table, edge_ref, zone_ref,
):
    lane = iota((72, 128), 1)
    wide = []
    for index in range(5):
        west = jnp.where(place_ref[1] > 0, from_west[0:72, :], 0.0)
        east = jnp.where(place_ref[1] < 15, from_east[0:72, :], 0.0)
        if index:
            west = pltpu.roll(west, 128 - index * 2 * HALO_COLS, 1)
            east = pltpu.roll(east, 128 - index * 2 * HALO_COLS, 1)
        edge = jnp.where(
            lane < HALO_COLS, east, jnp.where(lane >= 128 - HALO_COLS, west, 0.0)
        )
        wide.append(jnp.concatenate([tall[index], edge], axis=1))
    state, cond_x, cond_y, inverse, rainfall = wide
    north = pltpu.roll(cond_x, 1, 0)
    west = pltpu.roll(cond_y, 1, 1)
    gains = [
        1.0 - (north + cond_x + west + cond_y) * inverse,
        north * inverse, cond_x * inverse, west * inverse, cond_y * inverse, rainfall,
    ]
    for index, gain in enumerate(gains):
        gains_out[index] = gain
    inverse_out[...] = inverse[:64]
    cells = paired(from_west[72:136, :], from_east[72:136, :]).astype(jnp.int32)
    col = jnp.bitwise_and(cells, 255)
    is_west = iota((128, 128), 1) < 64
    zone_col = jnp.where(is_west, col - (256 - 2 * ZONE), col)
    inside = (zone_col >= 0) & (zone_col < 2 * ZONE)
    inside = inside & (jnp.where(is_west, zone_col, zone_col + ZONE) >= ZONE)
    zone_row = jnp.where((cells >= 0) & inside & (jnp.where(is_west, 0, zone_col) < ZONE), cells >> 8, -1)
    zone_row_out[...] = zone_row
    zone_col_out[...] = zone_col
    high, low = cell_place(packed(link_cell[...]))
    cell_high[...] = high
    cell_low[...] = low
    heads = sweep_and_gather(
        state, gains, high, low, (zone_row, zone_col), surface_out, heads_out, zone_out,
        cell_table, edge_ref, zone_ref,
    )
    build_message(out, heads, nodes[...], table)
    out[:, 768:896] = paired(coef[...], coef[...])
    out[:, 896:1024] = beside(coef[...])


def sweep_kernel(
    last, place_ref, surface, above, below, gains_ref, cell_high, cell_low, zone_row, zone_col,
    table, nodes, surface_out, heads_out, zone_out, out, cell_table, edge_ref, zone_ref,
):
    state = jnp.concatenate(
        [
            tall_block(
                place_ref, surface[:, block * 128 : block * 128 + 128], above, below, block * 4
            )
            for block in range(3)
        ],
        axis=1,
    )
    gains = [gains_ref[index] for index in range(6)]
    zone_place = None if last else (zone_row[...], zone_col[...])
    heads = sweep_and_gather(
        state, gains, cell_high[...], cell_low[...], zone_place, surface_out, heads_out, zone_out,
        cell_table, edge_ref, zone_ref,
    )
    build_message(out, heads, nodes[...], table)


def tile_kernel(
    first, last, got, surface, inverse, heads, zone, cell_high, cell_low, zone_row, zone_col, *rest
):
    rest = list(rest)
    if first:
        own_coef = low_halves(got[:, 768:896])
        zone_coef = got[:, 896:1024]
    else:
        own_coef = rest.pop(0)[...]
        zone_coef = rest.pop(0)[...]
    surface_out = rest.pop(0)
    if not last:
        up, down = rest.pop(0), rest.pop(0)
    if first:
        rest.pop(0)[...] = own_coef
        rest.pop(0)[...] = zone_coef
    value_ref, zone_value_ref = rest
    value_ref[...] = jnp.where(
        cell_high[...] >= 0, own_coef * (heads[...] - high_halves(got[:, 0:128])), 0.0
    )
    lost = summed(cell_high, cell_low, value_ref, 128, 128)
    left = surface[:, 0:128] - inverse[:, 0:128] * lost[:64]
    right = surface[:, 128:256] - inverse[:, 128:256] * lost[64:]
    surface_out[:, 0:128] = left
    surface_out[:, 128:256] = right
    if last:
        return
    zone_value_ref[...] = jnp.where(
        zone_row[...] >= 0, zone_coef * (zone[...] - got[:, 128:256]), 0.0
    )
    lost = summed(zone_row, zone_col, zone_value_ref, 64, 2 * ZONE)
    lost = jnp.concatenate([lost, jnp.zeros((64, 128 - 2 * ZONE), F32)], axis=1)
    lane = iota((64, 128), 1)
    lost = jnp.where(
        lane < ZONE, lost,
        jnp.where(lane >= 128 - ZONE, pltpu.roll(lost, 128 - 2 * ZONE, 1), 0.0),
    )
    edge = surface[:, 256:384] - inverse[:, 256:384] * lost
    surface_out[:, 256:384] = edge
    up[...] = strips([left, right, edge], 0)
    down[...] = strips([left, right, edge], 60)


def owner_kernel(
    last, place_ref, got, nodes, node_high, node_low, coef, table, meets, classes, matrices, *rest
):
    if last:
        pipes_out, value_ref, ends_ref = rest
    else:
        table_out, nodes_out, value_ref, ends_ref = rest
    value_ref[...] = jnp.where(
        node_high[...] >= 0, coef[...] * (low_halves(got[:, 0:128]) - nodes[...]), 0.0
    )
    inflow = summed(node_high, node_low, value_ref, 64, 128)
    balance = table[...] + inflow
    start = pl.multiple_of(place_ref[0] * 16, 16)
    for index in range(4):
        ends_ref[index * 16 : index * 16 + 16, :] = got[
            pl.ds(start, 16), 256 + index * 128 : 384 + index * 128
        ]
    meet = meets[...]
    meet_high = jnp.bitwise_and(meet >> 7, 1) * 16 + (meet >> 8)
    meet_high = jnp.where(iota((8, 128), 0) < 2, meet_high + 32, meet_high)
    met = gathered(ends_ref, 64, meet_high, meet) * boundary_gain
    node_row = iota((32, 128), 0)
    parts = []
    for half in range(2):
        part = balance[half * 32 : half * 32 + 32]
        part = part + jnp.where(
            node_row == 0, met[half : half + 1],
            jnp.where(node_row == 31, met[2 + half : 3 + half], 0.0),
        )
        products = jnp.dot(
            matrices[...], part, precision=lax.Precision.HIGHEST, preferred_element_type=F32
        )
        kind = classes[half : half + 1, :]
        updated = jnp.zeros((32, 128), F32)
        for index in range(CLASSES):
            updated = jnp.where(kind == index, products[index * 32 : index * 32 + 32], updated)
        parts.append(updated)
    if last:
        pipes_out[:, 0:128] = parts[0]
        pipes_out[:, 128:256] = parts[1]
        return
    table_out[0:32, :] = parts[0]
    table_out[32:64, :] = parts[1]
    nodes_out[...] = gathered(table_out, 64, node_high[...], node_low[...])


def shape(*dims, dtype=F32):
    return jax.ShapeDtypeStruct(dims, dtype)


def call(kernel, inputs, outputs, scratch=(), scalars=0, space=pltpu.VMEM, grant=32):
    smem = pl.BlockSpec(memory_space=pltpu.SMEM)
    vmem = pl.BlockSpec(memory_space=pltpu.VMEM)
    return pl.pallas_call(
        kernel,
        out_shape=outputs,
        in_specs=[smem] * scalars + [pl.BlockSpec(memory_space=space)] * (len(inputs) - scalars),
        out_specs=[vmem] * len(outputs),
        scratch_shapes=list(scratch),
        compiler_params=pltpu.CompilerParams(vmem_limit_bytes=grant << 20),
        cost_estimate=pl.CostEstimate(flops=10**9, bytes_accessed=1 << 20, transcendentals=0),
    )(*inputs)


def ring(block, axis, distance):
    size = lax.axis_size(axis)
    return lax.ppermute(block, axis, [(i, (i + distance) % size) for i in range(size)])


def body(
    surface_head, conduct_x, conduct_y, porosity, rainfall, pipe_head, pipe_class, pipe_up,
    pipe_down, pipe_matrices, link_cell, link_node, link_coef,
):
    place = jnp.stack([lax.axis_index("row"), lax.axis_index("col")]).astype(jnp.int32)
    link_cell = link_cell[0]
    link_node = link_node[:, 0, :]
    link_coef = link_coef[:, 0, :]
    meets = jnp.concatenate(
        [pipe_up.reshape(2, 128), pipe_down.reshape(2, 128), jnp.zeros((4, 128), jnp.int32)], axis=0
    )
    classes = pipe_class.reshape(2, 128)
    matrices = pipe_matrices.reshape(CLASSES * 32, 32)
    ints = functools.partial(shape, dtype=jnp.int32)

    fields, up, down = call(
        start_kernel, (surface_head, conduct_x, conduct_y, porosity, rainfall),
        [shape(5, 64, 256), shape(40, 128), shape(40, 128)],
        [pltpu.SemaphoreType.DMA((5,))], space=pl.ANY, grant=60,
    )
    above, below = ring(down, "row", 1), ring(up, "row", -1)
    tall, sent = call(
        pack_cols_kernel, (place, above, below, fields, link_cell),
        [shape(5, 72, 256), shape(136, 128)], scalars=1,
    )
    from_west, from_east = ring(sent, "col", 1), ring(sent, "col", -1)
    table, nodes, node_high, node_low, coef = call(
        owner_start_kernel, (pipe_head, link_node, link_coef),
        [shape(64, 128), shape(64, 128), ints(64, 128), ints(64, 128), shape(64, 128)],
    )
    gather_scratch = [
        pltpu.VMEM((128, 128), F32), pltpu.VMEM((64, 128), F32), pltpu.VMEM((8, 128), F32)
    ]
    swept_shapes = [shape(64, 384), shape(64, 128), shape(128, 128)]
    (gains, inverse, cell_high, cell_low, zone_row, zone_col, surface, heads, zone, sent) = call(
        first_sweep_kernel,
        (place, tall, from_west, from_east, link_cell, table, nodes, coef),
        [shape(6, 72, 384), shape(64, 384), ints(64, 128), ints(64, 128), ints(128, 128),
         ints(128, 128), *swept_shapes, shape(128, 1024)],
        gather_scratch, scalars=1,
    )
    sent, meets, classes, matrices = lax.optimization_barrier((sent, meets, classes, matrices))
    coefs = ()
    for step in range(STEPS):
        first, last = step == 0, step == STEPS - 1
        if step:
            surface, heads, zone, sent = call(
                functools.partial(sweep_kernel, last),
                (place, surface, above, below, gains, cell_high, cell_low, zone_row, zone_col,
                 table, nodes),
                [*swept_shapes, shape(128, 768)], gather_scratch, scalars=1,
            )
        got = lax.all_to_all(sent, ("row", "col"), split_axis=0, concat_axis=0, tiled=True)
        outputs = [shape(64, 256)] if last else [shape(64, 384), shape(12, 128), shape(12, 128)]
        if first:
            outputs += [shape(64, 128), shape(128, 128)]
        tile = call(
            functools.partial(tile_kernel, first, last),
            (got, surface, inverse, heads, zone, cell_high, cell_low, zone_row, zone_col, *coefs),
            outputs, [pltpu.VMEM((64, 128), F32), pltpu.VMEM((128, 128), F32)],
        )
        if not last:
            above, below = ring(tile[2], "row", 1), ring(tile[1], "row", -1)
        owner = call(
            functools.partial(owner_kernel, last),
            (place, got, nodes, node_high, node_low, coef, table, meets, classes, matrices),
            [shape(32, 256)] if last else [shape(64, 128), shape(64, 128)],
            [pltpu.VMEM((64, 128), F32), pltpu.VMEM((64, 128), F32)], scalars=1,
        )
        if last:
            return tile[0], owner[0]
        surface = tile[0]
        table, nodes = owner
        if first:
            coefs = tuple(tile[3:])


def solution(mesh):
    placed = (
        P("row", "col"),
        P("row", "col"),
        P("row", "col"),
        P("row", "col"),
        P("row", "col"),
        P(None, ("row", "col")),
        P(("row", "col")),
        P(("row", "col")),
        P(("row", "col")),
        P(),
        P(("row", "col"), None, None),
        P(None, ("row", "col"), None),
        P(None, ("row", "col"), None),
    )
    return jax.shard_map(
        body,
        mesh=mesh,
        in_specs=placed,
        out_specs=(P("row", "col"), P(None, ("row", "col"))),
        check_vma=False,
    )
```

```python
import functools

import jax
import jax.numpy as jnp
from jax import lax
from jax.experimental import pallas as pl
from jax.experimental.pallas import tpu as pltpu
from jax.sharding import PartitionSpec as P

CLASSES = 4
SWEEPS = 4
STEPS = 3
F32 = jnp.float32
BF16 = jnp.bfloat16

boundary_gain = 0.5

HALO_ROWS = 4
HALO_COLS = 12
ZONE = 8
ENDS = (0, 32, 31, 63)


def iota(shape, dim):
    return lax.broadcasted_iota(jnp.int32, shape, dim)


def packed(x):
    return jnp.concatenate([x[:64], x[64:]], axis=1)


def low_halves(block):
    lane = iota((64, 128), 1)
    return jnp.where(lane < 64, block[:64], pltpu.roll(block[64:], 64, 1))


def high_halves(block):
    lane = iota((64, 128), 1)
    return jnp.where(lane < 64, pltpu.roll(block[:64], 64, 1), block[64:])


def paired(low, high):
    lane = iota((64, 128), 1)
    top = jnp.where(lane < 64, low, pltpu.roll(high, 64, 1))
    bottom = jnp.where(lane < 64, pltpu.roll(low, 64, 1), high)
    return jnp.concatenate([top, bottom], axis=0)


def beside(values):
    lane = iota((128, 128), 1)
    both = paired(values, values)
    return jnp.where(lane < 64, pltpu.roll(both, 1, 0), pltpu.roll(both, 127, 0))


def gathered(table_ref, rows, high, low):
    low = jnp.bitwise_and(low, 127)
    tiles = []
    for start in range(0, high.shape[0], 8):
        tile_high, tile_low = high[start : start + 8], low[start : start + 8]
        found = jnp.zeros((8, 128), F32)
        for row in range(rows):
            line = jnp.broadcast_to(table_ref[row : row + 1, :], (8, 128))
            values = jnp.take_along_axis(line, tile_low, axis=1)
            found = jnp.where(tile_high == row, values, found)
        tiles.append(found)
    return jnp.concatenate(tiles, axis=0) if len(tiles) > 1 else tiles[0]


def repeated(line, size):
    block = jnp.broadcast_to(line, (16, 128)).astype(BF16)
    return jnp.concatenate([block] * (size // 16), axis=0) if size > 16 else block


def summed(high_ref, low_ref, value_ref, high_size, low_size):
    high_iota = iota((high_size, 128), 0).astype(F32).astype(BF16)
    low_iota = iota((low_size, 128), 0).astype(F32).astype(BF16)
    high_zero = jnp.zeros((high_size, 128), BF16)
    low_zero = jnp.zeros((low_size, 128), BF16)
    low_one = jnp.ones((low_size, 128), BF16)
    total = jnp.zeros((2 * high_size, low_size), F32)
    for start in range(0, high_ref.shape[0], 8):
        high = high_ref[start : start + 8, :].astype(F32)
        low = low_ref[start : start + 8, :].astype(F32)
        value = value_ref[start : start + 8, :]
        coarse = value.astype(BF16).astype(F32)
        fine = value - coarse
        coarse_hot, fine_hot, low_hot = [], [], []
        for j in range(8):
            same = repeated(high[j : j + 1], high_size) == high_iota
            coarse_hot.append(jnp.where(same, repeated(coarse[j : j + 1], high_size), high_zero))
            fine_hot.append(jnp.where(same, repeated(fine[j : j + 1], high_size), high_zero))
            same = repeated(low[j : j + 1], low_size) == low_iota
            low_hot.append(jnp.where(same, low_one, low_zero))
        value_hot = jnp.concatenate(
            [jnp.concatenate(coarse_hot, axis=1), jnp.concatenate(fine_hot, axis=1)], axis=0
        )
        total = total + lax.dot_general(
            value_hot, jnp.concatenate(low_hot, axis=1), (((1,), (1,)), ((), ())),
            preferred_element_type=F32,
        )
    return total[:high_size] + total[high_size:]


def cell_place(cell):
    high = jnp.where(
        cell >= 0, jnp.bitwise_and(cell >> 7, 1) * 64 + (cell >> 8), -1
    )
    return high, jnp.bitwise_and(cell, 127)


def node_place(node):
    high = jnp.where(
        node >= 0, jnp.bitwise_and(node >> 7, 1) * 32 + (node >> 8), -1
    )
    return high, jnp.bitwise_and(node, 127)


def pipe_table(state):
    return jnp.concatenate([state[:, :128], state[:, 128:]], axis=0)


def strips(blocks, start):
    return jnp.concatenate([block[start : start + HALO_ROWS] for block in blocks], axis=0)


def start_kernel(surface, cond_x, cond_y, porosity, rainfall, fields, up, down, arrived):
    copies = [
        pltpu.make_async_copy(source, fields.at[index], arrived.at[index])
        for index, source in enumerate((surface, cond_x, cond_y, porosity, rainfall))
    ]
    for copy in copies:
        copy.start()
    for copy in copies:
        copy.wait()
    fields[3] = 1.0 / fields[3]
    for index in range(5):
        halves = [fields[index, :, 0:128], fields[index, :, 128:256]]
        up[pl.ds(index * 8, 8), :] = strips(halves, 0)
        down[pl.ds(index * 8, 8), :] = strips(halves, 60)


def tall_block(place_ref, block, above, below, start):
    over = jnp.where(place_ref[0] > 0, above[start : start + 4, :], 0.0)
    under = jnp.where(place_ref[0] < 7, below[start : start + 4, :], 0.0)
    return jnp.concatenate([block, under, over], axis=0)


def pack_cols_kernel(place_ref, above, below, fields, link_cell, tall_out, out):
    lane = iota((72, 128), 1)
    message = jnp.zeros((72, 128), F32)
    for index in range(5):
        tall = [
            tall_block(
                place_ref, fields[index, :, half * 128 : half * 128 + 128], above, below,
                index * 8 + half * 4,
            )
            for half in range(2)
        ]
        tall_out[index, :, 0:128] = tall[0]
        tall_out[index, :, 128:256] = tall[1]
        edges = jnp.where(
            lane < HALO_COLS, tall[0], jnp.where(lane >= 128 - HALO_COLS, tall[1], 0.0)
        )
        if index:
            edges = pltpu.roll(edges, index * 2 * HALO_COLS, 1)
        message = message + edges
    out[0:72, :] = message
    out[72:136, :] = packed(link_cell[...]).astype(F32)


def owner_start_kernel(
    pipes, link_node, link_coef, kinds, laws, table, nodes, node_high, node_low, coef, classes,
    matrices,
):
    classes[...] = kinds[...]
    matrices[...] = laws[...]
    table[...] = pipe_table(pipes[...])
    high, low = node_place(packed(link_node[...]))
    node_high[...] = high
    node_low[...] = low
    coef[...] = packed(link_coef[...])
    nodes[...] = gathered(table, 64, high, low)


def swept(state, gains):
    def once(_, w):
        return (
            gains[0] * w
            + gains[1] * pltpu.roll(w, 1, 0)
            + gains[2] * pltpu.roll(w, 71, 0)
            + gains[3] * pltpu.roll(w, 1, 1)
            + gains[4] * pltpu.roll(w, 383, 1)
            + gains[5]
        )

    for i in range(SWEEPS):
        state = once(i, state)
    return state


def put(out, blocks, index, value):
    out[pl.ds(index, 128, stride=blocks), :] = value


def taken(got, blocks, index):
    return got[pl.ds(index, 128, stride=blocks), :]


def build_message(out, blocks, heads, nodes, table):
    put(out, blocks, 0, paired(heads, nodes))
    put(out, blocks, 1, beside(nodes))
    for index, row in enumerate(ENDS):
        put(out, blocks, 2 + index, jnp.broadcast_to(table[row : row + 1, :], (128, 128)))


def zone_heads(edge, zone_place, edge_ref, zone_ref):
    lane = iota((64, 128), 1)
    edge_ref[...] = jnp.where(lane < ZONE, edge, pltpu.roll(edge, 2 * ZONE, 1))
    lane8 = iota((8, 128), 1)
    table = jnp.zeros((8, 128), F32)
    for s in range(8):
        line = edge_ref[pl.ds(s, 8, stride=8), :]
        if s:
            line = pltpu.roll(line, s * 16, 1)
        table = jnp.where((lane8 >> 4) == s, line, table)
    zone_ref[...] = table
    zone_row, zone_col = zone_place
    high = jnp.where(zone_row >= 0, zone_row >> 3, -1)
    low = jnp.bitwise_and(zone_row, 7) * 16 + zone_col
    return gathered(zone_ref, 8, high, low)


def sweep_and_gather(
    state, gains, cell_high, cell_low, zone_place, surface_out, heads_out, zone_out, cell_table,
    edge_ref, zone_ref,
):
    state = swept(state, gains)
    surface_out[...] = state[:64]
    cell_table[0:64, :] = state[:64, 0:128]
    cell_table[64:128, :] = state[:64, 128:256]
    heads = gathered(cell_table, 128, cell_high, cell_low)
    heads_out[...] = heads
    if zone_place is not None:
        zone_out[...] = zone_heads(state[:64, 256:384], zone_place, edge_ref, zone_ref)
    return heads


def first_sweep_kernel(
    place_ref, tall, from_west, from_east, link_cell, table, nodes, coef,
    gains_out, inverse_out, cell_high, cell_low, zone_row_out, zone_col_out, surface_out, heads_out,
    zone_out, out, cell_table, edge_ref, zone_ref,
):
    lane = iota((72, 128), 1)
    wide = []
    for index in range(5):
        west = jnp.where(place_ref[1] > 0, from_west[0:72, :], 0.0)
        east = jnp.where(place_ref[1] < 15, from_east[0:72, :], 0.0)
        if index:
            west = pltpu.roll(west, 128 - index * 2 * HALO_COLS, 1)
            east = pltpu.roll(east, 128 - index * 2 * HALO_COLS, 1)
        edge = jnp.where(
            lane < HALO_COLS, east, jnp.where(lane >= 128 - HALO_COLS, west, 0.0)
        )
        wide.append(jnp.concatenate([tall[index], edge], axis=1))
    state, cond_x, cond_y, inverse, rainfall = wide
    north = pltpu.roll(cond_x, 1, 0)
    west = pltpu.roll(cond_y, 1, 1)
    gains = [
        1.0 - (north + cond_x + west + cond_y) * inverse,
        north * inverse, cond_x * inverse, west * inverse, cond_y * inverse, rainfall,
    ]
    for index, gain in enumerate(gains):
        gains_out[index] = gain
    inverse_out[...] = inverse[:64]
    cells = paired(from_west[72:136, :], from_east[72:136, :]).astype(jnp.int32)
    col = jnp.bitwise_and(cells, 255)
    is_west = iota((128, 128), 1) < 64
    zone_col = jnp.where(is_west, col - (256 - 2 * ZONE), col)
    inside = (zone_col >= 0) & (zone_col < 2 * ZONE)
    inside = inside & (jnp.where(is_west, zone_col, zone_col + ZONE) >= ZONE)
    zone_row = jnp.where((cells >= 0) & inside & (jnp.where(is_west, 0, zone_col) < ZONE), cells >> 8, -1)
    zone_row_out[...] = zone_row
    zone_col_out[...] = zone_col
    high, low = cell_place(packed(link_cell[...]))
    cell_high[...] = high
    cell_low[...] = low
    heads = sweep_and_gather(
        state, gains, high, low, (zone_row, zone_col), surface_out, heads_out, zone_out,
        cell_table, edge_ref, zone_ref,
    )
    build_message(out, 8, heads, nodes[...], table)
    put(out, 8, 6, paired(coef[...], coef[...]))
    put(out, 8, 7, beside(coef[...]))


def sweep_kernel(
    last, place_ref, surface, above, below, gains_ref, cell_high, cell_low, zone_row, zone_col,
    table, nodes, surface_out, heads_out, zone_out, out, cell_table, edge_ref, zone_ref,
):
    state = jnp.concatenate(
        [
            tall_block(
                place_ref, surface[:, block * 128 : block * 128 + 128], above, below, block * 4
            )
            for block in range(3)
        ],
        axis=1,
    )
    gains = [gains_ref[index] for index in range(6)]
    zone_place = None if last else (zone_row[...], zone_col[...])
    heads = sweep_and_gather(
        state, gains, cell_high[...], cell_low[...], zone_place, surface_out, heads_out, zone_out,
        cell_table, edge_ref, zone_ref,
    )
    build_message(out, 6, heads, nodes[...], table)


def tile_kernel(
    first, last, got, surface, inverse, heads, zone, cell_high, cell_low, zone_row, zone_col, *rest
):
    rest = list(rest)
    blocks = 8 if first else 6
    if first:
        own_coef = low_halves(taken(got, blocks, 6))
        zone_coef = taken(got, blocks, 7)
    else:
        own_coef = rest.pop(0)[...]
        zone_coef = rest.pop(0)[...]
    surface_out = rest.pop(0)
    if not last:
        up, down = rest.pop(0), rest.pop(0)
    if first:
        rest.pop(0)[...] = own_coef
        rest.pop(0)[...] = zone_coef
    value_ref, zone_value_ref = rest
    value_ref[...] = jnp.where(
        cell_high[...] >= 0, own_coef * (heads[...] - high_halves(taken(got, blocks, 0))), 0.0
    )
    lost = summed(cell_high, cell_low, value_ref, 128, 128)
    left = surface[:, 0:128] - inverse[:, 0:128] * lost[:64]
    right = surface[:, 128:256] - inverse[:, 128:256] * lost[64:]
    surface_out[:, 0:128] = left
    surface_out[:, 128:256] = right
    if last:
        return
    zone_value_ref[...] = jnp.where(
        zone_row[...] >= 0, zone_coef * (zone[...] - taken(got, blocks, 1)), 0.0
    )
    lost = summed(zone_row, zone_col, zone_value_ref, 64, 2 * ZONE)
    lost = jnp.concatenate([lost, jnp.zeros((64, 128 - 2 * ZONE), F32)], axis=1)
    lane = iota((64, 128), 1)
    lost = jnp.where(
        lane < ZONE, lost,
        jnp.where(lane >= 128 - ZONE, pltpu.roll(lost, 128 - 2 * ZONE, 1), 0.0),
    )
    edge = surface[:, 256:384] - inverse[:, 256:384] * lost
    surface_out[:, 256:384] = edge
    up[...] = strips([left, right, edge], 0)
    down[...] = strips([left, right, edge], 60)


def owner_kernel(
    first, last, place_ref, got, nodes, node_high, node_low, coef, table, meets, classes, matrices, *rest
):
    blocks = 8 if first else 6
    if last:
        pipes_out, value_ref, ends_ref = rest
    else:
        table_out, nodes_out, value_ref, ends_ref = rest
    value_ref[...] = jnp.where(
        node_high[...] >= 0, coef[...] * (low_halves(taken(got, blocks, 0)) - nodes[...]), 0.0
    )
    inflow = summed(node_high, node_low, value_ref, 64, 128)
    balance = table[...] + inflow
    start = pl.multiple_of(place_ref[0] * 16 * blocks, 32)
    for index in range(4):
        ends_ref[index * 16 : index * 16 + 16, :] = got[
            pl.ds(start + 2 + index, 16, stride=blocks), :
        ]
    meet = meets[...]
    meet_high = jnp.bitwise_and(meet >> 7, 1) * 16 + (meet >> 8)
    meet_high = jnp.where(iota((8, 128), 0) < 2, meet_high + 32, meet_high)
    met = gathered(ends_ref, 64, meet_high, meet) * boundary_gain
    node_row = iota((32, 128), 0)
    parts = []
    for half in range(2):
        part = balance[half * 32 : half * 32 + 32]
        part = part + jnp.where(
            node_row == 0, met[half : half + 1],
            jnp.where(node_row == 31, met[2 + half : 3 + half], 0.0),
        )
        products = jnp.dot(
            matrices[...], part, precision=lax.Precision.HIGHEST, preferred_element_type=F32
        )
        kind = classes[half : half + 1, :]
        updated = jnp.zeros((32, 128), F32)
        for index in range(CLASSES):
            updated = jnp.where(kind == index, products[index * 32 : index * 32 + 32], updated)
        parts.append(updated)
    if last:
        pipes_out[:, 0:128] = parts[0]
        pipes_out[:, 128:256] = parts[1]
        return
    table_out[0:32, :] = parts[0]
    table_out[32:64, :] = parts[1]
    nodes_out[...] = gathered(table_out, 64, node_high[...], node_low[...])


def final_kernel(
    place_ref, got, surface, inverse, heads, zone, cell_high, cell_low, zone_row, zone_col, own_coef,
    zone_coef, nodes, node_high, node_low, coef, table, meets, classes, matrices, surface_out,
    pipes_out, cell_value_ref, zone_value_ref, node_value_ref, ends_ref,
):
    owner_kernel(
        False, True, place_ref, got, nodes, node_high, node_low, coef, table, meets, classes,
        matrices, pipes_out, node_value_ref, ends_ref,
    )
    tile_kernel(
        False, True, got, surface, inverse, heads, zone, cell_high, cell_low, zone_row, zone_col,
        own_coef, zone_coef, surface_out, cell_value_ref, zone_value_ref,
    )


def shape(*dims, dtype=F32):
    return jax.ShapeDtypeStruct(dims, dtype)


def call(kernel, inputs, outputs, scratch=(), scalars=0, space=pltpu.VMEM, grant=32):
    smem = pl.BlockSpec(memory_space=pltpu.SMEM)
    vmem = pl.BlockSpec(memory_space=pltpu.VMEM)
    return pl.pallas_call(
        kernel,
        out_shape=outputs,
        in_specs=[smem] * scalars + [pl.BlockSpec(memory_space=space)] * (len(inputs) - scalars),
        out_specs=[vmem] * len(outputs),
        scratch_shapes=list(scratch),
        compiler_params=pltpu.CompilerParams(vmem_limit_bytes=grant << 20),
        cost_estimate=pl.CostEstimate(flops=10**9, bytes_accessed=1 << 20, transcendentals=0),
    )(*inputs)


def ring(block, axis, distance):
    size = lax.axis_size(axis)
    return lax.ppermute(block, axis, [(i, (i + distance) % size) for i in range(size)])


def body(
    surface_head, conduct_x, conduct_y, porosity, rainfall, pipe_head, pipe_class, pipe_up,
    pipe_down, pipe_matrices, link_cell, link_node, link_coef,
):
    place = jnp.stack([lax.axis_index("row"), lax.axis_index("col")]).astype(jnp.int32)
    link_cell = link_cell[0]
    link_node = link_node[:, 0, :]
    link_coef = link_coef[:, 0, :]
    meets = jnp.concatenate(
        [pipe_up.reshape(2, 128), pipe_down.reshape(2, 128), jnp.zeros((4, 128), jnp.int32)], axis=0
    )
    classes = pipe_class.reshape(2, 128)
    matrices = pipe_matrices.reshape(CLASSES * 32, 32)
    ints = functools.partial(shape, dtype=jnp.int32)

    fields, up, down = call(
        start_kernel, (surface_head, conduct_x, conduct_y, porosity, rainfall),
        [shape(5, 64, 256), shape(40, 128), shape(40, 128)],
        [pltpu.SemaphoreType.DMA((5,))], space=pl.ANY, grant=60,
    )
    above, below = ring(down, "row", 1), ring(up, "row", -1)
    tall, sent = call(
        pack_cols_kernel, (place, above, below, fields, link_cell),
        [shape(5, 72, 256), shape(136, 128)], scalars=1,
    )
    from_west, from_east = ring(sent, "col", 1), ring(sent, "col", -1)
    table, nodes, node_high, node_low, coef, classes, matrices = call(
        owner_start_kernel, (pipe_head, link_node, link_coef, classes, matrices),
        [shape(64, 128), shape(64, 128), ints(64, 128), ints(64, 128), shape(64, 128),
         ints(2, 128), shape(128, 32)],
    )
    gather_scratch = [
        pltpu.VMEM((128, 128), F32), pltpu.VMEM((64, 128), F32), pltpu.VMEM((8, 128), F32)
    ]
    swept_shapes = [shape(64, 384), shape(64, 128), shape(128, 128)]
    (gains, inverse, cell_high, cell_low, zone_row, zone_col, surface, heads, zone, sent) = call(
        first_sweep_kernel,
        (place, tall, from_west, from_east, link_cell, table, nodes, coef),
        [shape(6, 72, 384), shape(64, 384), ints(64, 128), ints(64, 128), ints(128, 128),
         ints(128, 128), *swept_shapes, shape(1024, 128)],
        gather_scratch, scalars=1,
    )
    sent, meets = lax.optimization_barrier((sent, meets))
    coefs = ()
    for step in range(STEPS):
        first, last = step == 0, step == STEPS - 1
        if step:
            surface, heads, zone, sent = call(
                functools.partial(sweep_kernel, last),
                (place, surface, above, below, gains, cell_high, cell_low, zone_row, zone_col,
                 table, nodes),
                [*swept_shapes, shape(768, 128)], gather_scratch, scalars=1,
            )
        got = lax.all_to_all(
            sent.reshape(128, 1, -1), ("row", "col"), split_axis=0, concat_axis=0, tiled=True
        ).reshape(-1, 128)
        tile_inputs = (surface, inverse, heads, zone, cell_high, cell_low, zone_row, zone_col, *coefs)
        owner_inputs = (nodes, node_high, node_low, coef, table, meets, classes, matrices)
        tile_scratch = [pltpu.VMEM((64, 128), F32), pltpu.VMEM((128, 128), F32)]
        owner_scratch = [pltpu.VMEM((64, 128), F32), pltpu.VMEM((64, 128), F32)]
        if last:
            return tuple(call(
                final_kernel, (place, got, *tile_inputs, *owner_inputs),
                [shape(64, 256), shape(32, 256)], tile_scratch + owner_scratch, scalars=1,
            ))
        outputs = [shape(64, 384), shape(12, 128), shape(12, 128)]
        if first:
            outputs += [shape(64, 128), shape(128, 128)]
        surface, up, down, *new_coefs = call(
            functools.partial(tile_kernel, first, False), (got, *tile_inputs), outputs, tile_scratch
        )
        above, below = ring(down, "row", 1), ring(up, "row", -1)
        table, nodes = call(
            functools.partial(owner_kernel, first, False), (place, got, *owner_inputs),
            [shape(64, 128), shape(64, 128)], owner_scratch, scalars=1,
        )
        if first:
            coefs = tuple(new_coefs)


def solution(mesh):
    placed = (
        P("row", "col"),
        P("row", "col"),
        P("row", "col"),
        P("row", "col"),
        P("row", "col"),
        P(None, ("row", "col")),
        P(("row", "col")),
        P(("row", "col")),
        P(("row", "col")),
        P(),
        P(("row", "col"), None, None),
        P(None, ("row", "col"), None),
        P(None, ("row", "col"), None),
    )
    return jax.shard_map(
        body,
        mesh=mesh,
        in_specs=placed,
        out_specs=(P("row", "col"), P(None, ("row", "col"))),
        check_vma=False,
    )
```

```python
import functools

import jax
import jax.numpy as jnp
from jax import lax
from jax.experimental import pallas as pl
from jax.experimental.pallas import tpu as pltpu
from jax.sharding import PartitionSpec as P

CLASSES = 4
SWEEPS = 4
STEPS = 3
F32 = jnp.float32
BF16 = jnp.bfloat16

boundary_gain = 0.5

HALO_ROWS = 4
HALO_COLS = 12
ZONE = 8
ENDS = (0, 32, 31, 63)


def iota(shape, dim):
    return lax.broadcasted_iota(jnp.int32, shape, dim)


def packed(x):
    return jnp.concatenate([x[:64], x[64:]], axis=1)


def low_halves(block):
    lane = iota((64, 128), 1)
    return jnp.where(lane < 64, block[:64], pltpu.roll(block[64:], 64, 1))


def high_halves(block):
    lane = iota((64, 128), 1)
    return jnp.where(lane < 64, pltpu.roll(block[:64], 64, 1), block[64:])


def paired(low, high):
    lane = iota((64, 128), 1)
    top = jnp.where(lane < 64, low, pltpu.roll(high, 64, 1))
    bottom = jnp.where(lane < 64, pltpu.roll(low, 64, 1), high)
    return jnp.concatenate([top, bottom], axis=0)


def beside(values):
    lane = iota((128, 128), 1)
    both = paired(values, values)
    return jnp.where(lane < 64, pltpu.roll(both, 1, 0), pltpu.roll(both, 127, 0))


def gathered(table_ref, rows, high, low):
    low = jnp.bitwise_and(low, 127)
    tiles = []
    for start in range(0, high.shape[0], 8):
        tile_high, tile_low = high[start : start + 8], low[start : start + 8]
        found = jnp.zeros((8, 128), F32)
        for row in range(rows):
            line = jnp.broadcast_to(table_ref[row : row + 1, :], (8, 128))
            values = jnp.take_along_axis(line, tile_low, axis=1)
            found = jnp.where(tile_high == row, values, found)
        tiles.append(found)
    return jnp.concatenate(tiles, axis=0) if len(tiles) > 1 else tiles[0]


def repeated(line, size):
    block = jnp.broadcast_to(line, (16, 128)).astype(BF16)
    return jnp.concatenate([block] * (size // 16), axis=0) if size > 16 else block


def summed(high_ref, low_ref, value_ref, high_size, low_size):
    high_iota = iota((high_size, 128), 0).astype(F32).astype(BF16)
    low_iota = iota((low_size, 128), 0).astype(F32).astype(BF16)
    high_zero = jnp.zeros((high_size, 128), BF16)
    low_zero = jnp.zeros((low_size, 128), BF16)
    low_one = jnp.ones((low_size, 128), BF16)
    total = jnp.zeros((2 * high_size, low_size), F32)
    for start in range(0, high_ref.shape[0], 8):
        high = high_ref[start : start + 8, :].astype(F32)
        low = low_ref[start : start + 8, :].astype(F32)
        value = value_ref[start : start + 8, :]
        coarse = value.astype(BF16).astype(F32)
        fine = value - coarse
        coarse_hot, fine_hot, low_hot = [], [], []
        for j in range(8):
            same = repeated(high[j : j + 1], high_size) == high_iota
            coarse_hot.append(jnp.where(same, repeated(coarse[j : j + 1], high_size), high_zero))
            fine_hot.append(jnp.where(same, repeated(fine[j : j + 1], high_size), high_zero))
            same = repeated(low[j : j + 1], low_size) == low_iota
            low_hot.append(jnp.where(same, low_one, low_zero))
        value_hot = jnp.concatenate(
            [jnp.concatenate(coarse_hot, axis=1), jnp.concatenate(fine_hot, axis=1)], axis=0
        )
        total = total + lax.dot_general(
            value_hot, jnp.concatenate(low_hot, axis=1), (((1,), (1,)), ((), ())),
            preferred_element_type=F32,
        )
    return total[:high_size] + total[high_size:]


def cell_place(cell):
    high = jnp.where(
        cell >= 0, jnp.bitwise_and(cell >> 7, 1) * 64 + (cell >> 8), -1
    )
    return high, jnp.bitwise_and(cell, 127)


def node_place(node):
    high = jnp.where(
        node >= 0, jnp.bitwise_and(node >> 7, 1) * 32 + (node >> 8), -1
    )
    return high, jnp.bitwise_and(node, 127)


def pipe_table(state):
    return jnp.concatenate([state[:, :128], state[:, 128:]], axis=0)


def strips(blocks, start):
    return jnp.concatenate([block[start : start + HALO_ROWS] for block in blocks], axis=0)


def even(place_ref, dim):
    return jnp.bitwise_and(place_ref[dim], 1) == 0


def start_kernel(
    place_ref, surface, cond_x, cond_y, porosity, rainfall, pipes, fields, near, far, tips, arrived
):
    copies = [
        pltpu.make_async_copy(source, fields.at[index], arrived.at[index])
        for index, source in enumerate((surface, cond_x, cond_y, porosity, rainfall))
    ]
    copies.append(pltpu.make_async_copy(pipes.at[24:32, :], tips, arrived.at[5]))
    for copy in copies:
        copy.start()
    for copy in copies:
        copy.wait()
    fields[3] = 1.0 / fields[3]
    for index in range(5):
        halves = [fields[index, :, 0:128], fields[index, :, 128:256]]
        top, bottom = strips(halves, 0), strips(halves, 60)
        near[pl.ds(index * 8, 8), :] = jnp.where(even(place_ref, 0), bottom, top)
        far[pl.ds(index * 8, 8), :] = jnp.where(even(place_ref, 0), top, bottom)
    near[40:48, :] = jnp.concatenate(
        [tips[7:8, 0:128], tips[7:8, 128:256], jnp.zeros((6, 128), F32)], axis=0
    )


def tall_block(place_ref, block, near, far, start):
    near, far = near[start : start + 4, :], far[start : start + 4, :]
    over = jnp.where(even(place_ref, 0), far, near)
    under = jnp.where(even(place_ref, 0), near, far)
    over = jnp.where(place_ref[0] > 0, over, 0.0)
    under = jnp.where(place_ref[0] < 7, under, 0.0)
    return jnp.concatenate([block, under, over], axis=0)


def pack_cols_kernel(place_ref, near, far, fields, link_cell, tall_out, out):
    lane = iota((72, 128), 1)
    message = jnp.zeros((72, 128), F32)
    for index in range(5):
        tall = [
            tall_block(
                place_ref, fields[index, :, half * 128 : half * 128 + 128], near, far,
                index * 8 + half * 4,
            )
            for half in range(2)
        ]
        tall_out[index, :, 0:128] = tall[0]
        tall_out[index, :, 128:256] = tall[1]
        edges = jnp.where(
            lane < HALO_COLS, tall[0], jnp.where(lane >= 128 - HALO_COLS, tall[1], 0.0)
        )
        if index:
            edges = pltpu.roll(edges, index * 2 * HALO_COLS, 1)
        message = message + edges
    out[0:72, :] = message
    out[72:136, :] = packed(link_cell[...]).astype(F32)


def owner_start_kernel(
    pipes, link_node, link_coef, kinds, laws, table, nodes, node_high, node_low, coef, classes,
    matrices,
):
    classes[...] = kinds[...]
    matrices[...] = laws[...]
    table[...] = pipe_table(pipes[...])
    high, low = node_place(packed(link_node[...]))
    node_high[...] = high
    node_low[...] = low
    coef[...] = packed(link_coef[...])
    nodes[...] = gathered(table, 64, high, low)


def swept(state, gains):
    def once(_, w):
        return (
            gains[0] * w
            + gains[1] * pltpu.roll(w, 1, 0)
            + gains[2] * pltpu.roll(w, 71, 0)
            + gains[3] * pltpu.roll(w, 1, 1)
            + gains[4] * pltpu.roll(w, 383, 1)
            + gains[5]
        )

    for i in range(SWEEPS):
        state = once(i, state)
    return state


def put(out, blocks, index, value):
    out[pl.ds(index, 128, stride=blocks), :] = value


def taken(got, blocks, index):
    return got[pl.ds(index, 128, stride=blocks), :]


def build_message(out, heads, nodes):
    put(out, 6, 0, paired(heads, nodes))
    put(out, 6, 1, beside(nodes))


def zone_heads(edge, zone_place, edge_ref, zone_ref):
    lane = iota((64, 128), 1)
    edge_ref[...] = jnp.where(lane < ZONE, edge, pltpu.roll(edge, 2 * ZONE, 1))
    lane8 = iota((8, 128), 1)
    table = jnp.zeros((8, 128), F32)
    for s in range(8):
        line = edge_ref[pl.ds(s, 8, stride=8), :]
        if s:
            line = pltpu.roll(line, s * 16, 1)
        table = jnp.where((lane8 >> 4) == s, line, table)
    zone_ref[...] = table
    zone_row, zone_col = zone_place
    high = jnp.where(zone_row >= 0, zone_row >> 3, -1)
    low = jnp.bitwise_and(zone_row, 7) * 16 + zone_col
    return gathered(zone_ref, 8, high, low)


def sweep_and_gather(
    state, gains, cell_high, cell_low, zone_place, surface_out, heads_out, zone_out, cell_table,
    edge_ref, zone_ref,
):
    state = swept(state, gains)
    surface_out[...] = state[:64]
    cell_table[0:64, :] = state[:64, 0:128]
    cell_table[64:128, :] = state[:64, 128:256]
    heads = gathered(cell_table, 128, cell_high, cell_low)
    heads_out[...] = heads
    if zone_place is not None:
        zone_out[...] = zone_heads(state[:64, 256:384], zone_place, edge_ref, zone_ref)
    return heads


def first_sweep_kernel(
    place_ref, tall, near_col, far_col, near, link_cell, table, nodes, coef,
    gains_out, inverse_out, cell_high, cell_low, zone_row_out, zone_col_out, surface_out, heads_out,
    zone_out, out, cell_table, edge_ref, zone_ref,
):
    lane = iota((72, 128), 1)
    wide = []
    from_west = jnp.where(even(place_ref, 1), far_col[...], near_col[...])
    from_east = jnp.where(even(place_ref, 1), near_col[...], far_col[...])
    for index in range(5):
        west = jnp.where(place_ref[1] > 0, from_west[0:72, :], 0.0)
        east = jnp.where(place_ref[1] < 15, from_east[0:72, :], 0.0)
        if index:
            west = pltpu.roll(west, 128 - index * 2 * HALO_COLS, 1)
            east = pltpu.roll(east, 128 - index * 2 * HALO_COLS, 1)
        edge = jnp.where(
            lane < HALO_COLS, east, jnp.where(lane >= 128 - HALO_COLS, west, 0.0)
        )
        wide.append(jnp.concatenate([tall[index], edge], axis=1))
    state, cond_x, cond_y, inverse, rainfall = wide
    north = pltpu.roll(cond_x, 1, 0)
    west = pltpu.roll(cond_y, 1, 1)
    gains = [
        1.0 - (north + cond_x + west + cond_y) * inverse,
        north * inverse, cond_x * inverse, west * inverse, cond_y * inverse, rainfall,
    ]
    for index, gain in enumerate(gains):
        gains_out[index] = gain
    inverse_out[...] = inverse[:64]
    cells = paired(from_west[72:136, :], from_east[72:136, :]).astype(jnp.int32)
    col = jnp.bitwise_and(cells, 255)
    is_west = iota((128, 128), 1) < 64
    zone_col = jnp.where(is_west, col - (256 - 2 * ZONE), col)
    inside = (zone_col >= 0) & (zone_col < 2 * ZONE)
    inside = inside & (jnp.where(is_west, zone_col, zone_col + ZONE) >= ZONE)
    zone_row = jnp.where((cells >= 0) & inside & (jnp.where(is_west, 0, zone_col) < ZONE), cells >> 8, -1)
    zone_row_out[...] = zone_row
    zone_col_out[...] = zone_col
    high, low = cell_place(packed(link_cell[...]))
    cell_high[...] = high
    cell_low[...] = low
    heads = sweep_and_gather(
        state, gains, high, low, (zone_row, zone_col), surface_out, heads_out, zone_out,
        cell_table, edge_ref, zone_ref,
    )
    build_message(out, heads, nodes[...])
    own_rows = (iota((128, 128), 0) >> 4) == place_ref[0]
    for half in range(2):
        own = jnp.broadcast_to(table[half * 32 : half * 32 + 1, :], (128, 128))
        other = jnp.broadcast_to(near[40 + half : 41 + half, :], (128, 128))
        put(out, 6, 2 + half, jnp.where(own_rows, own, other))
    put(out, 6, 4, paired(coef[...], coef[...]))
    put(out, 6, 5, beside(coef[...]))


def sweep_kernel(
    last, place_ref, surface, near, far, gains_ref, cell_high, cell_low, zone_row, zone_col,
    table, nodes, surface_out, heads_out, zone_out, out, cell_table, edge_ref, zone_ref,
):
    state = jnp.concatenate(
        [
            tall_block(
                place_ref, surface[:, block * 128 : block * 128 + 128], near, far, block * 4
            )
            for block in range(3)
        ],
        axis=1,
    )
    gains = [gains_ref[index] for index in range(6)]
    zone_place = None if last else (zone_row[...], zone_col[...])
    heads = sweep_and_gather(
        state, gains, cell_high[...], cell_low[...], zone_place, surface_out, heads_out, zone_out,
        cell_table, edge_ref, zone_ref,
    )
    build_message(out, heads, nodes[...])
    for index, row in enumerate(ENDS):
        put(out, 6, 2 + index, jnp.broadcast_to(table[row : row + 1, :], (128, 128)))


def tile_kernel(
    first, last, place_ref, got, surface, inverse, heads, zone, cell_high, cell_low, zone_row, zone_col, *rest
):
    rest = list(rest)
    if first:
        own_coef = low_halves(taken(got, 6, 4))
        zone_coef = taken(got, 6, 5)
    else:
        own_coef = rest.pop(0)[...]
        zone_coef = rest.pop(0)[...]
    surface_out = rest.pop(0)
    if not last:
        near, far = rest.pop(0), rest.pop(0)
    if first:
        rest.pop(0)[...] = own_coef
        rest.pop(0)[...] = zone_coef
    value_ref, zone_value_ref = rest
    value_ref[...] = jnp.where(
        cell_high[...] >= 0, own_coef * (heads[...] - high_halves(taken(got, 6, 0))), 0.0
    )
    lost = summed(cell_high, cell_low, value_ref, 128, 128)
    left = surface[:, 0:128] - inverse[:, 0:128] * lost[:64]
    right = surface[:, 128:256] - inverse[:, 128:256] * lost[64:]
    surface_out[:, 0:128] = left
    surface_out[:, 128:256] = right
    if last:
        return
    zone_value_ref[...] = jnp.where(
        zone_row[...] >= 0, zone_coef * (zone[...] - taken(got, 6, 1)), 0.0
    )
    lost = summed(zone_row, zone_col, zone_value_ref, 64, 2 * ZONE)
    lost = jnp.concatenate([lost, jnp.zeros((64, 128 - 2 * ZONE), F32)], axis=1)
    lane = iota((64, 128), 1)
    lost = jnp.where(
        lane < ZONE, lost,
        jnp.where(lane >= 128 - ZONE, pltpu.roll(lost, 128 - 2 * ZONE, 1), 0.0),
    )
    edge = surface[:, 256:384] - inverse[:, 256:384] * lost
    surface_out[:, 256:384] = edge
    top, bottom = strips([left, right, edge], 0), strips([left, right, edge], 60)
    near[...] = jnp.where(even(place_ref, 0), bottom, top)
    far[...] = jnp.where(even(place_ref, 0), top, bottom)


def owner_kernel(
    first, last, place_ref, got, nodes, node_high, node_low, coef, table, meets, classes, matrices, *rest
):
    if last:
        pipes_out, value_ref, ends_ref = rest
    else:
        table_out, nodes_out, value_ref, ends_ref = rest
    value_ref[...] = jnp.where(
        node_high[...] >= 0, coef[...] * (low_halves(taken(got, 6, 0)) - nodes[...]), 0.0
    )
    inflow = summed(node_high, node_low, value_ref, 64, 128)
    balance = table[...] + inflow
    start = pl.multiple_of(place_ref[0] * 96, 32)
    other = pl.multiple_of((place_ref[0] ^ 1) * 96, 32) if first else start
    for index in range(4):
        source, block = (other, index) if first and index >= 2 else (start, 2 + index)
        ends_ref[index * 16 : index * 16 + 16, :] = got[pl.ds(source + block, 16, stride=6), :]
    meet = meets[...]
    meet_high = jnp.bitwise_and(meet >> 7, 1) * 16 + (meet >> 8)
    meet_high = jnp.where(iota((8, 128), 0) < 2, meet_high + 32, meet_high)
    met = gathered(ends_ref, 64, meet_high, meet) * boundary_gain
    node_row = iota((32, 128), 0)
    parts = []
    for half in range(2):
        part = balance[half * 32 : half * 32 + 32]
        part = part + jnp.where(
            node_row == 0, met[half : half + 1],
            jnp.where(node_row == 31, met[2 + half : 3 + half], 0.0),
        )
        products = jnp.dot(
            matrices[...], part, precision=lax.Precision.HIGHEST, preferred_element_type=F32
        )
        kind = classes[half : half + 1, :]
        updated = jnp.zeros((32, 128), F32)
        for index in range(CLASSES):
            updated = jnp.where(kind == index, products[index * 32 : index * 32 + 32], updated)
        parts.append(updated)
    if last:
        pipes_out[:, 0:128] = parts[0]
        pipes_out[:, 128:256] = parts[1]
        return
    table_out[0:32, :] = parts[0]
    table_out[32:64, :] = parts[1]
    nodes_out[...] = gathered(table_out, 64, node_high[...], node_low[...])


def final_kernel(
    place_ref, got, surface, inverse, heads, zone, cell_high, cell_low, zone_row, zone_col, own_coef,
    zone_coef, nodes, node_high, node_low, coef, table, meets, classes, matrices, surface_out,
    pipes_out, cell_value_ref, zone_value_ref, node_value_ref, ends_ref,
):
    owner_kernel(
        False, True, place_ref, got, nodes, node_high, node_low, coef, table, meets, classes,
        matrices, pipes_out, node_value_ref, ends_ref,
    )
    tile_kernel(
        False, True, place_ref, got, surface, inverse, heads, zone, cell_high, cell_low, zone_row, zone_col,
        own_coef, zone_coef, surface_out, cell_value_ref, zone_value_ref,
    )


def shape(*dims, dtype=F32):
    return jax.ShapeDtypeStruct(dims, dtype)


def call(kernel, inputs, outputs, scratch=(), scalars=0, space=pltpu.VMEM, grant=32):
    smem = pl.BlockSpec(memory_space=pltpu.SMEM)
    vmem = pl.BlockSpec(memory_space=pltpu.VMEM)
    return pl.pallas_call(
        kernel,
        out_shape=outputs,
        in_specs=[smem] * scalars + [pl.BlockSpec(memory_space=space)] * (len(inputs) - scalars),
        out_specs=[vmem] * len(outputs),
        scratch_shapes=list(scratch),
        compiler_params=pltpu.CompilerParams(vmem_limit_bytes=grant << 20),
        cost_estimate=pl.CostEstimate(flops=10**9, bytes_accessed=1 << 20, transcendentals=0),
    )(*inputs)


def swapped(near, far, dim):
    sizes = lax.axis_size("row"), lax.axis_size("col")
    routes = [], []
    for row in range(sizes[0]):
        for col in range(sizes[1]):
            here = [row, col]
            partner = list(here)
            partner[dim] ^= 1
            other = list(here)
            other[dim] += 1 if here[dim] % 2 else -1
            if not 0 <= other[dim] < sizes[dim]:
                other = list(here)
                other[1 - dim] ^= 1
            for route, there in zip(routes, (partner, other)):
                route.append((row * sizes[1] + col, there[0] * sizes[1] + there[1]))
    return (
        lax.ppermute(near, ("row", "col"), routes[0]),
        lax.ppermute(far, ("row", "col"), routes[1]),
    )


def body(
    surface_head, conduct_x, conduct_y, porosity, rainfall, pipe_head, pipe_class, pipe_up,
    pipe_down, pipe_matrices, link_cell, link_node, link_coef,
):
    place = jnp.stack([lax.axis_index("row"), lax.axis_index("col")]).astype(jnp.int32)
    link_cell = link_cell[0]
    link_node = link_node[:, 0, :]
    link_coef = link_coef[:, 0, :]
    meets = jnp.concatenate(
        [pipe_up.reshape(2, 128), pipe_down.reshape(2, 128), jnp.zeros((4, 128), jnp.int32)], axis=0
    )
    classes = pipe_class.reshape(2, 128)
    matrices = pipe_matrices.reshape(CLASSES * 32, 32)
    ints = functools.partial(shape, dtype=jnp.int32)

    fields, near, far = call(
        start_kernel,
        (place, *(pltpu.with_memory_space_constraint(x, pltpu.HBM) for x in (
            surface_head, conduct_x, conduct_y, porosity, rainfall, pipe_head
        ))),
        [shape(5, 64, 256), shape(48, 128), shape(40, 128)],
        [pltpu.VMEM((8, 256), F32), pltpu.SemaphoreType.DMA((6,))], scalars=1, space=pltpu.HBM,
    )
    near, far = swapped(near, far, 0)
    tall, sent = call(
        pack_cols_kernel, (place, near, far, fields, link_cell),
        [shape(5, 72, 256), shape(136, 128)], scalars=1,
    )
    near_col, far_col = swapped(sent, sent, 1)
    table, nodes, node_high, node_low, coef, classes, matrices = call(
        owner_start_kernel, (pipe_head, link_node, link_coef, classes, matrices),
        [shape(64, 128), shape(64, 128), ints(64, 128), ints(64, 128), shape(64, 128),
         ints(2, 128), shape(128, 32)],
    )
    gather_scratch = [
        pltpu.VMEM((128, 128), F32), pltpu.VMEM((64, 128), F32), pltpu.VMEM((8, 128), F32)
    ]
    swept_shapes = [shape(64, 384), shape(64, 128), shape(128, 128)]
    (gains, inverse, cell_high, cell_low, zone_row, zone_col, surface, heads, zone, sent) = call(
        first_sweep_kernel,
        (place, tall, near_col, far_col, near, link_cell, table, nodes, coef),
        [shape(6, 72, 384), shape(64, 384), ints(64, 128), ints(64, 128), ints(128, 128),
         ints(128, 128), *swept_shapes, shape(768, 128)],
        gather_scratch, scalars=1,
    )
    sent, meets = lax.optimization_barrier((sent, meets))
    coefs = ()
    for step in range(STEPS):
        first, last = step == 0, step == STEPS - 1
        if step:
            surface, heads, zone, sent = call(
                functools.partial(sweep_kernel, last),
                (place, surface, near, far, gains, cell_high, cell_low, zone_row, zone_col,
                 table, nodes),
                [*swept_shapes, shape(768, 128)], gather_scratch, scalars=1,
            )
        got = lax.all_to_all(
            sent.reshape(128, 1, -1), ("row", "col"), split_axis=0, concat_axis=0, tiled=True
        ).reshape(-1, 128)
        tile_inputs = (surface, inverse, heads, zone, cell_high, cell_low, zone_row, zone_col, *coefs)
        owner_inputs = (nodes, node_high, node_low, coef, table, meets, classes, matrices)
        tile_scratch = [pltpu.VMEM((64, 128), F32), pltpu.VMEM((128, 128), F32)]
        owner_scratch = [pltpu.VMEM((64, 128), F32), pltpu.VMEM((64, 128), F32)]
        if last:
            return tuple(call(
                final_kernel, (place, got, *tile_inputs, *owner_inputs),
                [shape(64, 256), shape(32, 256)], tile_scratch + owner_scratch, scalars=1,
            ))
        outputs = [shape(64, 384), shape(12, 128), shape(12, 128)]
        if first:
            outputs += [shape(64, 128), shape(128, 128)]
        surface, near, far, *new_coefs = call(
            functools.partial(tile_kernel, first, False), (place, got, *tile_inputs), outputs,
            tile_scratch, scalars=1,
        )
        near, far = swapped(near, far, 0)
        table, nodes = call(
            functools.partial(owner_kernel, first, False), (place, got, *owner_inputs),
            [shape(64, 128), shape(64, 128)], owner_scratch, scalars=1,
        )
        if first:
            coefs = tuple(new_coefs)


def solution(mesh):
    placed = (
        P("row", "col"),
        P("row", "col"),
        P("row", "col"),
        P("row", "col"),
        P("row", "col"),
        P(None, ("row", "col")),
        P(("row", "col")),
        P(("row", "col")),
        P(("row", "col")),
        P(),
        P(("row", "col"), None, None),
        P(None, ("row", "col"), None),
        P(None, ("row", "col"), None),
    )
    return jax.shard_map(
        body,
        mesh=mesh,
        in_specs=placed,
        out_specs=(P("row", "col"), P(None, ("row", "col"))),
        check_vma=False,
    )
```

```python
import functools

import jax
import jax.numpy as jnp
from jax import lax
from jax.experimental import pallas as pl
from jax.experimental.pallas import tpu as pltpu
from jax.sharding import PartitionSpec as P

CLASSES = 4
SWEEPS = 4
STEPS = 3
F32 = jnp.float32
BF16 = jnp.bfloat16

boundary_gain = 0.5

HALO_ROWS = 4
HALO_COLS = 12
ZONE = 8
ENDS = (0, 32, 31, 63)


def iota(shape, dim):
    return lax.broadcasted_iota(jnp.int32, shape, dim)


def packed(x):
    return jnp.concatenate([x[:64], x[64:]], axis=1)


def low_halves(block):
    lane = iota((64, 128), 1)
    return jnp.where(lane < 64, block[:64], pltpu.roll(block[64:], 64, 1))


def high_halves(block):
    lane = iota((64, 128), 1)
    return jnp.where(lane < 64, pltpu.roll(block[:64], 64, 1), block[64:])


def paired(low, high):
    lane = iota((64, 128), 1)
    top = jnp.where(lane < 64, low, pltpu.roll(high, 64, 1))
    bottom = jnp.where(lane < 64, pltpu.roll(low, 64, 1), high)
    return jnp.concatenate([top, bottom], axis=0)


def beside(values):
    lane = iota((128, 128), 1)
    both = paired(values, values)
    return jnp.where(lane < 64, pltpu.roll(both, 1, 0), pltpu.roll(both, 127, 0))


def gathered(table_ref, rows, high, low):
    low = jnp.bitwise_and(low, 127)
    tiles = []
    for start in range(0, high.shape[0], 8):
        tile_high, tile_low = high[start : start + 8], low[start : start + 8]
        found = jnp.zeros((8, 128), F32)
        for row in range(rows):
            line = jnp.broadcast_to(table_ref[row : row + 1, :], (8, 128))
            values = jnp.take_along_axis(line, tile_low, axis=1)
            found = jnp.where(tile_high == row, values, found)
        tiles.append(found)
    return jnp.concatenate(tiles, axis=0) if len(tiles) > 1 else tiles[0]


def gathered_by_product(table, high_ref, low_ref, tiles):
    coarse = table.astype(BF16)
    fine = (table - coarse.astype(F32)).astype(BF16)
    parts = jnp.concatenate([coarse, fine], axis=1)
    row_iota = iota((128, 128), 0)
    high_iota = row_iota.astype(F32).astype(BF16)
    one, zero = jnp.ones((128, 128), BF16), jnp.zeros((128, 128), BF16)
    found = []
    for start in range(0, 8 * tiles, 8):
        high = high_ref[start : start + 8, :].astype(F32)
        low = low_ref[start : start + 8, :]
        hot = jnp.concatenate(
            [
                jnp.where(repeated(high[j : j + 1], 128) == high_iota, one, zero)
                for j in range(8)
            ],
            axis=1,
        )
        lines = lax.dot_general(
            parts, hot, (((0,), (0,)), ((), ())), preferred_element_type=F32
        )
        lines = lines[:128] + lines[128:]
        for j in range(8):
            line = jnp.where(
                row_iota == low[j : j + 1], lines[:, j * 128 : j * 128 + 128], 0.0
            )
            found.append(jnp.sum(line, axis=0, keepdims=True))
    return jnp.concatenate(found, axis=0)


def repeated(line, size):
    block = jnp.broadcast_to(line, (16, 128)).astype(BF16)
    return jnp.concatenate([block] * (size // 16), axis=0) if size > 16 else block


def summed(high_ref, low_ref, value_ref, high_size, low_size, by_low=False):
    refs, sizes = (high_ref, low_ref), (high_size, low_size)
    bearer = 1 if by_low else 0
    iotas = [iota((size, 128), 0).astype(F32).astype(BF16) for size in sizes]
    zeros = [jnp.zeros((size, 128), BF16) for size in sizes]
    one = jnp.ones((sizes[1 - bearer], 128), BF16)
    total = None
    for start in range(0, high_ref.shape[0], 8):
        places = [ref[start : start + 8, :].astype(F32) for ref in refs]
        value = value_ref[start : start + 8, :]
        coarse = value.astype(BF16).astype(F32)
        fine = value - coarse
        size, zero = sizes[bearer], zeros[bearer]
        coarse_hot, fine_hot, plain_hot = [], [], []
        for j in range(8):
            same = [
                repeated(places[side][j : j + 1], sizes[side]) == iotas[side] for side in range(2)
            ]
            coarse_hot.append(jnp.where(same[bearer], repeated(coarse[j : j + 1], size), zero))
            fine_hot.append(jnp.where(same[bearer], repeated(fine[j : j + 1], size), zero))
            plain_hot.append(jnp.where(same[1 - bearer], one, zeros[1 - bearer]))
        value_hot = jnp.concatenate(
            [jnp.concatenate(coarse_hot, axis=1), jnp.concatenate(fine_hot, axis=1)], axis=0
        )
        plain_hot = jnp.concatenate(plain_hot, axis=1)
        sides = (plain_hot, value_hot) if by_low else (value_hot, plain_hot)
        product = lax.dot_general(
            *sides, (((1,), (1,)), ((), ())), preferred_element_type=F32
        )
        total = product if total is None else total + product
    if by_low:
        return total[:, :low_size] + total[:, low_size:]
    return total[:high_size] + total[high_size:]


def cell_place(cell):
    high = jnp.where(
        cell >= 0, jnp.bitwise_and(cell >> 7, 1) * 64 + (cell >> 8), -1
    )
    return high, jnp.bitwise_and(cell, 127)


def node_place(node):
    high = jnp.where(
        node >= 0, jnp.bitwise_and(node >> 7, 1) * 32 + (node >> 8), -1
    )
    return high, jnp.bitwise_and(node, 127)


def pipe_table(state):
    return jnp.concatenate([state[:, :128], state[:, 128:]], axis=0)


def strips(blocks, start):
    return jnp.concatenate([block[start : start + HALO_ROWS] for block in blocks], axis=0)


def row_col():
    return lax.axis_index("row"), lax.axis_index("col")


def even(dim):
    return jnp.bitwise_and(row_col()[dim], 1) == 0


def start_kernel(
    surface, cond_x, cond_y, porosity, rainfall, pipes, fields, near, far, tips, arrived
):
    copies = [
        pltpu.make_async_copy(source, fields.at[index], arrived.at[index])
        for index, source in enumerate((surface, cond_x, cond_y, porosity, rainfall))
    ]
    copies.append(pltpu.make_async_copy(pipes.at[24:32, :], tips, arrived.at[5]))
    for copy in copies:
        copy.start()
    for copy in copies:
        copy.wait()
    fields[3] = 1.0 / fields[3]
    for index in range(5):
        halves = [fields[index, :, 0:128], fields[index, :, 128:256]]
        top, bottom = strips(halves, 0), strips(halves, 60)
        near[pl.ds(index * 8, 8), :] = jnp.where(even(0), bottom, top)
        far[pl.ds(index * 8, 8), :] = jnp.where(even(0), top, bottom)
    near[40:48, :] = jnp.concatenate(
        [tips[7:8, 0:128], tips[7:8, 128:256], jnp.zeros((6, 128), F32)], axis=0
    )


def tall_block(block, near, far, start):
    near, far = near[start : start + 4, :], far[start : start + 4, :]
    over = jnp.where(even(0), far, near)
    under = jnp.where(even(0), near, far)
    over = jnp.where(row_col()[0] > 0, over, 0.0)
    under = jnp.where(row_col()[0] < 7, under, 0.0)
    return jnp.concatenate([block, under, over], axis=0)


def pack_cols_kernel(near, far, fields, link_cell, tall_out, out):
    lane = iota((72, 128), 1)
    message = jnp.zeros((72, 128), F32)
    for index in range(5):
        tall = [
            tall_block(
                fields[index, :, half * 128 : half * 128 + 128], near, far,
                index * 8 + half * 4,
            )
            for half in range(2)
        ]
        tall_out[index, :, 0:128] = tall[0]
        tall_out[index, :, 128:256] = tall[1]
        edges = jnp.where(
            lane < HALO_COLS, tall[0], jnp.where(lane >= 128 - HALO_COLS, tall[1], 0.0)
        )
        if index:
            edges = pltpu.roll(edges, index * 2 * HALO_COLS, 1)
        message = message + edges
    out[0:72, :] = message
    out[72:136, :] = packed(link_cell[...]).astype(F32)


def owner_start_kernel(
    pipes, link_node, link_coef, kinds, laws, table, nodes, node_high, node_low, coef, classes,
    matrices,
):
    classes[...] = kinds[...]
    matrices[...] = laws[...]
    table[...] = pipe_table(pipes[...])
    high, low = node_place(packed(link_node[...]))
    node_high[...] = high
    node_low[...] = low
    coef[...] = packed(link_coef[...])
    nodes[...] = gathered(table, 64, high, low)


def swept(state, gains):
    def once(_, w):
        return (
            gains[0] * w
            + gains[1] * pltpu.roll(w, 1, 0)
            + gains[2] * pltpu.roll(w, 71, 0)
            + gains[3] * pltpu.roll(w, 1, 1)
            + gains[4] * pltpu.roll(w, 383, 1)
            + gains[5]
        )

    for i in range(SWEEPS):
        state = once(i, state)
    return state


def put(out, blocks, index, value):
    out[pl.ds(index, 128, stride=blocks), :] = value


def taken(got, blocks, index):
    return got[pl.ds(index, 128, stride=blocks), :]


def build_message(out, heads, nodes):
    put(out, 6, 0, paired(heads, nodes))
    put(out, 6, 1, beside(nodes))


def zone_heads(edge, zone_place, edge_ref, zone_ref):
    lane = iota((64, 128), 1)
    edge_ref[...] = jnp.where(lane < ZONE, edge, pltpu.roll(edge, 2 * ZONE, 1))
    lane8 = iota((8, 128), 1)
    table = jnp.zeros((8, 128), F32)
    for s in range(8):
        line = edge_ref[pl.ds(s, 8, stride=8), :]
        if s:
            line = pltpu.roll(line, s * 16, 1)
        table = jnp.where((lane8 >> 4) == s, line, table)
    zone_ref[...] = table
    zone_row, zone_col = zone_place
    high = jnp.where(zone_row >= 0, zone_row >> 3, -1)
    low = jnp.bitwise_and(zone_row, 7) * 16 + zone_col
    return gathered(zone_ref, 8, high, low)


def sweep_and_gather(
    state, gains, cell_high, cell_low, zone_place, surface_out, heads_out, zone_out, cell_table,
    edge_ref, zone_ref,
):
    state = swept(state, gains)
    surface_out[...] = state[:64]
    cell_table[0:64, :] = state[:64, 0:128]
    cell_table[64:128, :] = state[:64, 128:256]
    heads = jnp.concatenate(
        [
            gathered_by_product(cell_table[...], cell_high, cell_low, 4),
            gathered(cell_table, 128, cell_high[32:64, :], cell_low[32:64, :]),
        ],
        axis=0,
    )
    heads_out[...] = heads
    if zone_place is not None:
        zone_out[...] = zone_heads(state[:64, 256:384], zone_place, edge_ref, zone_ref)
    return heads


def first_sweep_kernel(
    tall, near_col, far_col, near, link_cell, table, nodes, coef,
    gains_out, inverse_out, cell_high, cell_low, zone_row_out, zone_col_out, surface_out, heads_out,
    zone_out, out, cell_table, edge_ref, zone_ref,
):
    lane = iota((72, 128), 1)
    wide = []
    from_west = jnp.where(even(1), far_col[...], near_col[...])
    from_east = jnp.where(even(1), near_col[...], far_col[...])
    for index in range(5):
        west = jnp.where(row_col()[1] > 0, from_west[0:72, :], 0.0)
        east = jnp.where(row_col()[1] < 15, from_east[0:72, :], 0.0)
        if index:
            west = pltpu.roll(west, 128 - index * 2 * HALO_COLS, 1)
            east = pltpu.roll(east, 128 - index * 2 * HALO_COLS, 1)
        edge = jnp.where(
            lane < HALO_COLS, east, jnp.where(lane >= 128 - HALO_COLS, west, 0.0)
        )
        wide.append(jnp.concatenate([tall[index], edge], axis=1))
    state, cond_x, cond_y, inverse, rainfall = wide
    north = pltpu.roll(cond_x, 1, 0)
    west = pltpu.roll(cond_y, 1, 1)
    gains = [
        1.0 - (north + cond_x + west + cond_y) * inverse,
        north * inverse, cond_x * inverse, west * inverse, cond_y * inverse, rainfall,
    ]
    for index, gain in enumerate(gains):
        gains_out[index] = gain
    inverse_out[...] = inverse[:64]
    cells = paired(from_west[72:136, :], from_east[72:136, :]).astype(jnp.int32)
    col = jnp.bitwise_and(cells, 255)
    is_west = iota((128, 128), 1) < 64
    zone_col = jnp.where(is_west, col - (256 - 2 * ZONE), col)
    inside = (zone_col >= 0) & (zone_col < 2 * ZONE)
    inside = inside & (jnp.where(is_west, zone_col, zone_col + ZONE) >= ZONE)
    zone_row = jnp.where((cells >= 0) & inside & (jnp.where(is_west, 0, zone_col) < ZONE), cells >> 8, -1)
    zone_row_out[...] = zone_row
    zone_col_out[...] = zone_col
    high, low = cell_place(packed(link_cell[...]))
    cell_high[...] = high
    cell_low[...] = low
    heads = sweep_and_gather(
        state, gains, cell_high, cell_low, (zone_row, zone_col), surface_out, heads_out, zone_out,
        cell_table, edge_ref, zone_ref,
    )
    build_message(out, heads, nodes[...])
    own_rows = (iota((128, 128), 0) >> 4) == row_col()[0]
    for half in range(2):
        own = jnp.broadcast_to(table[half * 32 : half * 32 + 1, :], (128, 128))
        other = jnp.broadcast_to(near[40 + half : 41 + half, :], (128, 128))
        put(out, 6, 2 + half, jnp.where(own_rows, own, other))
    put(out, 6, 4, paired(coef[...], coef[...]))
    put(out, 6, 5, beside(coef[...]))


def sweep_kernel(
    last, surface, near, far, gains_ref, cell_high, cell_low, zone_row, zone_col,
    table, nodes, surface_out, heads_out, zone_out, out, cell_table, edge_ref, zone_ref,
):
    state = jnp.concatenate(
        [
            tall_block(
                surface[:, block * 128 : block * 128 + 128], near, far, block * 4
            )
            for block in range(3)
        ],
        axis=1,
    )
    gains = [gains_ref[index] for index in range(6)]
    zone_place = None if last else (zone_row[...], zone_col[...])
    heads = sweep_and_gather(
        state, gains, cell_high, cell_low, zone_place, surface_out, heads_out, zone_out,
        cell_table, edge_ref, zone_ref,
    )
    build_message(out, heads, nodes[...])
    for index, row in enumerate(ENDS):
        put(out, 6, 2 + index, jnp.broadcast_to(table[row : row + 1, :], (128, 128)))


def tile_kernel(
    first, last, got, surface, inverse, heads, zone, cell_high, cell_low, zone_row, zone_col, *rest
):
    rest = list(rest)
    if first:
        own_coef = low_halves(taken(got, 6, 4))
        zone_coef = taken(got, 6, 5)
    else:
        own_coef = rest.pop(0)[...]
        zone_coef = rest.pop(0)[...]
    surface_out = rest.pop(0)
    if not last:
        near, far = rest.pop(0), rest.pop(0)
    if first:
        rest.pop(0)[...] = own_coef
        rest.pop(0)[...] = zone_coef
    value_ref, zone_value_ref = rest
    value_ref[...] = jnp.where(
        cell_high[...] >= 0, own_coef * (heads[...] - high_halves(taken(got, 6, 0))), 0.0
    )
    lost = summed(cell_high, cell_low, value_ref, 128, 128)
    left = surface[:, 0:128] - inverse[:, 0:128] * lost[:64]
    right = surface[:, 128:256] - inverse[:, 128:256] * lost[64:]
    surface_out[:, 0:128] = left
    surface_out[:, 128:256] = right
    if last:
        return
    zone_value_ref[...] = jnp.where(
        zone_row[...] >= 0, zone_coef * (zone[...] - taken(got, 6, 1)), 0.0
    )
    lost = summed(zone_row, zone_col, zone_value_ref, 64, 2 * ZONE, by_low=True)
    lost = jnp.concatenate([lost, jnp.zeros((64, 128 - 2 * ZONE), F32)], axis=1)
    lane = iota((64, 128), 1)
    lost = jnp.where(
        lane < ZONE, lost,
        jnp.where(lane >= 128 - ZONE, pltpu.roll(lost, 128 - 2 * ZONE, 1), 0.0),
    )
    edge = surface[:, 256:384] - inverse[:, 256:384] * lost
    surface_out[:, 256:384] = edge
    top, bottom = strips([left, right, edge], 0), strips([left, right, edge], 60)
    near[...] = jnp.where(even(0), bottom, top)
    far[...] = jnp.where(even(0), top, bottom)


def owner_kernel(
    first, last, got, nodes, node_high, node_low, coef, table, meets, classes, matrices, *rest
):
    if last:
        pipes_out, value_ref, ends_ref = rest
    else:
        table_out, nodes_out, value_ref, ends_ref = rest
    value_ref[...] = jnp.where(
        node_high[...] >= 0, coef[...] * (low_halves(taken(got, 6, 0)) - nodes[...]), 0.0
    )
    inflow = summed(node_high, node_low, value_ref, 64, 128)
    balance = table[...] + inflow
    start = pl.multiple_of(row_col()[0] * 96, 32)
    other = pl.multiple_of((row_col()[0] ^ 1) * 96, 32) if first else start
    for index in range(4):
        source, block = (other, index) if first and index >= 2 else (start, 2 + index)
        ends_ref[index * 16 : index * 16 + 16, :] = got[pl.ds(source + block, 16, stride=6), :]
    meet = meets[...]
    meet_high = jnp.bitwise_and(meet >> 7, 1) * 16 + (meet >> 8)
    meet_high = jnp.where(iota((8, 128), 0) < 2, meet_high + 32, meet_high)
    met = gathered(ends_ref, 64, meet_high, meet) * boundary_gain
    node_row = iota((32, 128), 0)
    parts = []
    for half in range(2):
        part = balance[half * 32 : half * 32 + 32]
        part = part + jnp.where(
            node_row == 0, met[half : half + 1],
            jnp.where(node_row == 31, met[2 + half : 3 + half], 0.0),
        )
        products = jnp.dot(
            matrices[...], part, precision=lax.Precision.HIGHEST, preferred_element_type=F32
        )
        kind = classes[half : half + 1, :]
        updated = jnp.zeros((32, 128), F32)
        for index in range(CLASSES):
            updated = jnp.where(kind == index, products[index * 32 : index * 32 + 32], updated)
        parts.append(updated)
    if last:
        pipes_out[:, 0:128] = parts[0]
        pipes_out[:, 128:256] = parts[1]
        return
    table_out[0:32, :] = parts[0]
    table_out[32:64, :] = parts[1]
    nodes_out[...] = gathered(table_out, 64, node_high[...], node_low[...])


def final_kernel(
    got, surface, inverse, heads, zone, cell_high, cell_low, zone_row, zone_col, own_coef,
    zone_coef, nodes, node_high, node_low, coef, table, meets, classes, matrices, surface_out,
    pipes_out, cell_value_ref, zone_value_ref, node_value_ref, ends_ref,
):
    owner_kernel(
        False, True, got, nodes, node_high, node_low, coef, table, meets, classes,
        matrices, pipes_out, node_value_ref, ends_ref,
    )
    tile_kernel(
        False, True, got, surface, inverse, heads, zone, cell_high, cell_low, zone_row, zone_col,
        own_coef, zone_coef, surface_out, cell_value_ref, zone_value_ref,
    )


def shape(*dims, dtype=F32):
    return jax.ShapeDtypeStruct(dims, dtype)


def call(kernel, inputs, outputs, scratch=(), space=pltpu.VMEM):
    vmem = pl.BlockSpec(memory_space=pltpu.VMEM)
    return pl.pallas_call(
        kernel,
        out_shape=outputs,
        in_specs=[pl.BlockSpec(memory_space=space)] * len(inputs),
        out_specs=[vmem] * len(outputs),
        scratch_shapes=list(scratch),
        compiler_params=pltpu.CompilerParams(vmem_limit_bytes=32 << 20),
        cost_estimate=pl.CostEstimate(flops=10**9, bytes_accessed=1 << 20, transcendentals=0),
    )(*inputs)


def swapped(near, far, dim):
    sizes = lax.axis_size("row"), lax.axis_size("col")
    routes = [], []
    for row in range(sizes[0]):
        for col in range(sizes[1]):
            here = [row, col]
            partner = list(here)
            partner[dim] ^= 1
            other = list(here)
            other[dim] += 1 if here[dim] % 2 else -1
            if not 0 <= other[dim] < sizes[dim]:
                other = list(here)
                other[1 - dim] ^= 1
            for route, there in zip(routes, (partner, other)):
                route.append((row * sizes[1] + col, there[0] * sizes[1] + there[1]))
    return (
        lax.ppermute(near, ("row", "col"), routes[0]),
        lax.ppermute(far, ("row", "col"), routes[1]),
    )


def body(
    surface_head, conduct_x, conduct_y, porosity, rainfall, pipe_head, pipe_class, pipe_up,
    pipe_down, pipe_matrices, link_cell, link_node, link_coef,
):
    link_cell = link_cell[0]
    meets = jnp.concatenate(
        [pipe_up.reshape(2, 128), pipe_down.reshape(2, 128), jnp.zeros((4, 128), jnp.int32)], axis=0
    )
    classes = pipe_class.reshape(2, 128)
    matrices = pipe_matrices.reshape(CLASSES * 32, 32)
    ints = functools.partial(shape, dtype=jnp.int32)

    fields, near, far = call(
        start_kernel,
        [pltpu.with_memory_space_constraint(x, pltpu.HBM) for x in (
            surface_head, conduct_x, conduct_y, porosity, rainfall, pipe_head
        )],
        [shape(5, 64, 256), shape(48, 128), shape(40, 128)],
        [pltpu.VMEM((8, 256), F32), pltpu.SemaphoreType.DMA((6,))], space=pltpu.HBM,
    )
    near, far = swapped(near, far, 0)
    tall, sent = call(
        pack_cols_kernel, (near, far, fields, link_cell),
        [shape(5, 72, 256), shape(136, 128)],
    )
    sent, link_node, link_coef = lax.optimization_barrier((sent, link_node, link_coef))
    link_node = link_node[:, 0, :]
    link_coef = link_coef[:, 0, :]
    near_col, far_col = swapped(sent, sent, 1)
    table, nodes, node_high, node_low, coef, classes, matrices = call(
        owner_start_kernel, (pipe_head, link_node, link_coef, classes, matrices),
        [shape(64, 128), shape(64, 128), ints(64, 128), ints(64, 128), shape(64, 128),
         ints(2, 128), shape(128, 32)],
    )
    gather_scratch = [
        pltpu.VMEM((128, 128), F32), pltpu.VMEM((64, 128), F32), pltpu.VMEM((8, 128), F32)
    ]
    swept_shapes = [shape(64, 384), shape(64, 128), shape(128, 128)]
    (gains, inverse, cell_high, cell_low, zone_row, zone_col, surface, heads, zone, sent) = call(
        first_sweep_kernel,
        (tall, near_col, far_col, near, link_cell, table, nodes, coef),
        [shape(6, 72, 384), shape(64, 384), ints(64, 128), ints(64, 128), ints(128, 128),
         ints(128, 128), *swept_shapes, shape(768, 128)],
        gather_scratch,
    )
    sent, meets = lax.optimization_barrier((sent, meets))
    coefs = ()
    for step in range(STEPS):
        first, last = step == 0, step == STEPS - 1
        if step:
            surface, heads, zone, sent = call(
                functools.partial(sweep_kernel, last),
                (surface, near, far, gains, cell_high, cell_low, zone_row, zone_col,
                 table, nodes),
                [*swept_shapes, shape(768, 128)], gather_scratch,
            )
        got = lax.all_to_all(
            sent.reshape(128, 1, -1), ("row", "col"), split_axis=0, concat_axis=0, tiled=True
        ).reshape(-1, 128)
        tile_inputs = (surface, inverse, heads, zone, cell_high, cell_low, zone_row, zone_col, *coefs)
        owner_inputs = (nodes, node_high, node_low, coef, table, meets, classes, matrices)
        tile_scratch = [pltpu.VMEM((64, 128), F32), pltpu.VMEM((128, 128), F32)]
        owner_scratch = [pltpu.VMEM((64, 128), F32), pltpu.VMEM((64, 128), F32)]
        if last:
            return tuple(call(
                final_kernel, (got, *tile_inputs, *owner_inputs),
                [shape(64, 256), shape(32, 256)], tile_scratch + owner_scratch,
            ))
        outputs = [shape(64, 384), shape(12, 128), shape(12, 128)]
        if first:
            outputs += [shape(64, 128), shape(128, 128)]
        surface, near, far, *new_coefs = call(
            functools.partial(tile_kernel, first, False), (got, *tile_inputs), outputs,
            tile_scratch,
        )
        near, far = swapped(near, far, 0)
        table, nodes = call(
            functools.partial(owner_kernel, first, False), (got, *owner_inputs),
            [shape(64, 128), shape(64, 128)], owner_scratch,
        )
        if first:
            coefs = tuple(new_coefs)


def solution(mesh):
    placed = (
        P("row", "col"),
        P("row", "col"),
        P("row", "col"),
        P("row", "col"),
        P("row", "col"),
        P(None, ("row", "col")),
        P(("row", "col")),
        P(("row", "col")),
        P(("row", "col")),
        P(),
        P(("row", "col"), None, None),
        P(None, ("row", "col"), None),
        P(None, ("row", "col"), None),
    )
    return jax.shard_map(
        body,
        mesh=mesh,
        in_specs=placed,
        out_specs=(P("row", "col"), P(None, ("row", "col"))),
        check_vma=False,
    )
```

```python
import functools

import jax
import jax.numpy as jnp
from jax import lax
from jax.experimental import pallas as pl
from jax.experimental.pallas import tpu as pltpu
from jax.sharding import PartitionSpec as P

CLASSES = 4
SWEEPS = 4
STEPS = 3
F32 = jnp.float32
BF16 = jnp.bfloat16

boundary_gain = 0.5

HALO_ROWS = 4
HALO_COLS = 12
ZONE = 8
ENDS = (0, 32, 31, 63)


def iota(shape, dim):
    return lax.broadcasted_iota(jnp.int32, shape, dim)


def packed(x):
    return jnp.concatenate([x[:64], x[64:]], axis=1)


def low_halves(block):
    lane = iota((64, 128), 1)
    return jnp.where(lane < 64, block[:64], pltpu.roll(block[64:], 64, 1))


def high_halves(block):
    lane = iota((64, 128), 1)
    return jnp.where(lane < 64, pltpu.roll(block[:64], 64, 1), block[64:])


def paired(low, high):
    lane = iota((64, 128), 1)
    top = jnp.where(lane < 64, low, pltpu.roll(high, 64, 1))
    bottom = jnp.where(lane < 64, pltpu.roll(low, 64, 1), high)
    return jnp.concatenate([top, bottom], axis=0)


def beside(values):
    lane = iota((128, 128), 1)
    both = paired(values, values)
    return jnp.where(lane < 64, pltpu.roll(both, 1, 0), pltpu.roll(both, 127, 0))


def gathered(table_ref, rows, high, low):
    low = jnp.bitwise_and(low, 127)
    tiles = []
    for start in range(0, high.shape[0], 8):
        tile_high, tile_low = high[start : start + 8], low[start : start + 8]
        found = jnp.zeros((8, 128), F32)
        for row in range(rows):
            line = jnp.broadcast_to(table_ref[row : row + 1, :], (8, 128))
            values = jnp.take_along_axis(line, tile_low, axis=1)
            found = jnp.where(tile_high == row, values, found)
        tiles.append(found)
    return jnp.concatenate(tiles, axis=0) if len(tiles) > 1 else tiles[0]


def gathered_by_product(table, high_ref, low_ref, tiles):
    coarse = table.astype(BF16)
    fine = (table - coarse.astype(F32)).astype(BF16)
    parts = jnp.concatenate([coarse, fine], axis=1)
    row_iota = iota((128, 128), 0)
    high_iota = row_iota.astype(F32).astype(BF16)
    one, zero = jnp.ones((128, 128), BF16), jnp.zeros((128, 128), BF16)
    found = []
    for start in range(0, 8 * tiles, 8):
        high = high_ref[start : start + 8, :].astype(F32)
        low = low_ref[start : start + 8, :]
        hot = jnp.concatenate(
            [
                jnp.where(repeated(high[j : j + 1], 128) == high_iota, one, zero)
                for j in range(8)
            ],
            axis=1,
        )
        lines = lax.dot_general(
            parts, hot, (((0,), (0,)), ((), ())), preferred_element_type=F32
        )
        lines = lines[:128] + lines[128:]
        for j in range(8):
            line = jnp.where(
                row_iota == low[j : j + 1], lines[:, j * 128 : j * 128 + 128], 0.0
            )
            found.append(jnp.sum(line, axis=0, keepdims=True))
    return jnp.concatenate(found, axis=0)


def repeated(line, size):
    block = jnp.broadcast_to(line, (16, 128)).astype(BF16)
    return jnp.concatenate([block] * (size // 16), axis=0) if size > 16 else block


def summed(high_ref, low_ref, value_ref, high_size, low_size, by_low=False):
    refs, sizes = (high_ref, low_ref), (high_size, low_size)
    bearer = 1 if by_low else 0
    iotas = [iota((size, 128), 0).astype(F32).astype(BF16) for size in sizes]
    zeros = [jnp.zeros((size, 128), BF16) for size in sizes]
    one = jnp.ones((sizes[1 - bearer], 128), BF16)
    total = None
    for start in range(0, high_ref.shape[0], 8):
        places = [ref[start : start + 8, :].astype(F32) for ref in refs]
        value = value_ref[start : start + 8, :]
        coarse = value.astype(BF16).astype(F32)
        fine = value - coarse
        size, zero = sizes[bearer], zeros[bearer]
        coarse_hot, fine_hot, plain_hot = [], [], []
        for j in range(8):
            same = [
                repeated(places[side][j : j + 1], sizes[side]) == iotas[side] for side in range(2)
            ]
            coarse_hot.append(jnp.where(same[bearer], repeated(coarse[j : j + 1], size), zero))
            fine_hot.append(jnp.where(same[bearer], repeated(fine[j : j + 1], size), zero))
            plain_hot.append(jnp.where(same[1 - bearer], one, zeros[1 - bearer]))
        value_hot = jnp.concatenate(
            [jnp.concatenate(coarse_hot, axis=1), jnp.concatenate(fine_hot, axis=1)], axis=0
        )
        plain_hot = jnp.concatenate(plain_hot, axis=1)
        sides = (plain_hot, value_hot) if by_low else (value_hot, plain_hot)
        product = lax.dot_general(
            *sides, (((1,), (1,)), ((), ())), preferred_element_type=F32
        )
        total = product if total is None else total + product
    if by_low:
        return total[:, :low_size] + total[:, low_size:]
    return total[:high_size] + total[high_size:]


def summed_by_columns(row_ref, value_ref, hot_ref):
    row_iota = iota((64, 128), 0).astype(F32).astype(BF16)
    zero = jnp.zeros((64, 128), BF16)
    total = jnp.zeros((128, 256), F32)
    for start in range(0, 64, 8):
        rows = row_ref[start : start + 8, :].astype(F32)
        value = value_ref[start : start + 8, :]
        coarse = value.astype(BF16).astype(F32)
        fine = value - coarse
        coarse_hot, fine_hot = [], []
        for j in range(8):
            same = repeated(rows[j : j + 1], 64) == row_iota
            coarse_hot.append(jnp.where(same, repeated(coarse[j : j + 1], 64), zero))
            fine_hot.append(jnp.where(same, repeated(fine[j : j + 1], 64), zero))
        value_hot = jnp.concatenate(
            [jnp.concatenate(coarse_hot, axis=1), jnp.concatenate(fine_hot, axis=1)], axis=0
        )
        total = total + jnp.dot(
            value_hot, hot_ref[start * 128 : start * 128 + 1024, :], preferred_element_type=F32
        )
    return total[:64] + total[64:]


def columns_kernel(link_cell, hot):
    cols = jnp.bitwise_and(packed(link_cell[...]), 255).astype(F32).T
    lane = iota((128, 256), 1).astype(F32)
    for j in range(64):
        same = jnp.broadcast_to(cols[:, j : j + 1], (128, 256)) == lane
        hot[j * 128 : j * 128 + 128, :] = jnp.where(same, 1.0, 0.0).astype(BF16)


def cell_place(cell):
    high = jnp.where(
        cell >= 0, jnp.bitwise_and(cell >> 7, 1) * 64 + (cell >> 8), -1
    )
    return high, jnp.bitwise_and(cell, 127)


def node_place(node):
    high = jnp.where(
        node >= 0, jnp.bitwise_and(node >> 7, 1) * 32 + (node >> 8), -1
    )
    return high, jnp.bitwise_and(node, 127)


def pipe_table(state):
    return jnp.concatenate([state[:, :128], state[:, 128:]], axis=0)


def strips(blocks, start):
    return jnp.concatenate([block[start : start + HALO_ROWS] for block in blocks], axis=0)


def row_col():
    return lax.axis_index("row"), lax.axis_index("col")


def even(dim):
    return jnp.bitwise_and(row_col()[dim], 1) == 0


def start_kernel(
    surface, cond_x, cond_y, porosity, rainfall, pipes, fields, near, far, tips, arrived
):
    copies = [
        pltpu.make_async_copy(source, fields.at[index], arrived.at[index])
        for index, source in enumerate((surface, cond_x, cond_y, porosity, rainfall))
    ]
    copies.append(pltpu.make_async_copy(pipes.at[24:32, :], tips, arrived.at[5]))
    for copy in copies:
        copy.start()
    for copy in copies:
        copy.wait()
    fields[3] = 1.0 / fields[3]
    for index in range(5):
        halves = [fields[index, :, 0:128], fields[index, :, 128:256]]
        top, bottom = strips(halves, 0), strips(halves, 60)
        near[pl.ds(index * 8, 8), :] = jnp.where(even(0), bottom, top)
        far[pl.ds(index * 8, 8), :] = jnp.where(even(0), top, bottom)
    near[40:48, :] = jnp.concatenate(
        [tips[7:8, 0:128], tips[7:8, 128:256], jnp.zeros((6, 128), F32)], axis=0
    )


def tall_block(block, near, far, start):
    near, far = near[start : start + 4, :], far[start : start + 4, :]
    over = jnp.where(even(0), far, near)
    under = jnp.where(even(0), near, far)
    over = jnp.where(row_col()[0] > 0, over, 0.0)
    under = jnp.where(row_col()[0] < 7, under, 0.0)
    return jnp.concatenate([block, under, over], axis=0)


def pack_cols_kernel(near, far, fields, link_cell, tall_out, out):
    lane = iota((72, 128), 1)
    message = jnp.zeros((72, 128), F32)
    for index in range(5):
        tall = [
            tall_block(
                fields[index, :, half * 128 : half * 128 + 128], near, far,
                index * 8 + half * 4,
            )
            for half in range(2)
        ]
        tall_out[index, :, 0:128] = tall[0]
        tall_out[index, :, 128:256] = tall[1]
        edges = jnp.where(
            lane < HALO_COLS, tall[0], jnp.where(lane >= 128 - HALO_COLS, tall[1], 0.0)
        )
        if index:
            edges = pltpu.roll(edges, index * 2 * HALO_COLS, 1)
        message = message + edges
    out[0:72, :] = message
    out[72:136, :] = packed(link_cell[...]).astype(F32)


def owner_start_kernel(
    pipes, link_node, link_coef, kinds, laws, table, nodes, node_high, node_low, coef, classes,
    matrices,
):
    classes[...] = kinds[...]
    matrices[...] = laws[...]
    table[...] = pipe_table(pipes[...])
    high, low = node_place(packed(link_node[...]))
    node_high[...] = high
    node_low[...] = low
    coef[...] = packed(link_coef[...])
    nodes[...] = gathered(table, 64, high, low)


def swept(state, gains):
    def once(_, w):
        return (
            gains[0] * w
            + gains[1] * pltpu.roll(w, 1, 0)
            + gains[2] * pltpu.roll(w, 71, 0)
            + gains[3] * pltpu.roll(w, 1, 1)
            + gains[4] * pltpu.roll(w, 383, 1)
            + gains[5]
        )

    for i in range(SWEEPS):
        state = once(i, state)
    return state


def put(out, blocks, index, value):
    out[pl.ds(index, 128, stride=blocks), :] = value


def taken(got, blocks, index):
    return got[pl.ds(index, 128, stride=blocks), :]


def build_message(out, blocks, heads, nodes):
    put(out, blocks, 0, paired(heads, nodes))
    if blocks == 6:
        put(out, blocks, 5, beside(nodes))


def zone_heads(edge, zone_place, edge_ref, zone_ref):
    lane = iota((64, 128), 1)
    edge_ref[...] = jnp.where(lane < ZONE, edge, pltpu.roll(edge, 2 * ZONE, 1))
    lane8 = iota((8, 128), 1)
    table = jnp.zeros((8, 128), F32)
    for s in range(8):
        line = edge_ref[pl.ds(s, 8, stride=8), :]
        if s:
            line = pltpu.roll(line, s * 16, 1)
        table = jnp.where((lane8 >> 4) == s, line, table)
    zone_ref[...] = table
    zone_row, zone_col = zone_place
    high = jnp.where(zone_row >= 0, zone_row >> 3, -1)
    low = jnp.bitwise_and(zone_row, 7) * 16 + zone_col
    return gathered(zone_ref, 8, high, low)


def sweep_and_gather(
    state, gains, cell_high, cell_low, zone_place, surface_out, heads_out, zone_out, cell_table,
    edge_ref, zone_ref,
):
    state = swept(state, gains)
    surface_out[...] = state[:64]
    cell_table[0:64, :] = state[:64, 0:128]
    cell_table[64:128, :] = state[:64, 128:256]
    heads = jnp.concatenate(
        [
            gathered_by_product(cell_table[...], cell_high, cell_low, 4),
            gathered(cell_table, 128, cell_high[32:64, :], cell_low[32:64, :]),
        ],
        axis=0,
    )
    heads_out[...] = heads
    if zone_place is not None:
        zone_out[...] = zone_heads(state[:64, 256:384], zone_place, edge_ref, zone_ref)
    return heads


def first_sweep_kernel(
    tall, near_col, far_col, near, link_cell, table, nodes, coef,
    gains_out, inverse_out, cell_high, cell_low, zone_row_out, zone_col_out, surface_out, heads_out,
    zone_out, out, cell_table, edge_ref, zone_ref,
):
    lane = iota((72, 128), 1)
    wide = []
    from_west = jnp.where(even(1), far_col[...], near_col[...])
    from_east = jnp.where(even(1), near_col[...], far_col[...])
    for index in range(5):
        west = jnp.where(row_col()[1] > 0, from_west[0:72, :], 0.0)
        east = jnp.where(row_col()[1] < 15, from_east[0:72, :], 0.0)
        if index:
            west = pltpu.roll(west, 128 - index * 2 * HALO_COLS, 1)
            east = pltpu.roll(east, 128 - index * 2 * HALO_COLS, 1)
        edge = jnp.where(
            lane < HALO_COLS, east, jnp.where(lane >= 128 - HALO_COLS, west, 0.0)
        )
        wide.append(jnp.concatenate([tall[index], edge], axis=1))
    state, cond_x, cond_y, inverse, rainfall = wide
    north = pltpu.roll(cond_x, 1, 0)
    west = pltpu.roll(cond_y, 1, 1)
    gains = [
        1.0 - (north + cond_x + west + cond_y) * inverse,
        north * inverse, cond_x * inverse, west * inverse, cond_y * inverse, rainfall,
    ]
    for index, gain in enumerate(gains):
        gains_out[index] = gain
    inverse_out[...] = inverse[:64]
    cells = paired(from_west[72:136, :], from_east[72:136, :]).astype(jnp.int32)
    col = jnp.bitwise_and(cells, 255)
    is_west = iota((128, 128), 1) < 64
    zone_col = jnp.where(is_west, col - (256 - 2 * ZONE), col)
    inside = (zone_col >= 0) & (zone_col < 2 * ZONE)
    inside = inside & (jnp.where(is_west, zone_col, zone_col + ZONE) >= ZONE)
    zone_row = jnp.where((cells >= 0) & inside & (jnp.where(is_west, 0, zone_col) < ZONE), cells >> 8, -1)
    zone_row_out[...] = zone_row
    zone_col_out[...] = zone_col
    high, low = cell_place(packed(link_cell[...]))
    cell_high[...] = high
    cell_low[...] = low
    heads = sweep_and_gather(
        state, gains, cell_high, cell_low, (zone_row, zone_col), surface_out, heads_out, zone_out,
        cell_table, edge_ref, zone_ref,
    )
    build_message(out, 6, heads, nodes[...])
    own_rows = (iota((128, 128), 0) >> 4) == row_col()[0]
    for half in range(2):
        own = jnp.broadcast_to(table[half * 32 : half * 32 + 1, :], (128, 128))
        other = jnp.broadcast_to(near[40 + half : 41 + half, :], (128, 128))
        put(out, 6, 1 + half, jnp.where(own_rows, own, other))
    put(out, 6, 3, paired(coef[...], coef[...]))
    put(out, 6, 4, beside(coef[...]))


def sweep_kernel(
    last, surface, near, far, gains_ref, cell_high, cell_low, zone_row, zone_col,
    table, nodes, surface_out, heads_out, zone_out, out, cell_table, edge_ref, zone_ref,
):
    state = jnp.concatenate(
        [
            tall_block(
                surface[:, block * 128 : block * 128 + 128], near, far, block * 4
            )
            for block in range(3)
        ],
        axis=1,
    )
    gains = [gains_ref[index] for index in range(6)]
    zone_place = None if last else (zone_row[...], zone_col[...])
    heads = sweep_and_gather(
        state, gains, cell_high, cell_low, zone_place, surface_out, heads_out, zone_out,
        cell_table, edge_ref, zone_ref,
    )
    blocks = 5 if last else 6
    build_message(out, blocks, heads, nodes[...])
    for index, row in enumerate(ENDS):
        put(out, blocks, 1 + index, jnp.broadcast_to(table[row : row + 1, :], (128, 128)))


def tile_kernel(
    first, last, got, surface, inverse, heads, zone, cell_high, hot, zone_row, zone_col, *rest
):
    rest = list(rest)
    if first:
        own_coef = low_halves(taken(got, 6, 3))
        zone_coef = taken(got, 6, 4)
    else:
        own_coef = rest.pop(0)[...]
        zone_coef = rest.pop(0)[...]
    surface_out = rest.pop(0)
    if not last:
        near, far = rest.pop(0), rest.pop(0)
    if first:
        rest.pop(0)[...] = own_coef
        rest.pop(0)[...] = zone_coef
    value_ref, zone_value_ref, row_ref = rest
    value_ref[...] = jnp.where(
        cell_high[...] >= 0, own_coef * (heads[...] - high_halves(taken(got, 5 if last else 6, 0))), 0.0
    )
    row_ref[...] = jnp.where(cell_high[...] >= 0, jnp.bitwise_and(cell_high[...], 63), -1)
    lost = summed_by_columns(row_ref, value_ref, hot)
    left = surface[:, 0:128] - inverse[:, 0:128] * lost[:, 0:128]
    right = surface[:, 128:256] - inverse[:, 128:256] * lost[:, 128:256]
    surface_out[:, 0:128] = left
    surface_out[:, 128:256] = right
    if last:
        return
    zone_value_ref[...] = jnp.where(
        zone_row[...] >= 0, zone_coef * (zone[...] - taken(got, 6, 5)), 0.0
    )
    lost = summed(zone_row, zone_col, zone_value_ref, 64, 2 * ZONE, by_low=True)
    lost = jnp.concatenate([lost, jnp.zeros((64, 128 - 2 * ZONE), F32)], axis=1)
    lane = iota((64, 128), 1)
    lost = jnp.where(
        lane < ZONE, lost,
        jnp.where(lane >= 128 - ZONE, pltpu.roll(lost, 128 - 2 * ZONE, 1), 0.0),
    )
    edge = surface[:, 256:384] - inverse[:, 256:384] * lost
    surface_out[:, 256:384] = edge
    top, bottom = strips([left, right, edge], 0), strips([left, right, edge], 60)
    near[...] = jnp.where(even(0), bottom, top)
    far[...] = jnp.where(even(0), top, bottom)


def owner_kernel(
    first, last, got, nodes, node_high, node_low, coef, table, meets, classes, matrices, *rest
):
    blocks = 5 if last else 6
    if last:
        pipes_out, value_ref, ends_ref = rest
    else:
        table_out, nodes_out, value_ref, ends_ref = rest
    value_ref[...] = jnp.where(
        node_high[...] >= 0, coef[...] * (low_halves(taken(got, blocks, 0)) - nodes[...]), 0.0
    )
    inflow = summed(node_high, node_low, value_ref, 64, 128)
    balance = table[...] + inflow
    start = pl.multiple_of(row_col()[0] * (16 * blocks), 16)
    other = pl.multiple_of((row_col()[0] ^ 1) * 96, 32) if first else start
    for index in range(4):
        source, block = (other, index - 1) if first and index >= 2 else (start, 1 + index)
        ends_ref[index * 16 : index * 16 + 16, :] = got[pl.ds(source + block, 16, stride=blocks), :]
    meet = meets[...]
    meet_high = jnp.bitwise_and(meet >> 7, 1) * 16 + (meet >> 8)
    meet_high = jnp.where(iota((8, 128), 0) < 2, meet_high + 32, meet_high)
    met = gathered(ends_ref, 64, meet_high, meet) * boundary_gain
    node_row = iota((32, 128), 0)
    parts = []
    for half in range(2):
        part = balance[half * 32 : half * 32 + 32]
        part = part + jnp.where(
            node_row == 0, met[half : half + 1],
            jnp.where(node_row == 31, met[2 + half : 3 + half], 0.0),
        )
        products = jnp.dot(
            matrices[...], part, precision=lax.Precision.HIGHEST, preferred_element_type=F32
        )
        kind = classes[half : half + 1, :]
        updated = jnp.zeros((32, 128), F32)
        for index in range(CLASSES):
            updated = jnp.where(kind == index, products[index * 32 : index * 32 + 32], updated)
        parts.append(updated)
    if last:
        pipes_out[:, 0:128] = parts[0]
        pipes_out[:, 128:256] = parts[1]
        return
    table_out[0:32, :] = parts[0]
    table_out[32:64, :] = parts[1]
    nodes_out[...] = gathered(table_out, 64, node_high[...], node_low[...])


def final_kernel(
    got, surface, inverse, heads, zone, cell_high, hot, zone_row, zone_col, own_coef, zone_coef,
    nodes, node_high, node_low, coef, table, meets, classes, matrices, surface_out,
    pipes_out, cell_value_ref, zone_value_ref, row_ref, node_value_ref, ends_ref,
):
    owner_kernel(
        False, True, got, nodes, node_high, node_low, coef, table, meets, classes,
        matrices, pipes_out, node_value_ref, ends_ref,
    )
    tile_kernel(
        False, True, got, surface, inverse, heads, zone, cell_high, hot, zone_row, zone_col,
        own_coef, zone_coef, surface_out, cell_value_ref, zone_value_ref, row_ref,
    )


def shape(*dims, dtype=F32):
    return jax.ShapeDtypeStruct(dims, dtype)


def call(kernel, inputs, outputs, scratch=(), space=pltpu.VMEM):
    vmem = pl.BlockSpec(memory_space=pltpu.VMEM)
    return pl.pallas_call(
        kernel,
        out_shape=outputs,
        in_specs=[pl.BlockSpec(memory_space=space)] * len(inputs),
        out_specs=[vmem] * len(outputs),
        scratch_shapes=list(scratch),
        compiler_params=pltpu.CompilerParams(vmem_limit_bytes=16 << 20),
        cost_estimate=pl.CostEstimate(flops=10**9, bytes_accessed=1 << 20, transcendentals=0),
    )(*inputs)


def swapped(near, far, dim):
    sizes = lax.axis_size("row"), lax.axis_size("col")
    routes = [], []
    for row in range(sizes[0]):
        for col in range(sizes[1]):
            here = [row, col]
            partner = list(here)
            partner[dim] ^= 1
            other = list(here)
            other[dim] += 1 if here[dim] % 2 else -1
            if not 0 <= other[dim] < sizes[dim]:
                other = list(here)
                other[1 - dim] ^= 1
            for route, there in zip(routes, (partner, other)):
                route.append((row * sizes[1] + col, there[0] * sizes[1] + there[1]))
    return (
        lax.ppermute(near, ("row", "col"), routes[0]),
        lax.ppermute(far, ("row", "col"), routes[1]),
    )


def body(
    surface_head, conduct_x, conduct_y, porosity, rainfall, pipe_head, pipe_class, pipe_up,
    pipe_down, pipe_matrices, link_cell, link_node, link_coef,
):
    link_cell = link_cell[0]
    meets = jnp.concatenate(
        [pipe_up.reshape(2, 128), pipe_down.reshape(2, 128), jnp.zeros((4, 128), jnp.int32)], axis=0
    )
    classes = pipe_class.reshape(2, 128)
    matrices = pipe_matrices.reshape(CLASSES * 32, 32)
    ints = functools.partial(shape, dtype=jnp.int32)

    fields, near, far = call(
        start_kernel,
        [pltpu.with_memory_space_constraint(x, pltpu.HBM) for x in (
            surface_head, conduct_x, conduct_y, porosity, rainfall, pipe_head
        )],
        [shape(5, 64, 256), shape(48, 128), shape(40, 128)],
        [pltpu.VMEM((8, 256), F32), pltpu.SemaphoreType.DMA((6,))], space=pltpu.HBM,
    )
    near, far = swapped(near, far, 0)
    tall, sent = call(
        pack_cols_kernel, (near, far, fields, link_cell),
        [shape(5, 72, 256), shape(136, 128)],
    )
    sent, link_node, link_coef, cells = lax.optimization_barrier(
        (sent, link_node, link_coef, link_cell)
    )
    link_node = link_node[:, 0, :]
    link_coef = link_coef[:, 0, :]
    near_col, far_col = swapped(sent, sent, 1)
    table, nodes, node_high, node_low, coef, classes, matrices = call(
        owner_start_kernel, (pipe_head, link_node, link_coef, classes, matrices),
        [shape(64, 128), shape(64, 128), ints(64, 128), ints(64, 128), shape(64, 128),
         ints(2, 128), shape(128, 32)],
    )
    (hot,) = call(columns_kernel, (cells,), [shape(8192, 256, dtype=BF16)])
    gather_scratch = [
        pltpu.VMEM((128, 128), F32), pltpu.VMEM((64, 128), F32), pltpu.VMEM((8, 128), F32)
    ]
    swept_shapes = [shape(64, 384), shape(64, 128), shape(128, 128)]
    (gains, inverse, cell_high, cell_low, zone_row, zone_col, surface, heads, zone, sent) = call(
        first_sweep_kernel,
        (tall, near_col, far_col, near, link_cell, table, nodes, coef),
        [shape(6, 72, 384), shape(64, 384), ints(64, 128), ints(64, 128), ints(128, 128),
         ints(128, 128), *swept_shapes, shape(768, 128)],
        gather_scratch,
    )
    sent, meets, hot = lax.optimization_barrier((sent, meets, hot))
    coefs = ()
    for step in range(STEPS):
        first, last = step == 0, step == STEPS - 1
        if step:
            surface, heads, zone, sent = call(
                functools.partial(sweep_kernel, last),
                (surface, near, far, gains, cell_high, cell_low, zone_row, zone_col,
                 table, nodes),
                [*swept_shapes, shape(640 if last else 768, 128)], gather_scratch,
            )
        got = lax.all_to_all(
            sent.reshape(128, 1, -1), ("row", "col"), split_axis=0, concat_axis=0, tiled=True
        ).reshape(-1, 128)
        tile_inputs = (surface, inverse, heads, zone, cell_high, hot, zone_row, zone_col, *coefs)
        owner_inputs = (nodes, node_high, node_low, coef, table, meets, classes, matrices)
        tile_scratch = [
            pltpu.VMEM((64, 128), F32), pltpu.VMEM((128, 128), F32), pltpu.VMEM((64, 128), jnp.int32)
        ]
        owner_scratch = [pltpu.VMEM((64, 128), F32), pltpu.VMEM((64, 128), F32)]
        if last:
            return tuple(call(
                final_kernel, (got, *tile_inputs, *owner_inputs),
                [shape(64, 256), shape(32, 256)], tile_scratch + owner_scratch,
            ))
        outputs = [shape(64, 384), shape(12, 128), shape(12, 128)]
        if first:
            outputs += [shape(64, 128), shape(128, 128)]
        surface, near, far, *new_coefs = call(
            functools.partial(tile_kernel, first, False), (got, *tile_inputs), outputs,
            tile_scratch,
        )
        near, far = swapped(near, far, 0)
        table, nodes = call(
            functools.partial(owner_kernel, first, False), (got, *owner_inputs),
            [shape(64, 128), shape(64, 128)], owner_scratch,
        )
        if first:
            coefs = tuple(new_coefs)


def solution(mesh):
    placed = (
        P("row", "col"),
        P("row", "col"),
        P("row", "col"),
        P("row", "col"),
        P("row", "col"),
        P(None, ("row", "col")),
        P(("row", "col")),
        P(("row", "col")),
        P(("row", "col")),
        P(),
        P(("row", "col"), None, None),
        P(None, ("row", "col"), None),
        P(None, ("row", "col"), None),
    )
    return jax.shard_map(
        body,
        mesh=mesh,
        in_specs=placed,
        out_specs=(P("row", "col"), P(None, ("row", "col"))),
        check_vma=False,
    )
```

```python
import functools

import jax
import jax.numpy as jnp
from jax import lax
from jax.experimental import pallas as pl
from jax.experimental.pallas import tpu as pltpu
from jax.sharding import PartitionSpec as P

CLASSES = 4
SWEEPS = 4
STEPS = 3
F32 = jnp.float32
BF16 = jnp.bfloat16

boundary_gain = 0.5

HALO_ROWS = 4
HALO_COLS = 12
ZONE = 8
ENDS = (0, 32, 31, 63)


def iota(shape, dim):
    return lax.broadcasted_iota(jnp.int32, shape, dim)


def packed(x):
    return jnp.concatenate([x[:64], x[64:]], axis=1)


def low_halves(block):
    lane = iota((64, 128), 1)
    return jnp.where(lane < 64, block[:64], pltpu.roll(block[64:], 64, 1))


def high_halves(block):
    lane = iota((64, 128), 1)
    return jnp.where(lane < 64, pltpu.roll(block[:64], 64, 1), block[64:])


def paired(low, high):
    lane = iota((64, 128), 1)
    top = jnp.where(lane < 64, low, pltpu.roll(high, 64, 1))
    bottom = jnp.where(lane < 64, pltpu.roll(low, 64, 1), high)
    return jnp.concatenate([top, bottom], axis=0)


def beside(values):
    lane = iota((128, 128), 1)
    both = paired(values, values)
    return jnp.where(lane < 64, pltpu.roll(both, 1, 0), pltpu.roll(both, 127, 0))


def gathered(table_ref, rows, high, low):
    low = jnp.bitwise_and(low, 127)
    tiles = []
    for start in range(0, high.shape[0], 8):
        tile_high, tile_low = high[start : start + 8], low[start : start + 8]
        found = jnp.zeros((8, 128), F32)
        for row in range(rows):
            line = jnp.broadcast_to(table_ref[row : row + 1, :], (8, 128))
            values = jnp.take_along_axis(line, tile_low, axis=1)
            found = jnp.where(tile_high == row, values, found)
        tiles.append(found)
    return jnp.concatenate(tiles, axis=0) if len(tiles) > 1 else tiles[0]


def gathered_by_product(table, high_ref, low_ref, tiles):
    coarse = table.astype(BF16)
    fine = (table - coarse.astype(F32)).astype(BF16)
    parts = jnp.concatenate([coarse, fine], axis=1)
    row_iota = iota((128, 128), 0)
    high_iota = row_iota.astype(F32).astype(BF16)
    one, zero = jnp.ones((128, 128), BF16), jnp.zeros((128, 128), BF16)
    found = []
    for start in range(0, 8 * tiles, 8):
        high = high_ref[start : start + 8, :].astype(F32)
        low = low_ref[start : start + 8, :]
        hot = jnp.concatenate(
            [
                jnp.where(repeated(high[j : j + 1], 128) == high_iota, one, zero)
                for j in range(8)
            ],
            axis=1,
        )
        lines = lax.dot_general(
            parts, hot, (((0,), (0,)), ((), ())), preferred_element_type=F32
        )
        lines = lines[:128] + lines[128:]
        for j in range(8):
            line = jnp.where(
                row_iota == low[j : j + 1], lines[:, j * 128 : j * 128 + 128], 0.0
            )
            found.append(jnp.sum(line, axis=0, keepdims=True))
    return jnp.concatenate(found, axis=0)


def repeated(line, size):
    block = jnp.broadcast_to(line, (16, 128)).astype(BF16)
    return jnp.concatenate([block] * (size // 16), axis=0) if size > 16 else block


def summed(high_ref, low_ref, value_ref, high_size, low_size, by_low=False):
    refs, sizes = (high_ref, low_ref), (high_size, low_size)
    bearer = 1 if by_low else 0
    iotas = [iota((size, 128), 0).astype(F32).astype(BF16) for size in sizes]
    zeros = [jnp.zeros((size, 128), BF16) for size in sizes]
    one = jnp.ones((sizes[1 - bearer], 128), BF16)
    total = None
    for start in range(0, high_ref.shape[0], 8):
        places = [ref[start : start + 8, :].astype(F32) for ref in refs]
        value = value_ref[start : start + 8, :]
        coarse = value.astype(BF16).astype(F32)
        fine = value - coarse
        size, zero = sizes[bearer], zeros[bearer]
        coarse_hot, fine_hot, plain_hot = [], [], []
        for j in range(8):
            same = [
                repeated(places[side][j : j + 1], sizes[side]) == iotas[side] for side in range(2)
            ]
            coarse_hot.append(jnp.where(same[bearer], repeated(coarse[j : j + 1], size), zero))
            fine_hot.append(jnp.where(same[bearer], repeated(fine[j : j + 1], size), zero))
            plain_hot.append(jnp.where(same[1 - bearer], one, zeros[1 - bearer]))
        value_hot = jnp.concatenate(
            [jnp.concatenate(coarse_hot, axis=1), jnp.concatenate(fine_hot, axis=1)], axis=0
        )
        plain_hot = jnp.concatenate(plain_hot, axis=1)
        sides = (plain_hot, value_hot) if by_low else (value_hot, plain_hot)
        product = lax.dot_general(
            *sides, (((1,), (1,)), ((), ())), preferred_element_type=F32
        )
        total = product if total is None else total + product
    if by_low:
        return total[:, :low_size] + total[:, low_size:]
    return total[:high_size] + total[high_size:]


def summed_by_columns(row_ref, value_ref, hot_ref):
    row_iota = iota((64, 128), 0).astype(F32).astype(BF16)
    zero = jnp.zeros((64, 128), BF16)
    total = jnp.zeros((128, 256), F32)
    for start in range(0, 64, 8):
        rows = row_ref[start : start + 8, :].astype(F32)
        value = value_ref[start : start + 8, :]
        coarse = value.astype(BF16).astype(F32)
        fine = value - coarse
        coarse_hot, fine_hot = [], []
        for j in range(8):
            same = repeated(rows[j : j + 1], 64) == row_iota
            coarse_hot.append(jnp.where(same, repeated(coarse[j : j + 1], 64), zero))
            fine_hot.append(jnp.where(same, repeated(fine[j : j + 1], 64), zero))
        value_hot = jnp.concatenate(
            [jnp.concatenate(coarse_hot, axis=1), jnp.concatenate(fine_hot, axis=1)], axis=0
        )
        total = total + jnp.dot(
            value_hot, hot_ref[start * 128 : start * 128 + 1024, :], preferred_element_type=F32
        )
    return total[:64] + total[64:]


def columns_kernel(link_cell, hot):
    cols = jnp.bitwise_and(packed(link_cell[...]), 255).astype(F32).T
    lane = iota((128, 256), 1).astype(F32)
    for j in range(64):
        same = jnp.broadcast_to(cols[:, j : j + 1], (128, 256)) == lane
        hot[j * 128 : j * 128 + 128, :] = jnp.where(same, 1.0, 0.0).astype(BF16)


def cell_place(cell):
    high = jnp.where(
        cell >= 0, jnp.bitwise_and(cell >> 7, 1) * 64 + (cell >> 8), -1
    )
    return high, jnp.bitwise_and(cell, 127)


def node_place(node):
    high = jnp.where(
        node >= 0, jnp.bitwise_and(node >> 7, 1) * 32 + (node >> 8), -1
    )
    return high, jnp.bitwise_and(node, 127)


def pipe_table(state):
    return jnp.concatenate([state[:, :128], state[:, 128:]], axis=0)


def strips(blocks, start):
    return jnp.concatenate([block[start : start + HALO_ROWS] for block in blocks], axis=0)


def row_col():
    return lax.axis_index("row"), lax.axis_index("col")


def even(dim):
    return jnp.bitwise_and(row_col()[dim], 1) == 0


def start_kernel(
    surface, cond_x, cond_y, porosity, rainfall, pipes, fields, near, far, tips, arrived
):
    copies = [
        pltpu.make_async_copy(source, fields.at[index], arrived.at[index])
        for index, source in enumerate((surface, cond_x, cond_y, porosity, rainfall))
    ]
    copies.append(pltpu.make_async_copy(pipes.at[24:32, :], tips, arrived.at[5]))
    for copy in copies:
        copy.start()
    for copy in copies:
        copy.wait()
    fields[3] = 1.0 / fields[3]
    for index in range(5):
        halves = [fields[index, :, 0:128], fields[index, :, 128:256]]
        top, bottom = strips(halves, 0), strips(halves, 60)
        near[pl.ds(index * 8, 8), :] = jnp.where(even(0), bottom, top)
        far[pl.ds(index * 8, 8), :] = jnp.where(even(0), top, bottom)
    near[40:48, :] = jnp.concatenate(
        [tips[7:8, 0:128], tips[7:8, 128:256], jnp.zeros((6, 128), F32)], axis=0
    )


def tall_block(block, near, far, start):
    near, far = near[start : start + 4, :], far[start : start + 4, :]
    over = jnp.where(even(0), far, near)
    under = jnp.where(even(0), near, far)
    over = jnp.where(row_col()[0] > 0, over, 0.0)
    under = jnp.where(row_col()[0] < 7, under, 0.0)
    return jnp.concatenate([block, under, over], axis=0)


def pack_cols_kernel(near, far, fields, link_cell, tall_out, out):
    lane = iota((72, 128), 1)
    message = jnp.zeros((72, 128), F32)
    for index in range(5):
        tall = [
            tall_block(
                fields[index, :, half * 128 : half * 128 + 128], near, far,
                index * 8 + half * 4,
            )
            for half in range(2)
        ]
        tall_out[index, :, 0:128] = tall[0]
        tall_out[index, :, 128:256] = tall[1]
        edges = jnp.where(
            lane < HALO_COLS, tall[0], jnp.where(lane >= 128 - HALO_COLS, tall[1], 0.0)
        )
        if index:
            edges = pltpu.roll(edges, index * 2 * HALO_COLS, 1)
        message = message + edges
    out[0:72, :] = message
    out[72:136, :] = packed(link_cell[...]).astype(F32)


def owner_start_kernel(
    pipes, link_node, link_coef, kinds, laws, uppers, lowers, table, nodes, node_high, node_low,
    coef, classes, matrices, meets,
):
    meets[...] = jnp.concatenate(
        [uppers[...], lowers[...], jnp.zeros((4, 128), jnp.int32)], axis=0
    )
    classes[...] = kinds[...]
    matrices[...] = laws[...]
    table[...] = pipe_table(pipes[...])
    high, low = node_place(packed(link_node[...]))
    node_high[...] = high
    node_low[...] = low
    coef[...] = packed(link_coef[...])
    nodes[...] = gathered(table, 64, high, low)


def swept(state, gains):
    def once(_, w):
        return (
            gains[0] * w
            + gains[1] * pltpu.roll(w, 1, 0)
            + gains[2] * pltpu.roll(w, 71, 0)
            + gains[3] * pltpu.roll(w, 1, 1)
            + gains[4] * pltpu.roll(w, 383, 1)
            + gains[5]
        )

    for i in range(SWEEPS):
        state = once(i, state)
    return state


def put(out, blocks, index, value):
    out[pl.ds(index, 128, stride=blocks), :] = value


def taken(got, blocks, index):
    return got[pl.ds(index, 128, stride=blocks), :]


def build_message(out, blocks, heads, nodes):
    put(out, blocks, 0, paired(heads, nodes))
    if blocks == 6:
        put(out, blocks, 5, beside(nodes))


def zone_heads(edge, zone_place, edge_ref, zone_ref):
    lane = iota((64, 128), 1)
    edge_ref[...] = jnp.where(lane < ZONE, edge, pltpu.roll(edge, 2 * ZONE, 1))
    lane8 = iota((8, 128), 1)
    table = jnp.zeros((8, 128), F32)
    for s in range(8):
        line = edge_ref[pl.ds(s, 8, stride=8), :]
        if s:
            line = pltpu.roll(line, s * 16, 1)
        table = jnp.where((lane8 >> 4) == s, line, table)
    zone_ref[...] = table
    zone_row, zone_col = zone_place
    high = jnp.where(zone_row >= 0, zone_row >> 3, -1)
    low = jnp.bitwise_and(zone_row, 7) * 16 + zone_col
    return gathered(zone_ref, 8, high, low)


def sweep_and_gather(
    state, gains, cell_high, cell_low, zone_place, surface_out, heads_out, zone_out, cell_table,
    edge_ref, zone_ref,
):
    state = swept(state, gains)
    surface_out[...] = state[:64]
    cell_table[0:64, :] = state[:64, 0:128]
    cell_table[64:128, :] = state[:64, 128:256]
    heads = jnp.concatenate(
        [
            gathered_by_product(cell_table[...], cell_high, cell_low, 4),
            gathered(cell_table, 128, cell_high[32:64, :], cell_low[32:64, :]),
        ],
        axis=0,
    )
    heads_out[...] = heads
    if zone_place is not None:
        zone_out[...] = zone_heads(state[:64, 256:384], zone_place, edge_ref, zone_ref)
    return heads


def first_sweep_kernel(
    tall, near_col, far_col, near, link_cell, table, nodes, coef,
    gains_out, inverse_out, cell_high, cell_low, zone_row_out, zone_col_out, surface_out, heads_out,
    zone_out, out, cell_table, edge_ref, zone_ref,
):
    lane = iota((72, 128), 1)
    wide = []
    from_west = jnp.where(even(1), far_col[...], near_col[...])
    from_east = jnp.where(even(1), near_col[...], far_col[...])
    for index in range(5):
        west = jnp.where(row_col()[1] > 0, from_west[0:72, :], 0.0)
        east = jnp.where(row_col()[1] < 15, from_east[0:72, :], 0.0)
        if index:
            west = pltpu.roll(west, 128 - index * 2 * HALO_COLS, 1)
            east = pltpu.roll(east, 128 - index * 2 * HALO_COLS, 1)
        edge = jnp.where(
            lane < HALO_COLS, east, jnp.where(lane >= 128 - HALO_COLS, west, 0.0)
        )
        wide.append(jnp.concatenate([tall[index], edge], axis=1))
    state, cond_x, cond_y, inverse, rainfall = wide
    north = pltpu.roll(cond_x, 1, 0)
    west = pltpu.roll(cond_y, 1, 1)
    gains = [
        1.0 - (north + cond_x + west + cond_y) * inverse,
        north * inverse, cond_x * inverse, west * inverse, cond_y * inverse, rainfall,
    ]
    for index, gain in enumerate(gains):
        gains_out[index] = gain
    inverse_out[...] = inverse[:64]
    cells = paired(from_west[72:136, :], from_east[72:136, :]).astype(jnp.int32)
    col = jnp.bitwise_and(cells, 255)
    is_west = iota((128, 128), 1) < 64
    zone_col = jnp.where(is_west, col - (256 - 2 * ZONE), col)
    inside = (zone_col >= 0) & (zone_col < 2 * ZONE)
    inside = inside & (jnp.where(is_west, zone_col, zone_col + ZONE) >= ZONE)
    zone_row = jnp.where((cells >= 0) & inside & (jnp.where(is_west, 0, zone_col) < ZONE), cells >> 8, -1)
    zone_row_out[...] = zone_row
    zone_col_out[...] = zone_col
    high, low = cell_place(packed(link_cell[...]))
    cell_high[...] = high
    cell_low[...] = low
    heads = sweep_and_gather(
        state, gains, cell_high, cell_low, (zone_row, zone_col), surface_out, heads_out, zone_out,
        cell_table, edge_ref, zone_ref,
    )
    build_message(out, 6, heads, nodes[...])
    own_rows = (iota((128, 128), 0) >> 4) == row_col()[0]
    for half in range(2):
        own = jnp.broadcast_to(table[half * 32 : half * 32 + 1, :], (128, 128))
        other = jnp.broadcast_to(near[40 + half : 41 + half, :], (128, 128))
        put(out, 6, 1 + half, jnp.where(own_rows, own, other))
    put(out, 6, 3, paired(coef[...], coef[...]))
    put(out, 6, 4, beside(coef[...]))


def sweep_kernel(
    last, surface, near, far, gains_ref, cell_high, cell_low, zone_row, zone_col,
    table, nodes, surface_out, heads_out, zone_out, out, cell_table, edge_ref, zone_ref,
):
    state = jnp.concatenate(
        [
            tall_block(
                surface[:, block * 128 : block * 128 + 128], near, far, block * 4
            )
            for block in range(3)
        ],
        axis=1,
    )
    gains = [gains_ref[index] for index in range(6)]
    zone_place = None if last else (zone_row[...], zone_col[...])
    heads = sweep_and_gather(
        state, gains, cell_high, cell_low, zone_place, surface_out, heads_out, zone_out,
        cell_table, edge_ref, zone_ref,
    )
    blocks = 5 if last else 6
    build_message(out, blocks, heads, nodes[...])
    for index, row in enumerate(ENDS):
        put(out, blocks, 1 + index, jnp.broadcast_to(table[row : row + 1, :], (128, 128)))


def tile_kernel(
    first, last, got, surface, inverse, heads, zone, cell_high, hot, zone_row, zone_col, *rest
):
    rest = list(rest)
    if first:
        own_coef = low_halves(taken(got, 6, 3))
        zone_coef = taken(got, 6, 4)
    else:
        own_coef = rest.pop(0)[...]
        zone_coef = rest.pop(0)[...]
    surface_out = rest.pop(0)
    if not last:
        near, far = rest.pop(0), rest.pop(0)
    if first:
        rest.pop(0)[...] = own_coef
        rest.pop(0)[...] = zone_coef
    value_ref, zone_value_ref, row_ref = rest
    value_ref[...] = jnp.where(
        cell_high[...] >= 0, own_coef * (heads[...] - high_halves(taken(got, 5 if last else 6, 0))), 0.0
    )
    row_ref[...] = jnp.where(cell_high[...] >= 0, jnp.bitwise_and(cell_high[...], 63), -1)
    lost = summed_by_columns(row_ref, value_ref, hot)
    left = surface[:, 0:128] - inverse[:, 0:128] * lost[:, 0:128]
    right = surface[:, 128:256] - inverse[:, 128:256] * lost[:, 128:256]
    surface_out[:, 0:128] = left
    surface_out[:, 128:256] = right
    if last:
        return
    zone_value_ref[...] = jnp.where(
        zone_row[...] >= 0, zone_coef * (zone[...] - taken(got, 6, 5)), 0.0
    )
    lost = summed(zone_row, zone_col, zone_value_ref, 64, 2 * ZONE, by_low=True)
    lost = jnp.concatenate([lost, jnp.zeros((64, 128 - 2 * ZONE), F32)], axis=1)
    lane = iota((64, 128), 1)
    lost = jnp.where(
        lane < ZONE, lost,
        jnp.where(lane >= 128 - ZONE, pltpu.roll(lost, 128 - 2 * ZONE, 1), 0.0),
    )
    edge = surface[:, 256:384] - inverse[:, 256:384] * lost
    surface_out[:, 256:384] = edge
    top, bottom = strips([left, right, edge], 0), strips([left, right, edge], 60)
    near[...] = jnp.where(even(0), bottom, top)
    far[...] = jnp.where(even(0), top, bottom)


def owner_kernel(
    first, last, got, nodes, node_high, node_low, coef, table, meets, classes, matrices, *rest
):
    blocks = 5 if last else 6
    if last:
        pipes_out, value_ref, ends_ref = rest
    else:
        table_out, nodes_out, value_ref, ends_ref = rest
    value_ref[...] = jnp.where(
        node_high[...] >= 0, coef[...] * (low_halves(taken(got, blocks, 0)) - nodes[...]), 0.0
    )
    inflow = summed(node_high, node_low, value_ref, 64, 128)
    balance = table[...] + inflow
    start = pl.multiple_of(row_col()[0] * (16 * blocks), 16)
    other = pl.multiple_of((row_col()[0] ^ 1) * 96, 32) if first else start
    for index in range(4):
        source, block = (other, index - 1) if first and index >= 2 else (start, 1 + index)
        ends_ref[index * 16 : index * 16 + 16, :] = got[pl.ds(source + block, 16, stride=blocks), :]
    meet = meets[...]
    meet_high = jnp.bitwise_and(meet >> 7, 1) * 16 + (meet >> 8)
    meet_high = jnp.where(iota((8, 128), 0) < 2, meet_high + 32, meet_high)
    met = gathered(ends_ref, 64, meet_high, meet) * boundary_gain
    node_row = iota((32, 128), 0)
    parts = []
    for half in range(2):
        part = balance[half * 32 : half * 32 + 32]
        part = part + jnp.where(
            node_row == 0, met[half : half + 1],
            jnp.where(node_row == 31, met[2 + half : 3 + half], 0.0),
        )
        products = jnp.dot(
            matrices[...], part, precision=lax.Precision.HIGHEST, preferred_element_type=F32
        )
        kind = classes[half : half + 1, :]
        updated = jnp.zeros((32, 128), F32)
        for index in range(CLASSES):
            updated = jnp.where(kind == index, products[index * 32 : index * 32 + 32], updated)
        parts.append(updated)
    if last:
        pipes_out[:, 0:128] = parts[0]
        pipes_out[:, 128:256] = parts[1]
        return
    table_out[0:32, :] = parts[0]
    table_out[32:64, :] = parts[1]
    nodes_out[...] = gathered(table_out, 64, node_high[...], node_low[...])


def shape(*dims, dtype=F32):
    return jax.ShapeDtypeStruct(dims, dtype)


def call(kernel, inputs, outputs, scratch=(), space=pltpu.VMEM):
    vmem = pl.BlockSpec(memory_space=pltpu.VMEM)
    return pl.pallas_call(
        kernel,
        out_shape=outputs,
        in_specs=[pl.BlockSpec(memory_space=space)] * len(inputs),
        out_specs=[vmem] * len(outputs),
        scratch_shapes=list(scratch),
        compiler_params=pltpu.CompilerParams(vmem_limit_bytes=16 << 20),
        cost_estimate=pl.CostEstimate(flops=10**9, bytes_accessed=1 << 20, transcendentals=0),
    )(*inputs)


def swapped(near, far, dim):
    sizes = lax.axis_size("row"), lax.axis_size("col")
    routes = [], []
    for row in range(sizes[0]):
        for col in range(sizes[1]):
            here = [row, col]
            partner = list(here)
            partner[dim] ^= 1
            other = list(here)
            other[dim] += 1 if here[dim] % 2 else -1
            if not 0 <= other[dim] < sizes[dim]:
                other = list(here)
                other[1 - dim] ^= 1
            for route, there in zip(routes, (partner, other)):
                route.append((row * sizes[1] + col, there[0] * sizes[1] + there[1]))
    return (
        lax.ppermute(near, ("row", "col"), routes[0]),
        lax.ppermute(far, ("row", "col"), routes[1]),
    )


def body(
    surface_head, conduct_x, conduct_y, porosity, rainfall, pipe_head, pipe_class, pipe_up,
    pipe_down, pipe_matrices, link_cell, link_node, link_coef,
):
    link_cell = link_cell[0]
    uppers, lowers = pipe_up.reshape(2, 128), pipe_down.reshape(2, 128)
    classes = pipe_class.reshape(2, 128)
    matrices = pipe_matrices.reshape(CLASSES * 32, 32)
    ints = functools.partial(shape, dtype=jnp.int32)

    fields, near, far = call(
        start_kernel,
        [pltpu.with_memory_space_constraint(x, pltpu.HBM) for x in (
            surface_head, conduct_x, conduct_y, porosity, rainfall, pipe_head
        )],
        [shape(5, 64, 256), shape(48, 128), shape(40, 128)],
        [pltpu.VMEM((8, 256), F32), pltpu.SemaphoreType.DMA((6,))], space=pltpu.HBM,
    )
    near, far = swapped(near, far, 0)
    tall, sent = call(
        pack_cols_kernel, (near, far, fields, link_cell),
        [shape(5, 72, 256), shape(136, 128)],
    )
    sent, link_node, link_coef, cells = lax.optimization_barrier(
        (sent, link_node, link_coef, link_cell)
    )
    link_node = link_node[:, 0, :]
    link_coef = link_coef[:, 0, :]
    near_col, far_col = swapped(sent, sent, 1)
    table, nodes, node_high, node_low, coef, classes, matrices, meets = call(
        owner_start_kernel, (pipe_head, link_node, link_coef, classes, matrices, uppers, lowers),
        [shape(64, 128), shape(64, 128), ints(64, 128), ints(64, 128), shape(64, 128),
         ints(2, 128), shape(128, 32), ints(8, 128)],
    )
    (hot,) = call(columns_kernel, (cells,), [shape(8192, 256, dtype=BF16)])
    gather_scratch = [
        pltpu.VMEM((128, 128), F32), pltpu.VMEM((64, 128), F32), pltpu.VMEM((8, 128), F32)
    ]
    swept_shapes = [shape(64, 384), shape(64, 128), shape(128, 128)]
    (gains, inverse, cell_high, cell_low, zone_row, zone_col, surface, heads, zone, sent) = call(
        first_sweep_kernel,
        (tall, near_col, far_col, near, link_cell, table, nodes, coef),
        [shape(6, 72, 384), shape(64, 384), ints(64, 128), ints(64, 128), ints(128, 128),
         ints(128, 128), *swept_shapes, shape(768, 128)],
        gather_scratch,
    )
    sent, hot = lax.optimization_barrier((sent, hot))
    coefs = ()
    for step in range(STEPS):
        first, last = step == 0, step == STEPS - 1
        if step:
            surface, heads, zone, sent = call(
                functools.partial(sweep_kernel, last),
                (surface, near, far, gains, cell_high, cell_low, zone_row, zone_col,
                 table, nodes),
                [*swept_shapes, shape(640 if last else 768, 128)], gather_scratch,
            )
        got = lax.all_to_all(
            sent.reshape(128, 1, -1), ("row", "col"), split_axis=0, concat_axis=0, tiled=True
        ).reshape(-1, 128)
        tile_inputs = (surface, inverse, heads, zone, cell_high, hot, zone_row, zone_col, *coefs)
        owner_inputs = (nodes, node_high, node_low, coef, table, meets, classes, matrices)
        tile_scratch = [
            pltpu.VMEM((64, 128), F32), pltpu.VMEM((128, 128), F32), pltpu.VMEM((64, 128), jnp.int32)
        ]
        owner_scratch = [pltpu.VMEM((64, 128), F32), pltpu.VMEM((64, 128), F32)]
        if last:
            (pipes_out,) = call(
                functools.partial(owner_kernel, False, True), (got, *owner_inputs),
                [shape(32, 256)], owner_scratch,
            )
            (surface_out,) = call(
                functools.partial(tile_kernel, False, True), (got, *tile_inputs), [shape(64, 256)],
                tile_scratch,
            )
            return surface_out, pipes_out
        outputs = [shape(64, 384), shape(12, 128), shape(12, 128)]
        if first:
            outputs += [shape(64, 128), shape(128, 128)]
        surface, near, far, *new_coefs = call(
            functools.partial(tile_kernel, first, False), (got, *tile_inputs), outputs,
            tile_scratch,
        )
        near, far = swapped(near, far, 0)
        table, nodes = call(
            functools.partial(owner_kernel, first, False), (got, *owner_inputs),
            [shape(64, 128), shape(64, 128)], owner_scratch,
        )
        if first:
            coefs = tuple(new_coefs)


def solution(mesh):
    placed = (
        P("row", "col"),
        P("row", "col"),
        P("row", "col"),
        P("row", "col"),
        P("row", "col"),
        P(None, ("row", "col")),
        P(("row", "col")),
        P(("row", "col")),
        P(("row", "col")),
        P(),
        P(("row", "col"), None, None),
        P(None, ("row", "col"), None),
        P(None, ("row", "col"), None),
    )
    return jax.shard_map(
        body,
        mesh=mesh,
        in_specs=placed,
        out_specs=(P("row", "col"), P(None, ("row", "col"))),
        check_vma=False,
    )
```

```python
import functools

import jax
import jax.numpy as jnp
from jax import lax
from jax.experimental import pallas as pl
from jax.experimental.pallas import tpu as pltpu
from jax.sharding import PartitionSpec as P

CLASSES = 4
SWEEPS = 4
STEPS = 3
F32 = jnp.float32
BF16 = jnp.bfloat16

boundary_gain = 0.5

HALO_ROWS = 4
HALO_COLS = 12
ZONE = 8
ENDS = (0, 32, 31, 63)


def iota(shape, dim):
    return lax.broadcasted_iota(jnp.int32, shape, dim)


def packed(x):
    return jnp.concatenate([x[:64], x[64:]], axis=1)


def low_halves(block):
    lane = iota((64, 128), 1)
    return jnp.where(lane < 64, block[:64], pltpu.roll(block[64:], 64, 1))


def high_halves(block):
    lane = iota((64, 128), 1)
    return jnp.where(lane < 64, pltpu.roll(block[:64], 64, 1), block[64:])


def paired(low, high):
    lane = iota((64, 128), 1)
    top = jnp.where(lane < 64, low, pltpu.roll(high, 64, 1))
    bottom = jnp.where(lane < 64, pltpu.roll(low, 64, 1), high)
    return jnp.concatenate([top, bottom], axis=0)


def beside(values):
    lane = iota((128, 128), 1)
    both = paired(values, values)
    return jnp.where(lane < 64, pltpu.roll(both, 1, 0), pltpu.roll(both, 127, 0))


def gathered(table_ref, rows, high, low):
    low = jnp.bitwise_and(low, 127)
    tiles = []
    for start in range(0, high.shape[0], 8):
        tile_high, tile_low = high[start : start + 8], low[start : start + 8]
        found = jnp.zeros((8, 128), F32)
        for row in range(rows):
            line = jnp.broadcast_to(table_ref[row : row + 1, :], (8, 128))
            values = jnp.take_along_axis(line, tile_low, axis=1)
            found = jnp.where(tile_high == row, values, found)
        tiles.append(found)
    return jnp.concatenate(tiles, axis=0) if len(tiles) > 1 else tiles[0]


def gathered_by_product(table, high_ref, low_ref, tiles):
    coarse = table.astype(BF16)
    fine = (table - coarse.astype(F32)).astype(BF16)
    parts = jnp.concatenate([coarse, fine], axis=1)
    row_iota = iota((128, 128), 0)
    high_iota = row_iota.astype(F32).astype(BF16)
    one, zero = jnp.ones((128, 128), BF16), jnp.zeros((128, 128), BF16)
    found = []
    for start in range(0, 8 * tiles, 8):
        high = high_ref[start : start + 8, :].astype(F32)
        low = low_ref[start : start + 8, :]
        hot = jnp.concatenate(
            [
                jnp.where(repeated(high[j : j + 1], 128) == high_iota, one, zero)
                for j in range(8)
            ],
            axis=1,
        )
        lines = lax.dot_general(
            parts, hot, (((0,), (0,)), ((), ())), preferred_element_type=F32
        )
        lines = lines[:128] + lines[128:]
        for j in range(8):
            line = jnp.where(
                row_iota == low[j : j + 1], lines[:, j * 128 : j * 128 + 128], 0.0
            )
            found.append(jnp.sum(line, axis=0, keepdims=True))
    return jnp.concatenate(found, axis=0)


def repeated(line, size):
    block = jnp.broadcast_to(line, (16, 128)).astype(BF16)
    return jnp.concatenate([block] * (size // 16), axis=0) if size > 16 else block


def summed(high_ref, low_ref, value_ref, high_size, low_size, by_low=False):
    refs, sizes = (high_ref, low_ref), (high_size, low_size)
    bearer = 1 if by_low else 0
    iotas = [iota((size, 128), 0).astype(F32).astype(BF16) for size in sizes]
    zeros = [jnp.zeros((size, 128), BF16) for size in sizes]
    one = jnp.ones((sizes[1 - bearer], 128), BF16)
    total = None
    for start in range(0, high_ref.shape[0], 8):
        places = [ref[start : start + 8, :].astype(F32) for ref in refs]
        value = value_ref[start : start + 8, :]
        coarse = value.astype(BF16).astype(F32)
        fine = value - coarse
        size, zero = sizes[bearer], zeros[bearer]
        coarse_hot, fine_hot, plain_hot = [], [], []
        for j in range(8):
            same = [
                repeated(places[side][j : j + 1], sizes[side]) == iotas[side] for side in range(2)
            ]
            coarse_hot.append(jnp.where(same[bearer], repeated(coarse[j : j + 1], size), zero))
            fine_hot.append(jnp.where(same[bearer], repeated(fine[j : j + 1], size), zero))
            plain_hot.append(jnp.where(same[1 - bearer], one, zeros[1 - bearer]))
        value_hot = jnp.concatenate(
            [jnp.concatenate(coarse_hot, axis=1), jnp.concatenate(fine_hot, axis=1)], axis=0
        )
        plain_hot = jnp.concatenate(plain_hot, axis=1)
        sides = (plain_hot, value_hot) if by_low else (value_hot, plain_hot)
        product = lax.dot_general(
            *sides, (((1,), (1,)), ((), ())), preferred_element_type=F32
        )
        total = product if total is None else total + product
    if by_low:
        return total[:, :low_size] + total[:, low_size:]
    return total[:high_size] + total[high_size:]


def summed_by_columns(row_ref, value_ref, hot_ref):
    row_iota = iota((64, 128), 0).astype(F32).astype(BF16)
    zero = jnp.zeros((64, 128), BF16)
    total = jnp.zeros((128, 256), F32)
    for start in range(0, 64, 8):
        rows = row_ref[start : start + 8, :].astype(F32)
        value = value_ref[start : start + 8, :]
        coarse = value.astype(BF16).astype(F32)
        fine = value - coarse
        coarse_hot, fine_hot = [], []
        for j in range(8):
            same = repeated(rows[j : j + 1], 64) == row_iota
            coarse_hot.append(jnp.where(same, repeated(coarse[j : j + 1], 64), zero))
            fine_hot.append(jnp.where(same, repeated(fine[j : j + 1], 64), zero))
        value_hot = jnp.concatenate(
            [jnp.concatenate(coarse_hot, axis=1), jnp.concatenate(fine_hot, axis=1)], axis=0
        )
        total = total + jnp.dot(
            value_hot, hot_ref[start * 128 : start * 128 + 1024, :], preferred_element_type=F32
        )
    return total[:64] + total[64:]


def columns_kernel(link_cell, hot):
    cols = jnp.bitwise_and(packed(link_cell[...]), 255).astype(F32).T
    lane = iota((128, 256), 1).astype(F32)
    for j in range(64):
        same = jnp.broadcast_to(cols[:, j : j + 1], (128, 256)) == lane
        hot[j * 128 : j * 128 + 128, :] = jnp.where(same, 1.0, 0.0).astype(BF16)


def cell_place(cell):
    high = jnp.where(
        cell >= 0, jnp.bitwise_and(cell >> 7, 1) * 64 + (cell >> 8), -1
    )
    return high, jnp.bitwise_and(cell, 127)


def node_place(node):
    high = jnp.where(
        node >= 0, jnp.bitwise_and(node >> 7, 1) * 32 + (node >> 8), -1
    )
    return high, jnp.bitwise_and(node, 127)


def pipe_table(state):
    return jnp.concatenate([state[:, :128], state[:, 128:]], axis=0)


def strips(blocks, start):
    return jnp.concatenate([block[start : start + HALO_ROWS] for block in blocks], axis=0)


def row_col():
    return lax.axis_index("row"), lax.axis_index("col")


def even(dim):
    return jnp.bitwise_and(row_col()[dim], 1) == 0


def start_kernel(
    surface, cond_x, cond_y, porosity, rainfall, pipes, fields, near, far, tips, arrived
):
    copies = [
        pltpu.make_async_copy(source, fields.at[index], arrived.at[index])
        for index, source in enumerate((surface, cond_x, cond_y, porosity, rainfall))
    ]
    copies.append(pltpu.make_async_copy(pipes.at[24:32, :], tips, arrived.at[5]))
    for copy in copies:
        copy.start()
    for copy in copies:
        copy.wait()
    fields[3] = 1.0 / fields[3]
    for index in range(5):
        halves = [fields[index, :, 0:128], fields[index, :, 128:256]]
        top, bottom = strips(halves, 0), strips(halves, 60)
        near[pl.ds(index * 8, 8), :] = jnp.where(even(0), bottom, top)
        far[pl.ds(index * 8, 8), :] = jnp.where(even(0), top, bottom)
    near[40:48, :] = jnp.concatenate(
        [tips[7:8, 0:128], tips[7:8, 128:256], jnp.zeros((6, 128), F32)], axis=0
    )


def tall_block(block, near, far, start):
    near, far = near[start : start + 4, :], far[start : start + 4, :]
    over = jnp.where(even(0), far, near)
    under = jnp.where(even(0), near, far)
    over = jnp.where(row_col()[0] > 0, over, 0.0)
    under = jnp.where(row_col()[0] < 7, under, 0.0)
    return jnp.concatenate([block, under, over], axis=0)


def pack_cols_kernel(near, far, fields, link_cell, tall_out, out):
    lane = iota((72, 128), 1)
    message = jnp.zeros((72, 128), F32)
    for index in range(5):
        tall = [
            tall_block(
                fields[index, :, half * 128 : half * 128 + 128], near, far,
                index * 8 + half * 4,
            )
            for half in range(2)
        ]
        tall_out[index, :, 0:128] = tall[0]
        tall_out[index, :, 128:256] = tall[1]
        edges = jnp.where(
            lane < HALO_COLS, tall[0], jnp.where(lane >= 128 - HALO_COLS, tall[1], 0.0)
        )
        if index:
            edges = pltpu.roll(edges, index * 2 * HALO_COLS, 1)
        message = message + edges
    out[0:72, :] = message
    out[72:136, :] = packed(link_cell[...]).astype(F32)


def owner_start_kernel(
    pipes, link_node, link_coef, kinds, laws, uppers, lowers, table, nodes, node_high, node_low,
    coef, classes, matrices, meets,
):
    meets[...] = jnp.concatenate(
        [uppers[...], lowers[...], jnp.zeros((4, 128), jnp.int32)], axis=0
    )
    classes[...] = kinds[...]
    matrices[...] = laws[...]
    table[...] = pipe_table(pipes[...])
    high, low = node_place(packed(link_node[...]))
    node_high[...] = high
    node_low[...] = low
    coef[...] = packed(link_coef[...])
    nodes[...] = gathered(table, 64, high, low)


def swept(state, gains):
    def once(_, w):
        return (
            gains[0] * w
            + gains[1] * pltpu.roll(w, 1, 0)
            + gains[2] * pltpu.roll(w, 71, 0)
            + gains[3] * pltpu.roll(w, 1, 1)
            + gains[4] * pltpu.roll(w, 383, 1)
            + gains[5]
        )

    for i in range(SWEEPS):
        state = once(i, state)
    return state


def put(out, blocks, index, value):
    out[pl.ds(index, 128, stride=blocks), :] = value


def taken(got, blocks, index):
    return got[pl.ds(index, 128, stride=blocks), :]


def build_message(out, blocks, heads, nodes):
    put(out, blocks, 0, paired(heads, nodes))
    if blocks == 6:
        put(out, blocks, 5, beside(nodes))


def zone_heads(edge, zone_place, edge_ref, zone_ref):
    lane = iota((64, 128), 1)
    edge_ref[...] = jnp.where(lane < ZONE, edge, pltpu.roll(edge, 2 * ZONE, 1))
    lane8 = iota((8, 128), 1)
    table = jnp.zeros((8, 128), F32)
    for s in range(8):
        line = edge_ref[pl.ds(s, 8, stride=8), :]
        if s:
            line = pltpu.roll(line, s * 16, 1)
        table = jnp.where((lane8 >> 4) == s, line, table)
    zone_ref[...] = table
    zone_row, zone_col = zone_place
    high = jnp.where(zone_row >= 0, zone_row >> 3, -1)
    low = jnp.bitwise_and(zone_row, 7) * 16 + zone_col
    return gathered(zone_ref, 8, high, low)


def sweep_and_gather(
    state, gains, cell_high, cell_low, zone_place, surface_out, heads_out, zone_out, cell_table,
    edge_ref, zone_ref,
):
    state = swept(state, gains)
    surface_out[...] = state[:64]
    cell_table[0:64, :] = state[:64, 0:128]
    cell_table[64:128, :] = state[:64, 128:256]
    heads = jnp.concatenate(
        [
            gathered_by_product(cell_table[...], cell_high, cell_low, 4),
            gathered(cell_table, 128, cell_high[32:64, :], cell_low[32:64, :]),
        ],
        axis=0,
    )
    heads_out[...] = heads
    if zone_place is not None:
        zone_out[...] = zone_heads(state[:64, 256:384], zone_place, edge_ref, zone_ref)
    return heads


def first_sweep_kernel(
    tall, near_col, far_col, near, link_cell, table, nodes, coef,
    gains_out, inverse_out, cell_high, cell_low, zone_row_out, zone_col_out, surface_out, heads_out,
    zone_out, out, cell_table, edge_ref, zone_ref,
):
    lane = iota((72, 128), 1)
    wide = []
    from_west = jnp.where(even(1), far_col[...], near_col[...])
    from_east = jnp.where(even(1), near_col[...], far_col[...])
    for index in range(5):
        west = jnp.where(row_col()[1] > 0, from_west[0:72, :], 0.0)
        east = jnp.where(row_col()[1] < 15, from_east[0:72, :], 0.0)
        if index:
            west = pltpu.roll(west, 128 - index * 2 * HALO_COLS, 1)
            east = pltpu.roll(east, 128 - index * 2 * HALO_COLS, 1)
        edge = jnp.where(
            lane < HALO_COLS, east, jnp.where(lane >= 128 - HALO_COLS, west, 0.0)
        )
        wide.append(jnp.concatenate([tall[index], edge], axis=1))
    state, cond_x, cond_y, inverse, rainfall = wide
    north = pltpu.roll(cond_x, 1, 0)
    west = pltpu.roll(cond_y, 1, 1)
    gains = [
        1.0 - (north + cond_x + west + cond_y) * inverse,
        north * inverse, cond_x * inverse, west * inverse, cond_y * inverse, rainfall,
    ]
    for index, gain in enumerate(gains):
        gains_out[index] = gain
    inverse_out[...] = inverse[:64]
    cells = paired(from_west[72:136, :], from_east[72:136, :]).astype(jnp.int32)
    col = jnp.bitwise_and(cells, 255)
    is_west = iota((128, 128), 1) < 64
    zone_col = jnp.where(is_west, col - (256 - 2 * ZONE), col)
    inside = (zone_col >= 0) & (zone_col < 2 * ZONE)
    inside = inside & (jnp.where(is_west, zone_col, zone_col + ZONE) >= ZONE)
    zone_row = jnp.where((cells >= 0) & inside & (jnp.where(is_west, 0, zone_col) < ZONE), cells >> 8, -1)
    zone_row_out[...] = zone_row
    zone_col_out[...] = zone_col
    high, low = cell_place(packed(link_cell[...]))
    cell_high[...] = high
    cell_low[...] = low
    heads = sweep_and_gather(
        state, gains, cell_high, cell_low, (zone_row, zone_col), surface_out, heads_out, zone_out,
        cell_table, edge_ref, zone_ref,
    )
    build_message(out, 6, heads, nodes[...])
    own_rows = (iota((128, 128), 0) >> 4) == row_col()[0]
    for half in range(2):
        own = jnp.broadcast_to(table[half * 32 : half * 32 + 1, :], (128, 128))
        other = jnp.broadcast_to(near[40 + half : 41 + half, :], (128, 128))
        put(out, 6, 1 + half, jnp.where(own_rows, own, other))
    put(out, 6, 3, paired(coef[...], coef[...]))
    put(out, 6, 4, beside(coef[...]))


def sweep_kernel(
    last, surface, near, far, gains_ref, cell_high, cell_low, zone_row, zone_col,
    table, nodes, surface_out, heads_out, zone_out, out, cell_table, edge_ref, zone_ref,
):
    state = jnp.concatenate(
        [
            tall_block(
                surface[:, block * 128 : block * 128 + 128], near, far, block * 4
            )
            for block in range(3)
        ],
        axis=1,
    )
    gains = [gains_ref[index] for index in range(6)]
    zone_place = None if last else (zone_row[...], zone_col[...])
    heads = sweep_and_gather(
        state, gains, cell_high, cell_low, zone_place, surface_out, heads_out, zone_out,
        cell_table, edge_ref, zone_ref,
    )
    blocks = 5 if last else 6
    build_message(out, blocks, heads, nodes[...])
    for index, row in enumerate(ENDS):
        put(out, blocks, 1 + index, jnp.broadcast_to(table[row : row + 1, :], (128, 128)))


def tile_kernel(
    first, last, got, surface, inverse, heads, zone, cell_high, hot, zone_row, zone_col, *rest
):
    rest = list(rest)
    if first:
        own_coef = low_halves(taken(got, 6, 3))
        zone_coef = taken(got, 6, 4)
    else:
        own_coef = rest.pop(0)[...]
        zone_coef = rest.pop(0)[...]
    surface_out = rest.pop(0)
    if not last:
        near, far = rest.pop(0), rest.pop(0)
    if first:
        rest.pop(0)[...] = own_coef
        rest.pop(0)[...] = zone_coef
    value_ref, zone_value_ref, row_ref = rest
    value_ref[...] = jnp.where(
        cell_high[...] >= 0, own_coef * (heads[...] - high_halves(taken(got, 5 if last else 6, 0))), 0.0
    )
    row_ref[...] = jnp.where(cell_high[...] >= 0, jnp.bitwise_and(cell_high[...], 63), -1)
    lost = summed_by_columns(row_ref, value_ref, hot)
    left = surface[:, 0:128] - inverse[:, 0:128] * lost[:, 0:128]
    right = surface[:, 128:256] - inverse[:, 128:256] * lost[:, 128:256]
    surface_out[:, 0:128] = left
    surface_out[:, 128:256] = right
    if last:
        return
    zone_value_ref[...] = jnp.where(
        zone_row[...] >= 0, zone_coef * (zone[...] - taken(got, 6, 5)), 0.0
    )
    lost = summed(zone_row, zone_col, zone_value_ref, 64, 2 * ZONE, by_low=True)
    lost = jnp.concatenate([lost, jnp.zeros((64, 128 - 2 * ZONE), F32)], axis=1)
    lane = iota((64, 128), 1)
    lost = jnp.where(
        lane < ZONE, lost,
        jnp.where(lane >= 128 - ZONE, pltpu.roll(lost, 128 - 2 * ZONE, 1), 0.0),
    )
    edge = surface[:, 256:384] - inverse[:, 256:384] * lost
    surface_out[:, 256:384] = edge
    top, bottom = strips([left, right, edge], 0), strips([left, right, edge], 60)
    near[...] = jnp.where(even(0), bottom, top)
    far[...] = jnp.where(even(0), top, bottom)


def owner_kernel(
    first, last, got, nodes, node_high, node_low, coef, table, meets, classes, matrices, *rest
):
    blocks = 5 if last else 6
    if last:
        pipes_out, value_ref, ends_ref = rest
    else:
        table_out, nodes_out, value_ref, ends_ref = rest
    value_ref[...] = jnp.where(
        node_high[...] >= 0, coef[...] * (low_halves(taken(got, blocks, 0)) - nodes[...]), 0.0
    )
    inflow = summed(node_high, node_low, value_ref, 64, 128)
    balance = table[...] + inflow
    start = pl.multiple_of(row_col()[0] * (16 * blocks), 16)
    other = pl.multiple_of((row_col()[0] ^ 1) * 96, 32) if first else start
    for index in range(4):
        source, block = (other, index - 1) if first and index >= 2 else (start, 1 + index)
        ends_ref[index * 16 : index * 16 + 16, :] = got[pl.ds(source + block, 16, stride=blocks), :]
    meet = meets[...]
    meet_high = jnp.bitwise_and(meet >> 7, 1) * 16 + (meet >> 8)
    meet_high = jnp.where(iota((8, 128), 0) < 2, meet_high + 32, meet_high)
    met = gathered(ends_ref, 64, meet_high, meet) * boundary_gain
    node_row = iota((32, 128), 0)
    parts = []
    for half in range(2):
        part = balance[half * 32 : half * 32 + 32]
        part = part + jnp.where(
            node_row == 0, met[half : half + 1],
            jnp.where(node_row == 31, met[2 + half : 3 + half], 0.0),
        )
        products = jnp.dot(
            matrices[...], part, precision=lax.Precision.HIGHEST, preferred_element_type=F32
        )
        kind = classes[half : half + 1, :]
        updated = jnp.zeros((32, 128), F32)
        for index in range(CLASSES):
            updated = jnp.where(kind == index, products[index * 32 : index * 32 + 32], updated)
        parts.append(updated)
    if last:
        pipes_out[:, 0:128] = parts[0]
        pipes_out[:, 128:256] = parts[1]
        return
    table_out[0:32, :] = parts[0]
    table_out[32:64, :] = parts[1]
    nodes_out[...] = gathered(table_out, 64, node_high[...], node_low[...])


def shape(*dims, dtype=F32):
    return jax.ShapeDtypeStruct(dims, dtype)


def call(kernel, inputs, outputs, scratch=(), space=pltpu.VMEM):
    vmem = pl.BlockSpec(memory_space=pltpu.VMEM)
    return pl.pallas_call(
        kernel,
        out_shape=outputs,
        in_specs=[pl.BlockSpec(memory_space=space)] * len(inputs),
        out_specs=[vmem] * len(outputs),
        scratch_shapes=list(scratch),
        compiler_params=pltpu.CompilerParams(vmem_limit_bytes=16 << 20),
        cost_estimate=pl.CostEstimate(flops=10**9, bytes_accessed=1 << 20, transcendentals=0),
    )(*inputs)


def copy_kernel(source, out):
    out[...] = source[...]


def swapped(near, far, dim, copied=None):
    sizes = lax.axis_size("row"), lax.axis_size("col")
    routes = [], []
    for row in range(sizes[0]):
        for col in range(sizes[1]):
            here = [row, col]
            partner = list(here)
            partner[dim] ^= 1
            other = list(here)
            other[dim] += 1 if here[dim] % 2 else -1
            if not 0 <= other[dim] < sizes[dim]:
                other = list(here)
                other[1 - dim] ^= 1
            for route, there in zip(routes, (partner, other)):
                route.append((row * sizes[1] + col, there[0] * sizes[1] + there[1]))
    if copied == "near":
        (near,) = call(copy_kernel, (near,), [shape(*near.shape)])
    if copied == "far":
        (far,) = call(copy_kernel, (far,), [shape(*far.shape)])
    far = lax.ppermute(far, ("row", "col"), routes[1])
    return lax.ppermute(near, ("row", "col"), routes[0]), far


def body(
    surface_head, conduct_x, conduct_y, porosity, rainfall, pipe_head, pipe_class, pipe_up,
    pipe_down, pipe_matrices, link_cell, link_node, link_coef,
):
    link_cell = link_cell[0]
    uppers, lowers = pipe_up.reshape(2, 128), pipe_down.reshape(2, 128)
    classes = pipe_class.reshape(2, 128)
    matrices = pipe_matrices.reshape(CLASSES * 32, 32)
    ints = functools.partial(shape, dtype=jnp.int32)

    fields, near, far = call(
        start_kernel,
        [pltpu.with_memory_space_constraint(x, pltpu.HBM) for x in (
            surface_head, conduct_x, conduct_y, porosity, rainfall, pipe_head
        )],
        [shape(5, 64, 256), shape(48, 128), shape(40, 128)],
        [pltpu.VMEM((8, 256), F32), pltpu.SemaphoreType.DMA((6,))], space=pltpu.HBM,
    )
    near, far = swapped(near, far, 0, "near")
    link_node = link_node[:, 0, :]
    link_coef = link_coef[:, 0, :]
    table, nodes, node_high, node_low, coef, classes, matrices, meets = call(
        owner_start_kernel, (pipe_head, link_node, link_coef, classes, matrices, uppers, lowers),
        [shape(64, 128), shape(64, 128), ints(64, 128), ints(64, 128), shape(64, 128),
         ints(2, 128), shape(128, 32), ints(8, 128)],
    )
    near, far, nodes = lax.optimization_barrier((near, far, nodes))
    tall, sent = call(
        pack_cols_kernel, (near, far, fields, link_cell),
        [shape(5, 72, 256), shape(136, 128)],
    )
    sent, cells = lax.optimization_barrier((sent, link_cell))
    near_col, far_col = swapped(sent, sent, 1)
    (hot,) = call(columns_kernel, (cells,), [shape(8192, 256, dtype=BF16)])
    gather_scratch = [
        pltpu.VMEM((128, 128), F32), pltpu.VMEM((64, 128), F32), pltpu.VMEM((8, 128), F32)
    ]
    swept_shapes = [shape(64, 384), shape(64, 128), shape(128, 128)]
    (gains, inverse, cell_high, cell_low, zone_row, zone_col, surface, heads, zone, sent) = call(
        first_sweep_kernel,
        (tall, near_col, far_col, near, link_cell, table, nodes, coef),
        [shape(6, 72, 384), shape(64, 384), ints(64, 128), ints(64, 128), ints(128, 128),
         ints(128, 128), *swept_shapes, shape(768, 128)],
        gather_scratch,
    )
    sent, hot = lax.optimization_barrier((sent, hot))
    coefs = ()
    for step in range(STEPS):
        first, last = step == 0, step == STEPS - 1
        if step:
            surface, heads, zone, sent = call(
                functools.partial(sweep_kernel, last),
                (surface, near, far, gains, cell_high, cell_low, zone_row, zone_col,
                 table, nodes),
                [*swept_shapes, shape(640 if last else 768, 128)], gather_scratch,
            )
        got = lax.all_to_all(
            sent.reshape(128, 1, -1), ("row", "col"), split_axis=0, concat_axis=0, tiled=True
        ).reshape(-1, 128)
        tile_inputs = (surface, inverse, heads, zone, cell_high, hot, zone_row, zone_col, *coefs)
        owner_inputs = (nodes, node_high, node_low, coef, table, meets, classes, matrices)
        tile_scratch = [
            pltpu.VMEM((64, 128), F32), pltpu.VMEM((128, 128), F32), pltpu.VMEM((64, 128), jnp.int32)
        ]
        owner_scratch = [pltpu.VMEM((64, 128), F32), pltpu.VMEM((64, 128), F32)]
        if last:
            (pipes_out,) = call(
                functools.partial(owner_kernel, False, True), (got, *owner_inputs),
                [shape(32, 256)], owner_scratch,
            )
            (surface_out,) = call(
                functools.partial(tile_kernel, False, True), (got, *tile_inputs), [shape(64, 256)],
                tile_scratch,
            )
            return surface_out, pipes_out
        outputs = [shape(64, 384), shape(12, 128), shape(12, 128)]
        if first:
            outputs += [shape(64, 128), shape(128, 128)]
        surface, near, far, *new_coefs = call(
            functools.partial(tile_kernel, first, False), (got, *tile_inputs), outputs,
            tile_scratch,
        )
        near, far = swapped(near, far, 0, "far")
        table, nodes = call(
            functools.partial(owner_kernel, first, False), (got, *owner_inputs),
            [shape(64, 128), shape(64, 128)], owner_scratch,
        )
        if first:
            coefs = tuple(new_coefs)


def solution(mesh):
    placed = (
        P("row", "col"),
        P("row", "col"),
        P("row", "col"),
        P("row", "col"),
        P("row", "col"),
        P(None, ("row", "col")),
        P(("row", "col")),
        P(("row", "col")),
        P(("row", "col")),
        P(),
        P(("row", "col"), None, None),
        P(None, ("row", "col"), None),
        P(None, ("row", "col"), None),
    )
    return jax.shard_map(
        body,
        mesh=mesh,
        in_specs=placed,
        out_specs=(P("row", "col"), P(None, ("row", "col"))),
        check_vma=False,
    )
```

```python
import functools

import jax
import jax.numpy as jnp
from jax import lax
from jax.experimental import pallas as pl
from jax.experimental.pallas import tpu as pltpu
from jax.sharding import PartitionSpec as P

CLASSES = 4
SWEEPS = 4
STEPS = 3
F32 = jnp.float32
BF16 = jnp.bfloat16

boundary_gain = 0.5

HALO_ROWS = 4
HALO_COLS = 12
ZONE = 8
ENDS = (0, 32, 31, 63)


def iota(shape, dim):
    return lax.broadcasted_iota(jnp.int32, shape, dim)


def packed(x):
    return jnp.concatenate([x[:64], x[64:]], axis=1)


def low_halves(block):
    lane = iota((64, 128), 1)
    return jnp.where(lane < 64, block[:64], pltpu.roll(block[64:], 64, 1))


def high_halves(block):
    lane = iota((64, 128), 1)
    return jnp.where(lane < 64, pltpu.roll(block[:64], 64, 1), block[64:])


def paired(low, high):
    lane = iota((64, 128), 1)
    top = jnp.where(lane < 64, low, pltpu.roll(high, 64, 1))
    bottom = jnp.where(lane < 64, pltpu.roll(low, 64, 1), high)
    return jnp.concatenate([top, bottom], axis=0)


def beside(values):
    lane = iota((128, 128), 1)
    both = paired(values, values)
    return jnp.where(lane < 64, pltpu.roll(both, 1, 0), pltpu.roll(both, 127, 0))


def gathered(table_ref, rows, high, low):
    low = jnp.bitwise_and(low, 127)
    tiles = []
    for start in range(0, high.shape[0], 8):
        tile_high, tile_low = high[start : start + 8], low[start : start + 8]
        found = jnp.zeros((8, 128), F32)
        for row in range(rows):
            line = jnp.broadcast_to(table_ref[row : row + 1, :], (8, 128))
            values = jnp.take_along_axis(line, tile_low, axis=1)
            found = jnp.where(tile_high == row, values, found)
        tiles.append(found)
    return jnp.concatenate(tiles, axis=0) if len(tiles) > 1 else tiles[0]


def gathered_by_product(table, high_ref, low_ref, tiles):
    coarse = table.astype(BF16)
    fine = (table - coarse.astype(F32)).astype(BF16)
    parts = jnp.concatenate([coarse, fine], axis=1)
    row_iota = iota((128, 128), 0)
    high_iota = row_iota.astype(F32).astype(BF16)
    one, zero = jnp.ones((128, 128), BF16), jnp.zeros((128, 128), BF16)
    found = []
    for start in range(0, 8 * tiles, 8):
        high = high_ref[start : start + 8, :].astype(F32)
        low = low_ref[start : start + 8, :]
        hot = jnp.concatenate(
            [
                jnp.where(repeated(high[j : j + 1], 128) == high_iota, one, zero)
                for j in range(8)
            ],
            axis=1,
        )
        lines = lax.dot_general(
            parts, hot, (((0,), (0,)), ((), ())), preferred_element_type=F32
        )
        lines = lines[:128] + lines[128:]
        for j in range(8):
            line = jnp.where(
                row_iota == low[j : j + 1], lines[:, j * 128 : j * 128 + 128], 0.0
            )
            found.append(jnp.sum(line, axis=0, keepdims=True))
    return jnp.concatenate(found, axis=0)


def repeated(line, size):
    block = jnp.broadcast_to(line, (16, 128)).astype(BF16)
    return jnp.concatenate([block] * (size // 16), axis=0) if size > 16 else block


def summed(high_ref, low_ref, value_ref, high_size, low_size, by_low=False):
    refs, sizes = (high_ref, low_ref), (high_size, low_size)
    bearer = 1 if by_low else 0
    iotas = [iota((size, 128), 0).astype(F32).astype(BF16) for size in sizes]
    zeros = [jnp.zeros((size, 128), BF16) for size in sizes]
    one = jnp.ones((sizes[1 - bearer], 128), BF16)
    total = None
    for start in range(0, high_ref.shape[0], 8):
        places = [ref[start : start + 8, :].astype(F32) for ref in refs]
        value = value_ref[start : start + 8, :]
        coarse = value.astype(BF16).astype(F32)
        fine = value - coarse
        size, zero = sizes[bearer], zeros[bearer]
        coarse_hot, fine_hot, plain_hot = [], [], []
        for j in range(8):
            same = [
                repeated(places[side][j : j + 1], sizes[side]) == iotas[side] for side in range(2)
            ]
            coarse_hot.append(jnp.where(same[bearer], repeated(coarse[j : j + 1], size), zero))
            fine_hot.append(jnp.where(same[bearer], repeated(fine[j : j + 1], size), zero))
            plain_hot.append(jnp.where(same[1 - bearer], one, zeros[1 - bearer]))
        value_hot = jnp.concatenate(
            [jnp.concatenate(coarse_hot, axis=1), jnp.concatenate(fine_hot, axis=1)], axis=0
        )
        plain_hot = jnp.concatenate(plain_hot, axis=1)
        sides = (plain_hot, value_hot) if by_low else (value_hot, plain_hot)
        product = lax.dot_general(
            *sides, (((1,), (1,)), ((), ())), preferred_element_type=F32
        )
        total = product if total is None else total + product
    if by_low:
        return total[:, :low_size] + total[:, low_size:]
    return total[:high_size] + total[high_size:]


def summed_by_columns(row_ref, value_ref, hot_ref):
    row_iota = iota((64, 128), 0).astype(F32).astype(BF16)
    zero = jnp.zeros((64, 128), BF16)
    total = jnp.zeros((128, 256), F32)
    for start in range(0, 64, 8):
        rows = row_ref[start : start + 8, :].astype(F32)
        value = value_ref[start : start + 8, :]
        coarse = value.astype(BF16).astype(F32)
        fine = value - coarse
        coarse_hot, fine_hot = [], []
        for j in range(8):
            same = repeated(rows[j : j + 1], 64) == row_iota
            coarse_hot.append(jnp.where(same, repeated(coarse[j : j + 1], 64), zero))
            fine_hot.append(jnp.where(same, repeated(fine[j : j + 1], 64), zero))
        value_hot = jnp.concatenate(
            [jnp.concatenate(coarse_hot, axis=1), jnp.concatenate(fine_hot, axis=1)], axis=0
        )
        total = total + jnp.dot(
            value_hot, hot_ref[start * 128 : start * 128 + 1024, :], preferred_element_type=F32
        )
    return total[:64] + total[64:]


def columns_kernel(link_cell, hot):
    cols = jnp.bitwise_and(packed(link_cell[...]), 255).astype(F32).T
    lane = iota((128, 256), 1).astype(F32)
    for j in range(64):
        same = jnp.broadcast_to(cols[:, j : j + 1], (128, 256)) == lane
        hot[j * 128 : j * 128 + 128, :] = jnp.where(same, 1.0, 0.0).astype(BF16)


def cell_place(cell):
    high = jnp.where(
        cell >= 0, jnp.bitwise_and(cell >> 7, 1) * 64 + (cell >> 8), -1
    )
    return high, jnp.bitwise_and(cell, 127)


def node_place(node):
    high = jnp.where(
        node >= 0, jnp.bitwise_and(node >> 7, 1) * 32 + (node >> 8), -1
    )
    return high, jnp.bitwise_and(node, 127)


def pipe_table(state):
    return jnp.concatenate([state[:, :128], state[:, 128:]], axis=0)


def strips(blocks, start):
    return jnp.concatenate([block[start : start + HALO_ROWS] for block in blocks], axis=0)


def row_col():
    return lax.axis_index("row"), lax.axis_index("col")


def even(dim):
    return jnp.bitwise_and(row_col()[dim], 1) == 0


def start_kernel(
    surface, cond_x, cond_y, porosity, rainfall, pipes, fields, near, far, tips, arrived
):
    copies = [
        pltpu.make_async_copy(source, fields.at[index], arrived.at[index])
        for index, source in enumerate((surface, cond_x, cond_y, porosity, rainfall))
    ]
    copies.append(pltpu.make_async_copy(pipes.at[24:32, :], tips, arrived.at[5]))
    for copy in copies:
        copy.start()
    for copy in copies:
        copy.wait()
    fields[3] = 1.0 / fields[3]
    for index in range(5):
        halves = [fields[index, :, 0:128], fields[index, :, 128:256]]
        top, bottom = strips(halves, 0), strips(halves, 60)
        near[pl.ds(index * 8, 8), :] = jnp.where(even(0), bottom, top)
        far[pl.ds(index * 8, 8), :] = jnp.where(even(0), top, bottom)
    near[40:48, :] = jnp.concatenate(
        [tips[7:8, 0:128], tips[7:8, 128:256], jnp.zeros((6, 128), F32)], axis=0
    )


def tall_block(block, near, far, start):
    near, far = near[start : start + 4, :], far[start : start + 4, :]
    over = jnp.where(even(0), far, near)
    under = jnp.where(even(0), near, far)
    over = jnp.where(row_col()[0] > 0, over, 0.0)
    under = jnp.where(row_col()[0] < 7, under, 0.0)
    return jnp.concatenate([block, under, over], axis=0)


def pack_cols_kernel(near, far, fields, link_cell, tall_out, out):
    lane = iota((72, 128), 1)
    message = jnp.zeros((72, 128), F32)
    for index in range(5):
        tall = [
            tall_block(
                fields[index, :, half * 128 : half * 128 + 128], near, far,
                index * 8 + half * 4,
            )
            for half in range(2)
        ]
        tall_out[index, :, 0:128] = tall[0]
        tall_out[index, :, 128:256] = tall[1]
        edges = jnp.where(
            lane < HALO_COLS, tall[0], jnp.where(lane >= 128 - HALO_COLS, tall[1], 0.0)
        )
        if index:
            edges = pltpu.roll(edges, index * 2 * HALO_COLS, 1)
        message = message + edges
    out[0:72, :] = message
    out[72:136, :] = packed(link_cell[...]).astype(F32)


def owner_start_kernel(
    pipes, link_node, link_coef, kinds, laws, uppers, lowers, table, nodes, node_high, node_low,
    coef, classes, matrices, meets,
):
    meets[...] = jnp.concatenate(
        [uppers[...], lowers[...], jnp.zeros((4, 128), jnp.int32)], axis=0
    )
    classes[...] = kinds[...]
    matrices[...] = laws[...]
    table[...] = pipe_table(pipes[...])
    high, low = node_place(packed(link_node[...]))
    node_high[...] = high
    node_low[...] = low
    coef[...] = packed(link_coef[...])
    nodes[...] = gathered(table, 64, high, low)


def swept(state, gains):
    def once(_, w):
        return (
            gains[0] * w
            + gains[1] * pltpu.roll(w, 1, 0)
            + gains[2] * pltpu.roll(w, 71, 0)
            + gains[3] * pltpu.roll(w, 1, 1)
            + gains[4] * pltpu.roll(w, 383, 1)
            + gains[5]
        )

    for i in range(SWEEPS):
        state = once(i, state)
    return state


def put(out, blocks, index, value):
    out[pl.ds(index, 128, stride=blocks), :] = value


def taken(got, blocks, index):
    return got[pl.ds(index, 128, stride=blocks), :]


def build_message(out, blocks, heads, nodes, own_ends, other_ends):
    put(out, blocks, 0, paired(heads, nodes))
    own_rows = (iota((128, 128), 0) >> 4) == row_col()[0]
    for half in range(2):
        own = jnp.broadcast_to(own_ends[half], (128, 128))
        other = jnp.broadcast_to(other_ends[half], (128, 128))
        put(out, blocks, 1 + half, jnp.where(own_rows, own, other))
    if blocks > 3:
        put(out, blocks, blocks - 1, beside(nodes))


def partner_rows(blocks):
    return pl.multiple_of((row_col()[0] ^ 1) * (16 * blocks), 16)


def zone_heads(edge, zone_place, edge_ref, zone_ref):
    lane = iota((64, 128), 1)
    edge_ref[...] = jnp.where(lane < ZONE, edge, pltpu.roll(edge, 2 * ZONE, 1))
    lane8 = iota((8, 128), 1)
    table = jnp.zeros((8, 128), F32)
    for s in range(8):
        line = edge_ref[pl.ds(s, 8, stride=8), :]
        if s:
            line = pltpu.roll(line, s * 16, 1)
        table = jnp.where((lane8 >> 4) == s, line, table)
    zone_ref[...] = table
    zone_row, zone_col = zone_place
    high = jnp.where(zone_row >= 0, zone_row >> 3, -1)
    low = jnp.bitwise_and(zone_row, 7) * 16 + zone_col
    return gathered(zone_ref, 8, high, low)


def sweep_and_gather(
    state, gains, cell_high, cell_low, zone_place, surface_out, heads_out, zone_out, cell_table,
    edge_ref, zone_ref,
):
    state = swept(state, gains)
    surface_out[...] = state[:64]
    cell_table[0:64, :] = state[:64, 0:128]
    cell_table[64:128, :] = state[:64, 128:256]
    heads = jnp.concatenate(
        [
            gathered_by_product(cell_table[...], cell_high, cell_low, 4),
            gathered(cell_table, 128, cell_high[32:64, :], cell_low[32:64, :]),
        ],
        axis=0,
    )
    heads_out[...] = heads
    if zone_place is not None:
        zone_out[...] = zone_heads(state[:64, 256:384], zone_place, edge_ref, zone_ref)
    return heads


def first_sweep_kernel(
    tall, near_col, far_col, near, link_cell, table, nodes, coef,
    gains_out, inverse_out, cell_high, cell_low, zone_row_out, zone_col_out, surface_out, heads_out,
    zone_out, out, cell_table, edge_ref, zone_ref,
):
    lane = iota((72, 128), 1)
    wide = []
    from_west = jnp.where(even(1), far_col[...], near_col[...])
    from_east = jnp.where(even(1), near_col[...], far_col[...])
    for index in range(5):
        west = jnp.where(row_col()[1] > 0, from_west[0:72, :], 0.0)
        east = jnp.where(row_col()[1] < 15, from_east[0:72, :], 0.0)
        if index:
            west = pltpu.roll(west, 128 - index * 2 * HALO_COLS, 1)
            east = pltpu.roll(east, 128 - index * 2 * HALO_COLS, 1)
        edge = jnp.where(
            lane < HALO_COLS, east, jnp.where(lane >= 128 - HALO_COLS, west, 0.0)
        )
        wide.append(jnp.concatenate([tall[index], edge], axis=1))
    state, cond_x, cond_y, inverse, rainfall = wide
    north = pltpu.roll(cond_x, 1, 0)
    west = pltpu.roll(cond_y, 1, 1)
    gains = [
        1.0 - (north + cond_x + west + cond_y) * inverse,
        north * inverse, cond_x * inverse, west * inverse, cond_y * inverse, rainfall,
    ]
    for index, gain in enumerate(gains):
        gains_out[index] = gain
    inverse_out[...] = inverse[:64]
    cells = paired(from_west[72:136, :], from_east[72:136, :]).astype(jnp.int32)
    col = jnp.bitwise_and(cells, 255)
    is_west = iota((128, 128), 1) < 64
    zone_col = jnp.where(is_west, col - (256 - 2 * ZONE), col)
    inside = (zone_col >= 0) & (zone_col < 2 * ZONE)
    inside = inside & (jnp.where(is_west, zone_col, zone_col + ZONE) >= ZONE)
    zone_row = jnp.where((cells >= 0) & inside & (jnp.where(is_west, 0, zone_col) < ZONE), cells >> 8, -1)
    zone_row_out[...] = zone_row
    zone_col_out[...] = zone_col
    high, low = cell_place(packed(link_cell[...]))
    cell_high[...] = high
    cell_low[...] = low
    heads = sweep_and_gather(
        state, gains, cell_high, cell_low, (zone_row, zone_col), surface_out, heads_out, zone_out,
        cell_table, edge_ref, zone_ref,
    )
    build_message(
        out, 6, heads, nodes[...], (table[0:1, :], table[32:33, :]), (near[40:41, :], near[41:42, :])
    )
    put(out, 6, 3, paired(coef[...], coef[...]))
    put(out, 6, 4, beside(coef[...]))


def sweep_kernel(
    last, surface, near, far, gains_ref, cell_high, cell_low, zone_row, zone_col,
    table, nodes, surface_out, heads_out, zone_out, out, cell_table, edge_ref, zone_ref,
):
    state = jnp.concatenate(
        [
            tall_block(
                surface[:, block * 128 : block * 128 + 128], near, far, block * 4
            )
            for block in range(3)
        ],
        axis=1,
    )
    gains = [gains_ref[index] for index in range(6)]
    zone_place = None if last else (zone_row[...], zone_col[...])
    heads = sweep_and_gather(
        state, gains, cell_high, cell_low, zone_place, surface_out, heads_out, zone_out,
        cell_table, edge_ref, zone_ref,
    )
    build_message(
        out, 3 if last else 4, heads, nodes[...], (table[0:1, :], table[32:33, :]),
        (table[31:32, :], table[63:64, :]),
    )


def relayed(got, blocks):
    return jnp.concatenate(
        [got[pl.ds(partner_rows(blocks) + block, 16, stride=blocks), :] for block in (1, 2)], axis=0
    )


def relay_kernel(got, out):
    out[...] = relayed(got, 3)


def tile_kernel(
    first, last, got, surface, inverse, heads, zone, cell_high, hot, zone_row, zone_col, *rest
):
    rest = list(rest)
    blocks = 6 if first else 3 if last else 4
    if first:
        own_coef = low_halves(taken(got, 6, 3))
        zone_coef = taken(got, 6, 4)
    else:
        own_coef = rest.pop(0)[...]
        zone_coef = rest.pop(0)[...]
    surface_out = rest.pop(0)
    if not last:
        near, far = rest.pop(0), rest.pop(0)
    if first:
        rest.pop(0)[...] = own_coef
        rest.pop(0)[...] = zone_coef
    value_ref, zone_value_ref, row_ref = rest
    value_ref[...] = jnp.where(
        cell_high[...] >= 0, own_coef * (heads[...] - high_halves(taken(got, blocks, 0))), 0.0
    )
    row_ref[...] = jnp.where(cell_high[...] >= 0, jnp.bitwise_and(cell_high[...], 63), -1)
    lost = summed_by_columns(row_ref, value_ref, hot)
    left = surface[:, 0:128] - inverse[:, 0:128] * lost[:, 0:128]
    right = surface[:, 128:256] - inverse[:, 128:256] * lost[:, 128:256]
    surface_out[:, 0:128] = left
    surface_out[:, 128:256] = right
    if last:
        return
    zone_value_ref[...] = jnp.where(
        zone_row[...] >= 0, zone_coef * (zone[...] - taken(got, blocks, blocks - 1)), 0.0
    )
    lost = summed(zone_row, zone_col, zone_value_ref, 64, 2 * ZONE, by_low=True)
    lost = jnp.concatenate([lost, jnp.zeros((64, 128 - 2 * ZONE), F32)], axis=1)
    lane = iota((64, 128), 1)
    lost = jnp.where(
        lane < ZONE, lost,
        jnp.where(lane >= 128 - ZONE, pltpu.roll(lost, 128 - 2 * ZONE, 1), 0.0),
    )
    edge = surface[:, 256:384] - inverse[:, 256:384] * lost
    surface_out[:, 256:384] = edge
    top, bottom = strips([left, right, edge], 0), strips([left, right, edge], 60)
    near[0:12, :] = jnp.where(even(0), bottom, top)
    far[...] = jnp.where(even(0), top, bottom)
    if not first:
        near[16:48, :] = relayed(got, blocks)


def inflow_of(blocks, got, nodes, node_high, node_low, coef, value_ref):
    value_ref[...] = jnp.where(
        node_high[...] >= 0, coef[...] * (low_halves(taken(got, blocks, 0)) - nodes[...]), 0.0
    )
    return summed(node_high, node_low, value_ref, 64, 128)


def inflow_kernel(got, nodes, node_high, node_low, coef, out, value_ref):
    out[...] = inflow_of(4, got, nodes, node_high, node_low, coef, value_ref)


def owner_kernel(
    first, last, got, nodes, node_high, node_low, coef, table, meets, classes, matrices, *rest
):
    blocks = 6 if first else 3 if last else 4
    rest = list(rest)
    relay = None if first else rest.pop(0)
    inflow = None if first or last else rest.pop(0)[...]
    if last:
        pipes_out, value_ref, ends_ref = rest
    else:
        table_out, nodes_out, value_ref, ends_ref = rest
    if inflow is None:
        inflow = inflow_of(blocks, got, nodes, node_high, node_low, coef, value_ref)
    balance = table[...] + inflow
    start = pl.multiple_of(row_col()[0] * (16 * blocks), 16)
    for half in range(2):
        ends_ref[half * 16 : half * 16 + 16, :] = got[
            pl.ds(start + 1 + half, 16, stride=blocks), :
        ]
    if first:
        ends_ref[32:64, :] = relayed(got, blocks)
    else:
        ends_ref[32:64, :] = relay[0:32, :] if last else relay[16:48, :]
    meet = meets[...]
    meet_high = jnp.bitwise_and(meet >> 7, 1) * 16 + (meet >> 8)
    meet_high = jnp.where(iota((8, 128), 0) < 2, meet_high + 32, meet_high)
    met = gathered(ends_ref, 64, meet_high, meet) * boundary_gain
    node_row = iota((32, 128), 0)
    parts = []
    for half in range(2):
        part = balance[half * 32 : half * 32 + 32]
        part = part + jnp.where(
            node_row == 0, met[half : half + 1],
            jnp.where(node_row == 31, met[2 + half : 3 + half], 0.0),
        )
        products = jnp.dot(
            matrices[...], part, precision=lax.Precision.HIGHEST, preferred_element_type=F32
        )
        kind = classes[half : half + 1, :]
        updated = jnp.zeros((32, 128), F32)
        for index in range(CLASSES):
            updated = jnp.where(kind == index, products[index * 32 : index * 32 + 32], updated)
        parts.append(updated)
    if last:
        pipes_out[:, 0:128] = parts[0]
        pipes_out[:, 128:256] = parts[1]
        return
    table_out[0:32, :] = parts[0]
    table_out[32:64, :] = parts[1]
    nodes_out[...] = gathered(table_out, 64, node_high[...], node_low[...])


def shape(*dims, dtype=F32):
    return jax.ShapeDtypeStruct(dims, dtype)


def call(kernel, inputs, outputs, scratch=(), space=pltpu.VMEM, flops=10**9):
    vmem = pl.BlockSpec(memory_space=pltpu.VMEM)
    return pl.pallas_call(
        kernel,
        out_shape=outputs,
        in_specs=[pl.BlockSpec(memory_space=space)] * len(inputs),
        out_specs=[vmem] * len(outputs),
        scratch_shapes=list(scratch),
        compiler_params=pltpu.CompilerParams(vmem_limit_bytes=16 << 20),
        cost_estimate=pl.CostEstimate(flops=flops, bytes_accessed=1 << 20, transcendentals=0),
    )(*inputs)


def copy_kernel(source, out):
    out[...] = source[...]


def swapped(near, far, dim, copied=None):
    sizes = lax.axis_size("row"), lax.axis_size("col")
    routes = [], []
    for row in range(sizes[0]):
        for col in range(sizes[1]):
            here = [row, col]
            partner = list(here)
            partner[dim] ^= 1
            other = list(here)
            other[dim] += 1 if here[dim] % 2 else -1
            if not 0 <= other[dim] < sizes[dim]:
                other = list(here)
                other[1 - dim] ^= 1
            for route, there in zip(routes, (partner, other)):
                route.append((row * sizes[1] + col, there[0] * sizes[1] + there[1]))
    if far is None:
        return lax.ppermute(near, ("row", "col"), routes[0])
    if copied == "near":
        (near,) = call(copy_kernel, (near,), [shape(*near.shape)])
    if copied == "far":
        (far,) = call(copy_kernel, (far,), [shape(*far.shape)])
    far = lax.ppermute(far, ("row", "col"), routes[1])
    return lax.ppermute(near, ("row", "col"), routes[0]), far


def body(
    surface_head, conduct_x, conduct_y, porosity, rainfall, pipe_head, pipe_class, pipe_up,
    pipe_down, pipe_matrices, link_cell, link_node, link_coef,
):
    link_cell = link_cell[0]
    uppers, lowers = pipe_up.reshape(2, 128), pipe_down.reshape(2, 128)
    classes = pipe_class.reshape(2, 128)
    matrices = pipe_matrices.reshape(CLASSES * 32, 32)
    ints = functools.partial(shape, dtype=jnp.int32)

    fields, near, far = call(
        start_kernel,
        [pltpu.with_memory_space_constraint(x, pltpu.HBM) for x in (
            surface_head, conduct_x, conduct_y, porosity, rainfall, pipe_head
        )],
        [shape(5, 64, 256), shape(48, 128), shape(40, 128)],
        [pltpu.VMEM((8, 256), F32), pltpu.SemaphoreType.DMA((6,))], space=pltpu.HBM,
    )
    near, far = swapped(near, far, 0, "near")
    link_node = link_node[:, 0, :]
    link_coef = link_coef[:, 0, :]
    table, nodes, node_high, node_low, coef, classes, matrices, meets = call(
        owner_start_kernel, (pipe_head, link_node, link_coef, classes, matrices, uppers, lowers),
        [shape(64, 128), shape(64, 128), ints(64, 128), ints(64, 128), shape(64, 128),
         ints(2, 128), shape(128, 32), ints(8, 128)],
    )
    near, far, nodes = lax.optimization_barrier((near, far, nodes))
    tall, sent = call(
        pack_cols_kernel, (near, far, fields, link_cell),
        [shape(5, 72, 256), shape(136, 128)],
    )
    sent, cells = lax.optimization_barrier((sent, link_cell))
    near_col, far_col = swapped(sent, sent, 1)
    (hot,) = call(columns_kernel, (cells,), [shape(8192, 256, dtype=BF16)])
    gather_scratch = [
        pltpu.VMEM((128, 128), F32), pltpu.VMEM((64, 128), F32), pltpu.VMEM((8, 128), F32)
    ]
    swept_shapes = [shape(64, 384), shape(64, 128), shape(128, 128)]
    (gains, inverse, cell_high, cell_low, zone_row, zone_col, surface, heads, zone, sent) = call(
        first_sweep_kernel,
        (tall, near_col, far_col, near, link_cell, table, nodes, coef),
        [shape(6, 72, 384), shape(64, 384), ints(64, 128), ints(64, 128), ints(128, 128),
         ints(128, 128), *swept_shapes, shape(768, 128)],
        gather_scratch,
    )
    sent, hot = lax.optimization_barrier((sent, hot))
    coefs = ()
    for step in range(STEPS):
        first, last = step == 0, step == STEPS - 1
        if step:
            surface, heads, zone, sent = call(
                functools.partial(sweep_kernel, last),
                (surface, near, far, gains, cell_high, cell_low, zone_row, zone_col,
                 table, nodes),
                [*swept_shapes, shape(384 if last else 512, 128)], gather_scratch,
            )
        got = lax.all_to_all(
            sent.reshape(128, 1, -1), ("row", "col"), split_axis=0, concat_axis=0, tiled=True
        ).reshape(-1, 128)
        tile_inputs = (surface, inverse, heads, zone, cell_high, hot, zone_row, zone_col, *coefs)
        owner_inputs = (nodes, node_high, node_low, coef, table, meets, classes, matrices)
        tile_scratch = [
            pltpu.VMEM((64, 128), F32), pltpu.VMEM((128, 128), F32), pltpu.VMEM((64, 128), jnp.int32)
        ]
        owner_scratch = [pltpu.VMEM((64, 128), F32), pltpu.VMEM((64, 128), F32)]
        if last:
            (relay,) = call(relay_kernel, (got,), [shape(32, 128)])
            relay = swapped(relay, None, 0)
            (surface_out,) = call(
                functools.partial(tile_kernel, False, True), (got, *tile_inputs), [shape(64, 256)],
                tile_scratch,
            )
            (pipes_out,) = call(
                functools.partial(owner_kernel, False, True), (got, *owner_inputs, relay),
                [shape(32, 256)], owner_scratch,
            )
            return surface_out, pipes_out
        outputs = [shape(64, 384), shape(12 if first else 48, 128), shape(12, 128)]
        if first:
            outputs += [shape(64, 128), shape(128, 128)]
        surface, near, far, *new_coefs = call(
            functools.partial(tile_kernel, first, False), (got, *tile_inputs), outputs,
            tile_scratch,
        )
        near, far = swapped(near, far, 0, "far" if first else None)
        if not first:
            (inflow,) = call(
                inflow_kernel, (got, nodes, node_high, node_low, coef), [shape(64, 128)],
                owner_scratch[:1], flops=10**6,
            )
            owner_inputs += (near, inflow)
        table, nodes = call(
            functools.partial(owner_kernel, first, False), (got, *owner_inputs),
            [shape(64, 128), shape(64, 128)], owner_scratch,
        )
        if first:
            coefs = tuple(new_coefs)


def solution(mesh):
    placed = (
        P("row", "col"),
        P("row", "col"),
        P("row", "col"),
        P("row", "col"),
        P("row", "col"),
        P(None, ("row", "col")),
        P(("row", "col")),
        P(("row", "col")),
        P(("row", "col")),
        P(),
        P(("row", "col"), None, None),
        P(None, ("row", "col"), None),
        P(None, ("row", "col"), None),
    )
    return jax.shard_map(
        body,
        mesh=mesh,
        in_specs=placed,
        out_specs=(P("row", "col"), P(None, ("row", "col"))),
        check_vma=False,
    )
```

```python
import functools

import jax
import jax.numpy as jnp
from jax import lax
from jax.experimental import pallas as pl
from jax.experimental.pallas import tpu as pltpu
from jax.sharding import PartitionSpec as P

CLASSES = 4
SWEEPS = 4
STEPS = 3
F32 = jnp.float32
BF16 = jnp.bfloat16

boundary_gain = 0.5

HALO_ROWS = 4
HALO_COLS = 12
ZONE = 8
ENDS = (0, 32, 31, 63)


def iota(shape, dim):
    return lax.broadcasted_iota(jnp.int32, shape, dim)


def packed(x):
    return jnp.concatenate([x[:64], x[64:]], axis=1)


def low_halves(block):
    lane = iota((64, 128), 1)
    return jnp.where(lane < 64, block[:64], pltpu.roll(block[64:], 64, 1))


def high_halves(block):
    lane = iota((64, 128), 1)
    return jnp.where(lane < 64, pltpu.roll(block[:64], 64, 1), block[64:])


def paired(low, high):
    lane = iota((64, 128), 1)
    top = jnp.where(lane < 64, low, pltpu.roll(high, 64, 1))
    bottom = jnp.where(lane < 64, pltpu.roll(low, 64, 1), high)
    return jnp.concatenate([top, bottom], axis=0)


def beside(values):
    lane = iota((128, 128), 1)
    both = paired(values, values)
    return jnp.where(lane < 64, pltpu.roll(both, 1, 0), pltpu.roll(both, 127, 0))


def gathered(table_ref, rows, high, low):
    low = jnp.bitwise_and(low, 127)
    tiles = []
    for start in range(0, high.shape[0], 8):
        tile_high, tile_low = high[start : start + 8], low[start : start + 8]
        found = jnp.zeros((8, 128), F32)
        for row in range(rows):
            line = jnp.broadcast_to(table_ref[row : row + 1, :], (8, 128))
            values = jnp.take_along_axis(line, tile_low, axis=1)
            found = jnp.where(tile_high == row, values, found)
        tiles.append(found)
    return jnp.concatenate(tiles, axis=0) if len(tiles) > 1 else tiles[0]


def gathered_by_product(table, high_ref, low_ref, tiles):
    coarse = table.astype(BF16)
    fine = (table - coarse.astype(F32)).astype(BF16)
    parts = jnp.concatenate([coarse, fine], axis=1)
    row_iota = iota((128, 128), 0)
    high_iota = row_iota.astype(F32).astype(BF16)
    one, zero = jnp.ones((128, 128), BF16), jnp.zeros((128, 128), BF16)
    found = []
    for start in range(0, 8 * tiles, 8):
        high = high_ref[start : start + 8, :].astype(F32)
        low = low_ref[start : start + 8, :]
        hot = jnp.concatenate(
            [
                jnp.where(repeated(high[j : j + 1], 128) == high_iota, one, zero)
                for j in range(8)
            ],
            axis=1,
        )
        lines = lax.dot_general(
            parts, hot, (((0,), (0,)), ((), ())), preferred_element_type=F32
        )
        lines = lines[:128] + lines[128:]
        for j in range(8):
            line = jnp.where(
                row_iota == low[j : j + 1], lines[:, j * 128 : j * 128 + 128], 0.0
            )
            found.append(jnp.sum(line, axis=0, keepdims=True))
    return jnp.concatenate(found, axis=0)


def repeated(line, size):
    block = jnp.broadcast_to(line, (16, 128)).astype(BF16)
    return jnp.concatenate([block] * (size // 16), axis=0) if size > 16 else block


def summed(high_ref, low_ref, value_ref, high_size, low_size, by_low=False):
    refs, sizes = (high_ref, low_ref), (high_size, low_size)
    bearer = 1 if by_low else 0
    iotas = [iota((size, 128), 0).astype(F32).astype(BF16) for size in sizes]
    zeros = [jnp.zeros((size, 128), BF16) for size in sizes]
    one = jnp.ones((sizes[1 - bearer], 128), BF16)
    total = None
    for start in range(0, high_ref.shape[0], 8):
        places = [ref[start : start + 8, :].astype(F32) for ref in refs]
        value = value_ref[start : start + 8, :]
        coarse = value.astype(BF16).astype(F32)
        fine = value - coarse
        size, zero = sizes[bearer], zeros[bearer]
        coarse_hot, fine_hot, plain_hot = [], [], []
        for j in range(8):
            same = [
                repeated(places[side][j : j + 1], sizes[side]) == iotas[side] for side in range(2)
            ]
            coarse_hot.append(jnp.where(same[bearer], repeated(coarse[j : j + 1], size), zero))
            fine_hot.append(jnp.where(same[bearer], repeated(fine[j : j + 1], size), zero))
            plain_hot.append(jnp.where(same[1 - bearer], one, zeros[1 - bearer]))
        value_hot = jnp.concatenate(
            [jnp.concatenate(coarse_hot, axis=1), jnp.concatenate(fine_hot, axis=1)], axis=0
        )
        plain_hot = jnp.concatenate(plain_hot, axis=1)
        sides = (plain_hot, value_hot) if by_low else (value_hot, plain_hot)
        product = lax.dot_general(
            *sides, (((1,), (1,)), ((), ())), preferred_element_type=F32
        )
        total = product if total is None else total + product
    if by_low:
        return total[:, :low_size] + total[:, low_size:]
    return total[:high_size] + total[high_size:]


def summed_by_columns(row_ref, value_ref, hot_ref):
    row_iota = iota((64, 128), 0).astype(F32).astype(BF16)
    zero = jnp.zeros((64, 128), BF16)
    total = jnp.zeros((128, 256), F32)
    for start in range(0, 64, 8):
        rows = row_ref[start : start + 8, :].astype(F32)
        value = value_ref[start : start + 8, :]
        coarse = value.astype(BF16).astype(F32)
        fine = value - coarse
        coarse_hot, fine_hot = [], []
        for j in range(8):
            same = repeated(rows[j : j + 1], 64) == row_iota
            coarse_hot.append(jnp.where(same, repeated(coarse[j : j + 1], 64), zero))
            fine_hot.append(jnp.where(same, repeated(fine[j : j + 1], 64), zero))
        value_hot = jnp.concatenate(
            [jnp.concatenate(coarse_hot, axis=1), jnp.concatenate(fine_hot, axis=1)], axis=0
        )
        total = total + jnp.dot(
            value_hot, hot_ref[start * 128 : start * 128 + 1024, :], preferred_element_type=F32
        )
    return total[:64] + total[64:]


def columns_kernel(link_cell, hot):
    cols = jnp.bitwise_and(packed(link_cell[...]), 255).astype(F32).T
    lane = iota((128, 256), 1).astype(F32)
    for j in range(64):
        same = jnp.broadcast_to(cols[:, j : j + 1], (128, 256)) == lane
        hot[j * 128 : j * 128 + 128, :] = jnp.where(same, 1.0, 0.0).astype(BF16)


def cell_place(cell):
    high = jnp.where(
        cell >= 0, jnp.bitwise_and(cell >> 7, 1) * 64 + (cell >> 8), -1
    )
    return high, jnp.bitwise_and(cell, 127)


def node_place(node):
    high = jnp.where(
        node >= 0, jnp.bitwise_and(node >> 7, 1) * 32 + (node >> 8), -1
    )
    return high, jnp.bitwise_and(node, 127)


def pipe_table(state):
    return jnp.concatenate([state[:, :128], state[:, 128:]], axis=0)


def strips(blocks, start):
    return jnp.concatenate([block[start : start + HALO_ROWS] for block in blocks], axis=0)


def row_col():
    return lax.axis_index("row"), lax.axis_index("col")


def even(dim):
    return jnp.bitwise_and(row_col()[dim], 1) == 0


def start_kernel(
    surface, cond_x, cond_y, porosity, rainfall, pipes, fields, near, far, tips, arrived
):
    copies = [
        pltpu.make_async_copy(source, fields.at[index], arrived.at[index])
        for index, source in enumerate((surface, cond_x, cond_y, porosity, rainfall))
    ]
    copies.append(pltpu.make_async_copy(pipes.at[24:32, :], tips, arrived.at[5]))
    for copy in copies:
        copy.start()
    for copy in copies:
        copy.wait()
    fields[3] = 1.0 / fields[3]
    for index in range(5):
        halves = [fields[index, :, 0:128], fields[index, :, 128:256]]
        top, bottom = strips(halves, 0), strips(halves, 60)
        near[pl.ds(index * 8, 8), :] = jnp.where(even(0), bottom, top)
        far[pl.ds(index * 8, 8), :] = jnp.where(even(0), top, bottom)
    near[40:48, :] = jnp.concatenate(
        [tips[7:8, 0:128], tips[7:8, 128:256], jnp.zeros((6, 128), F32)], axis=0
    )


def tall_block(block, near, far, start):
    near, far = near[start : start + 4, :], far[start : start + 4, :]
    over = jnp.where(even(0), far, near)
    under = jnp.where(even(0), near, far)
    over = jnp.where(row_col()[0] > 0, over, 0.0)
    under = jnp.where(row_col()[0] < 7, under, 0.0)
    return jnp.concatenate([block, under, over], axis=0)


def pack_cols_kernel(near, far, fields, link_cell, tall_out, out):
    lane = iota((72, 128), 1)
    message = jnp.zeros((72, 128), F32)
    for index in range(5):
        tall = [
            tall_block(
                fields[index, :, half * 128 : half * 128 + 128], near, far,
                index * 8 + half * 4,
            )
            for half in range(2)
        ]
        tall_out[index, :, 0:128] = tall[0]
        tall_out[index, :, 128:256] = tall[1]
        edges = jnp.where(
            lane < HALO_COLS, tall[0], jnp.where(lane >= 128 - HALO_COLS, tall[1], 0.0)
        )
        if index:
            edges = pltpu.roll(edges, index * 2 * HALO_COLS, 1)
        message = message + edges
    out[0:72, :] = message
    out[72:136, :] = packed(link_cell[...]).astype(F32)


def owner_start_kernel(
    pipes, link_node, link_coef, kinds, laws, uppers, lowers, table, nodes, node_high, node_low,
    coef, classes, matrices, meets,
):
    meets[...] = jnp.concatenate(
        [uppers[...], lowers[...], jnp.zeros((4, 128), jnp.int32)], axis=0
    )
    classes[...] = kinds[...]
    matrices[...] = laws[...]
    table[...] = pipe_table(pipes[...])
    high, low = node_place(packed(link_node[...]))
    node_high[...] = high
    node_low[...] = low
    coef[...] = packed(link_coef[...])
    nodes[...] = gathered(table, 64, high, low)


def swept(state, gains):
    def once(_, w):
        return (
            gains[0] * w
            + gains[1] * pltpu.roll(w, 1, 0)
            + gains[2] * pltpu.roll(w, 71, 0)
            + gains[3] * pltpu.roll(w, 1, 1)
            + gains[4] * pltpu.roll(w, 383, 1)
            + gains[5]
        )

    for i in range(SWEEPS):
        state = once(i, state)
    return state


def put(out, blocks, index, value):
    out[pl.ds(index, 128, stride=blocks), :] = value


def taken(got, blocks, index):
    return got[pl.ds(index, 128, stride=blocks), :]


def build_rest(out, blocks, nodes, own_ends, other_ends):
    own_rows = (iota((128, 128), 0) >> 4) == row_col()[0]
    for half in range(2):
        own = jnp.broadcast_to(own_ends[half], (128, 128))
        other = jnp.broadcast_to(other_ends[half], (128, 128))
        put(out, blocks, 1 + half, jnp.where(own_rows, own, other))
    if blocks > 3:
        put(out, blocks, blocks - 1, beside(nodes))


def build_message(out, blocks, heads, nodes, own_ends, other_ends):
    put(out, blocks, 0, paired(heads, nodes))
    build_rest(out, blocks, nodes, own_ends, other_ends)


def partner_rows(blocks):
    return pl.multiple_of((row_col()[0] ^ 1) * (16 * blocks), 16)


def zone_heads(edge, zone_place, edge_ref, zone_ref):
    lane = iota((64, 128), 1)
    edge_ref[...] = jnp.where(lane < ZONE, edge, pltpu.roll(edge, 2 * ZONE, 1))
    lane8 = iota((8, 128), 1)
    table = jnp.zeros((8, 128), F32)
    for s in range(8):
        line = edge_ref[pl.ds(s, 8, stride=8), :]
        if s:
            line = pltpu.roll(line, s * 16, 1)
        table = jnp.where((lane8 >> 4) == s, line, table)
    zone_ref[...] = table
    zone_row, zone_col = zone_place
    high = jnp.where(zone_row >= 0, zone_row >> 3, -1)
    low = jnp.bitwise_and(zone_row, 7) * 16 + zone_col
    return gathered(zone_ref, 8, high, low)


def sweep_and_gather(
    state, gains, cell_high, cell_low, zone_place, surface_out, heads_out, zone_out, cell_table,
    edge_ref, zone_ref,
):
    state = swept(state, gains)
    surface_out[...] = state[:64]
    cell_table[0:64, :] = state[:64, 0:128]
    cell_table[64:128, :] = state[:64, 128:256]
    heads = jnp.concatenate(
        [
            gathered_by_product(cell_table[...], cell_high, cell_low, 4),
            gathered(cell_table, 128, cell_high[32:64, :], cell_low[32:64, :]),
        ],
        axis=0,
    )
    heads_out[...] = heads
    if zone_place is not None:
        zone_out[...] = zone_heads(state[:64, 256:384], zone_place, edge_ref, zone_ref)
    return heads


def first_sweep_kernel(
    tall, near_col, far_col, near, link_cell, table, nodes, coef,
    gains_out, inverse_out, cell_high, cell_low, zone_row_out, zone_col_out, surface_out, heads_out,
    zone_out, out, cell_table, edge_ref, zone_ref,
):
    lane = iota((72, 128), 1)
    wide = []
    from_west = jnp.where(even(1), far_col[...], near_col[...])
    from_east = jnp.where(even(1), near_col[...], far_col[...])
    for index in range(5):
        west = jnp.where(row_col()[1] > 0, from_west[0:72, :], 0.0)
        east = jnp.where(row_col()[1] < 15, from_east[0:72, :], 0.0)
        if index:
            west = pltpu.roll(west, 128 - index * 2 * HALO_COLS, 1)
            east = pltpu.roll(east, 128 - index * 2 * HALO_COLS, 1)
        edge = jnp.where(
            lane < HALO_COLS, east, jnp.where(lane >= 128 - HALO_COLS, west, 0.0)
        )
        wide.append(jnp.concatenate([tall[index], edge], axis=1))
    state, cond_x, cond_y, inverse, rainfall = wide
    north = pltpu.roll(cond_x, 1, 0)
    west = pltpu.roll(cond_y, 1, 1)
    gains = [
        1.0 - (north + cond_x + west + cond_y) * inverse,
        north * inverse, cond_x * inverse, west * inverse, cond_y * inverse, rainfall,
    ]
    for index, gain in enumerate(gains):
        gains_out[index] = gain
    inverse_out[...] = inverse[:64]
    cells = paired(from_west[72:136, :], from_east[72:136, :]).astype(jnp.int32)
    col = jnp.bitwise_and(cells, 255)
    is_west = iota((128, 128), 1) < 64
    zone_col = jnp.where(is_west, col - (256 - 2 * ZONE), col)
    inside = (zone_col >= 0) & (zone_col < 2 * ZONE)
    inside = inside & (jnp.where(is_west, zone_col, zone_col + ZONE) >= ZONE)
    zone_row = jnp.where((cells >= 0) & inside & (jnp.where(is_west, 0, zone_col) < ZONE), cells >> 8, -1)
    zone_row_out[...] = zone_row
    zone_col_out[...] = zone_col
    high, low = cell_place(packed(link_cell[...]))
    cell_high[...] = high
    cell_low[...] = low
    heads = sweep_and_gather(
        state, gains, cell_high, cell_low, (zone_row, zone_col), surface_out, heads_out, zone_out,
        cell_table, edge_ref, zone_ref,
    )
    build_message(
        out, 6, heads, nodes[...], (table[0:1, :], table[32:33, :]), (near[40:41, :], near[41:42, :])
    )
    put(out, 6, 3, paired(coef[...], coef[...]))
    put(out, 6, 4, beside(coef[...]))


def sweep_kernel(
    last, surface, near, far, gains_ref, cell_high, cell_low, zone_row, zone_col,
    message, nodes, surface_out, heads_out, zone_out, out, cell_table, edge_ref, zone_ref,
):
    state = jnp.concatenate(
        [
            tall_block(
                surface[:, block * 128 : block * 128 + 128], near, far, block * 4
            )
            for block in range(3)
        ],
        axis=1,
    )
    gains = [gains_ref[index] for index in range(6)]
    zone_place = None if last else (zone_row[...], zone_col[...])
    heads = sweep_and_gather(
        state, gains, cell_high, cell_low, zone_place, surface_out, heads_out, zone_out,
        cell_table, edge_ref, zone_ref,
    )
    put(out, 3 if last else 4, 0, paired(heads, nodes[...]))


def relayed(got, blocks):
    return jnp.concatenate(
        [got[pl.ds(partner_rows(blocks) + block, 16, stride=blocks), :] for block in (1, 2)], axis=0
    )


def relay_kernel(got, out):
    out[...] = relayed(got, 3)


def tile_kernel(
    first, last, got, surface, inverse, heads, zone, cell_high, hot, zone_row, zone_col, *rest
):
    rest = list(rest)
    blocks = 6 if first else 3 if last else 4
    if first:
        own_coef = low_halves(taken(got, 6, 3))
        zone_coef = taken(got, 6, 4)
    else:
        own_coef = rest.pop(0)[...]
        zone_coef = rest.pop(0)[...]
    surface_out = rest.pop(0)
    if not last:
        near, far = rest.pop(0), rest.pop(0)
    if first:
        rest.pop(0)[...] = own_coef
        rest.pop(0)[...] = zone_coef
    value_ref, zone_value_ref, row_ref = rest
    value_ref[...] = jnp.where(
        cell_high[...] >= 0, own_coef * (heads[...] - high_halves(taken(got, blocks, 0))), 0.0
    )
    row_ref[...] = jnp.where(cell_high[...] >= 0, jnp.bitwise_and(cell_high[...], 63), -1)
    lost = summed_by_columns(row_ref, value_ref, hot)
    left = surface[:, 0:128] - inverse[:, 0:128] * lost[:, 0:128]
    right = surface[:, 128:256] - inverse[:, 128:256] * lost[:, 128:256]
    surface_out[:, 0:128] = left
    surface_out[:, 128:256] = right
    if last:
        return
    zone_value_ref[...] = jnp.where(
        zone_row[...] >= 0, zone_coef * (zone[...] - taken(got, blocks, blocks - 1)), 0.0
    )
    lost = summed(zone_row, zone_col, zone_value_ref, 64, 2 * ZONE, by_low=True)
    lost = jnp.concatenate([lost, jnp.zeros((64, 128 - 2 * ZONE), F32)], axis=1)
    lane = iota((64, 128), 1)
    lost = jnp.where(
        lane < ZONE, lost,
        jnp.where(lane >= 128 - ZONE, pltpu.roll(lost, 128 - 2 * ZONE, 1), 0.0),
    )
    edge = surface[:, 256:384] - inverse[:, 256:384] * lost
    surface_out[:, 256:384] = edge
    top, bottom = strips([left, right, edge], 0), strips([left, right, edge], 60)
    near[0:12, :] = jnp.where(even(0), bottom, top)
    far[...] = jnp.where(even(0), top, bottom)
    if not first:
        near[16:48, :] = relayed(got, blocks)


def inflow_of(blocks, got, nodes, node_high, node_low, coef, value_ref):
    value_ref[...] = jnp.where(
        node_high[...] >= 0, coef[...] * (low_halves(taken(got, blocks, 0)) - nodes[...]), 0.0
    )
    return summed(node_high, node_low, value_ref, 64, 128)


def inflow_kernel(got, nodes, node_high, node_low, coef, out, value_ref):
    out[...] = inflow_of(4, got, nodes, node_high, node_low, coef, value_ref)


def owner_kernel(
    first, last, got, nodes, node_high, node_low, coef, table, meets, classes, matrices, *rest
):
    blocks = 6 if first else 3 if last else 4
    rest = list(rest)
    relay = None if first else rest.pop(0)
    inflow = None if first or last else rest.pop(0)[...]
    if last:
        pipes_out, value_ref, ends_ref = rest
    else:
        table_out, nodes_out, out, value_ref, ends_ref = rest
    if inflow is None:
        inflow = inflow_of(blocks, got, nodes, node_high, node_low, coef, value_ref)
    balance = table[...] + inflow
    start = pl.multiple_of(row_col()[0] * (16 * blocks), 16)
    for half in range(2):
        ends_ref[half * 16 : half * 16 + 16, :] = got[
            pl.ds(start + 1 + half, 16, stride=blocks), :
        ]
    if first:
        ends_ref[32:64, :] = relayed(got, blocks)
    else:
        ends_ref[32:64, :] = relay[0:32, :] if last else relay[16:48, :]
    meet = meets[...]
    meet_high = jnp.bitwise_and(meet >> 7, 1) * 16 + (meet >> 8)
    meet_high = jnp.where(iota((8, 128), 0) < 2, meet_high + 32, meet_high)
    met = gathered(ends_ref, 64, meet_high, meet) * boundary_gain
    node_row = iota((32, 128), 0)
    parts = []
    for half in range(2):
        part = balance[half * 32 : half * 32 + 32]
        part = part + jnp.where(
            node_row == 0, met[half : half + 1],
            jnp.where(node_row == 31, met[2 + half : 3 + half], 0.0),
        )
        products = jnp.dot(
            matrices[...], part, precision=lax.Precision.HIGHEST, preferred_element_type=F32
        )
        kind = classes[half : half + 1, :]
        updated = jnp.zeros((32, 128), F32)
        for index in range(CLASSES):
            updated = jnp.where(kind == index, products[index * 32 : index * 32 + 32], updated)
        parts.append(updated)
    if last:
        pipes_out[:, 0:128] = parts[0]
        pipes_out[:, 128:256] = parts[1]
        return
    table_out[0:32, :] = parts[0]
    table_out[32:64, :] = parts[1]
    heads = gathered(table_out, 64, node_high[...], node_low[...])
    nodes_out[...] = heads
    build_rest(
        out, 4 if first else 3, heads, (parts[0][0:1], parts[1][0:1]),
        (parts[0][31:32], parts[1][31:32]),
    )


def shape(*dims, dtype=F32):
    return jax.ShapeDtypeStruct(dims, dtype)


def call(kernel, inputs, outputs, scratch=(), space=pltpu.VMEM, flops=10**9, aliases=()):
    vmem = pl.BlockSpec(memory_space=pltpu.VMEM)
    return pl.pallas_call(
        kernel,
        out_shape=outputs,
        in_specs=[pl.BlockSpec(memory_space=space)] * len(inputs),
        out_specs=[vmem] * len(outputs),
        scratch_shapes=list(scratch),
        input_output_aliases=dict(aliases),
        compiler_params=pltpu.CompilerParams(vmem_limit_bytes=16 << 20),
        cost_estimate=pl.CostEstimate(flops=flops, bytes_accessed=1 << 20, transcendentals=0),
    )(*inputs)


def copy_kernel(source, out):
    out[...] = source[...]


def swapped(near, far, dim, copied=None):
    sizes = lax.axis_size("row"), lax.axis_size("col")
    routes = [], []
    for row in range(sizes[0]):
        for col in range(sizes[1]):
            here = [row, col]
            partner = list(here)
            partner[dim] ^= 1
            other = list(here)
            other[dim] += 1 if here[dim] % 2 else -1
            if not 0 <= other[dim] < sizes[dim]:
                other = list(here)
                other[1 - dim] ^= 1
            for route, there in zip(routes, (partner, other)):
                route.append((row * sizes[1] + col, there[0] * sizes[1] + there[1]))
    if far is None:
        return lax.ppermute(near, ("row", "col"), routes[0])
    if copied == "near":
        (near,) = call(copy_kernel, (near,), [shape(*near.shape)])
    if copied == "far":
        (far,) = call(copy_kernel, (far,), [shape(*far.shape)])
    far = lax.ppermute(far, ("row", "col"), routes[1])
    return lax.ppermute(near, ("row", "col"), routes[0]), far


def body(
    surface_head, conduct_x, conduct_y, porosity, rainfall, pipe_head, pipe_class, pipe_up,
    pipe_down, pipe_matrices, link_cell, link_node, link_coef,
):
    link_cell = link_cell[0]
    uppers, lowers = pipe_up.reshape(2, 128), pipe_down.reshape(2, 128)
    classes = pipe_class.reshape(2, 128)
    matrices = pipe_matrices.reshape(CLASSES * 32, 32)
    ints = functools.partial(shape, dtype=jnp.int32)

    fields, near, far = call(
        start_kernel,
        [pltpu.with_memory_space_constraint(x, pltpu.HBM) for x in (
            surface_head, conduct_x, conduct_y, porosity, rainfall, pipe_head
        )],
        [shape(5, 64, 256), shape(48, 128), shape(40, 128)],
        [pltpu.VMEM((8, 256), F32), pltpu.SemaphoreType.DMA((6,))], space=pltpu.HBM,
    )
    near, far = swapped(near, far, 0, "near")
    link_node = link_node[:, 0, :]
    link_coef = link_coef[:, 0, :]
    table, nodes, node_high, node_low, coef, classes, matrices, meets = call(
        owner_start_kernel, (pipe_head, link_node, link_coef, classes, matrices, uppers, lowers),
        [shape(64, 128), shape(64, 128), ints(64, 128), ints(64, 128), shape(64, 128),
         ints(2, 128), shape(128, 32), ints(8, 128)],
    )
    near, far, nodes = lax.optimization_barrier((near, far, nodes))
    tall, sent = call(
        pack_cols_kernel, (near, far, fields, link_cell),
        [shape(5, 72, 256), shape(136, 128)],
    )
    sent, cells = lax.optimization_barrier((sent, link_cell))
    near_col, far_col = swapped(sent, sent, 1)
    (hot,) = call(columns_kernel, (cells,), [shape(8192, 256, dtype=BF16)])
    gather_scratch = [
        pltpu.VMEM((128, 128), F32), pltpu.VMEM((64, 128), F32), pltpu.VMEM((8, 128), F32)
    ]
    swept_shapes = [shape(64, 384), shape(64, 128), shape(128, 128)]
    (gains, inverse, cell_high, cell_low, zone_row, zone_col, surface, heads, zone, sent) = call(
        first_sweep_kernel,
        (tall, near_col, far_col, near, link_cell, table, nodes, coef),
        [shape(6, 72, 384), shape(64, 384), ints(64, 128), ints(64, 128), ints(128, 128),
         ints(128, 128), *swept_shapes, shape(768, 128)],
        gather_scratch,
    )
    sent, hot = lax.optimization_barrier((sent, hot))
    coefs = ()
    for step in range(STEPS):
        first, last = step == 0, step == STEPS - 1
        if step:
            surface, heads, zone, sent = call(
                functools.partial(sweep_kernel, last),
                (surface, near, far, gains, cell_high, cell_low, zone_row, zone_col,
                 sent, nodes),
                [*swept_shapes, shape(384 if last else 512, 128)], gather_scratch, aliases={8: 3},
            )
        got = lax.all_to_all(
            sent.reshape(128, 1, -1), ("row", "col"), split_axis=0, concat_axis=0, tiled=True
        ).reshape(-1, 128)
        tile_inputs = (surface, inverse, heads, zone, cell_high, hot, zone_row, zone_col, *coefs)
        owner_inputs = (nodes, node_high, node_low, coef, table, meets, classes, matrices)
        tile_scratch = [
            pltpu.VMEM((64, 128), F32), pltpu.VMEM((128, 128), F32), pltpu.VMEM((64, 128), jnp.int32)
        ]
        owner_scratch = [pltpu.VMEM((64, 128), F32), pltpu.VMEM((64, 128), F32)]
        if last:
            (relay,) = call(relay_kernel, (got,), [shape(32, 128)])
            relay = swapped(relay, None, 0)
            (surface_out,) = call(
                functools.partial(tile_kernel, False, True), (got, *tile_inputs), [shape(64, 256)],
                tile_scratch,
            )
            (pipes_out,) = call(
                functools.partial(owner_kernel, False, True), (got, *owner_inputs, relay),
                [shape(32, 256)], owner_scratch,
            )
            return surface_out, pipes_out
        outputs = [shape(64, 384), shape(12 if first else 48, 128), shape(12, 128)]
        if first:
            outputs += [shape(64, 128), shape(128, 128)]
        surface, near, far, *new_coefs = call(
            functools.partial(tile_kernel, first, False), (got, *tile_inputs), outputs,
            tile_scratch,
        )
        near, far = swapped(near, far, 0, "far" if first else None)
        if not first:
            (inflow,) = call(
                inflow_kernel, (got, nodes, node_high, node_low, coef), [shape(64, 128)],
                owner_scratch[:1], flops=10**6,
            )
            owner_inputs += (near, inflow)
        table, nodes, sent = call(
            functools.partial(owner_kernel, first, False), (got, *owner_inputs),
            [shape(64, 128), shape(64, 128), shape(512 if first else 384, 128)], owner_scratch,
        )
        if first:
            coefs = tuple(new_coefs)


def solution(mesh):
    placed = (
        P("row", "col"),
        P("row", "col"),
        P("row", "col"),
        P("row", "col"),
        P("row", "col"),
        P(None, ("row", "col")),
        P(("row", "col")),
        P(("row", "col")),
        P(("row", "col")),
        P(),
        P(("row", "col"), None, None),
        P(None, ("row", "col"), None),
        P(None, ("row", "col"), None),
    )
    return jax.shard_map(
        body,
        mesh=mesh,
        in_specs=placed,
        out_specs=(P("row", "col"), P(None, ("row", "col"))),
        check_vma=False,
    )
```

```python
import functools

import jax
import jax.numpy as jnp
from jax import lax
from jax.experimental import pallas as pl
from jax.experimental.pallas import tpu as pltpu
from jax.sharding import PartitionSpec as P

CLASSES = 4
SWEEPS = 4
STEPS = 3
F32 = jnp.float32
BF16 = jnp.bfloat16

boundary_gain = 0.5

HALO_ROWS = 4
HALO_COLS = 12
ZONE = 8
ENDS = (0, 32, 31, 63)


def iota(shape, dim):
    return lax.broadcasted_iota(jnp.int32, shape, dim)


def packed(x):
    return jnp.concatenate([x[:64], x[64:]], axis=1)


def low_halves(block):
    lane = iota((64, 128), 1)
    return jnp.where(lane < 64, block[:64], pltpu.roll(block[64:], 64, 1))


def high_halves(block):
    lane = iota((64, 128), 1)
    return jnp.where(lane < 64, pltpu.roll(block[:64], 64, 1), block[64:])


def paired(low, high):
    lane = iota((64, 128), 1)
    top = jnp.where(lane < 64, low, pltpu.roll(high, 64, 1))
    bottom = jnp.where(lane < 64, pltpu.roll(low, 64, 1), high)
    return jnp.concatenate([top, bottom], axis=0)


def beside(values):
    lane = iota((128, 128), 1)
    both = paired(values, values)
    return jnp.where(lane < 64, pltpu.roll(both, 1, 0), pltpu.roll(both, 127, 0))


def gathered(table_ref, rows, high, low):
    low = jnp.bitwise_and(low, 127)
    tiles = []
    for start in range(0, high.shape[0], 8):
        tile_high, tile_low = high[start : start + 8], low[start : start + 8]
        found = jnp.zeros((8, 128), F32)
        for row in range(rows):
            line = jnp.broadcast_to(table_ref[row : row + 1, :], (8, 128))
            values = jnp.take_along_axis(line, tile_low, axis=1)
            found = jnp.where(tile_high == row, values, found)
        tiles.append(found)
    return jnp.concatenate(tiles, axis=0) if len(tiles) > 1 else tiles[0]


def gathered_by_product(table, high_ref, low_ref, tiles):
    coarse = table.astype(BF16)
    fine = (table - coarse.astype(F32)).astype(BF16)
    parts = jnp.concatenate([coarse, fine], axis=1)
    row_iota = iota((128, 128), 0)
    high_iota = row_iota.astype(F32).astype(BF16)
    one, zero = jnp.ones((128, 128), BF16), jnp.zeros((128, 128), BF16)
    found = []
    for start in range(0, 8 * tiles, 8):
        high = high_ref[start : start + 8, :].astype(F32)
        low = low_ref[start : start + 8, :]
        hot = jnp.concatenate(
            [
                jnp.where(repeated(high[j : j + 1], 128) == high_iota, one, zero)
                for j in range(8)
            ],
            axis=1,
        )
        lines = lax.dot_general(
            parts, hot, (((0,), (0,)), ((), ())), preferred_element_type=F32
        )
        lines = lines[:128] + lines[128:]
        for j in range(8):
            line = jnp.where(
                row_iota == low[j : j + 1], lines[:, j * 128 : j * 128 + 128], 0.0
            )
            found.append(jnp.sum(line, axis=0, keepdims=True))
    return jnp.concatenate(found, axis=0)


def repeated(line, size):
    block = jnp.broadcast_to(line, (16, 128)).astype(BF16)
    return jnp.concatenate([block] * (size // 16), axis=0) if size > 16 else block


def summed(high_ref, low_ref, value_ref, high_size, low_size, by_low=False):
    refs, sizes = (high_ref, low_ref), (high_size, low_size)
    bearer = 1 if by_low else 0
    iotas = [iota((size, 128), 0).astype(F32).astype(BF16) for size in sizes]
    zeros = [jnp.zeros((size, 128), BF16) for size in sizes]
    one = jnp.ones((sizes[1 - bearer], 128), BF16)
    total = None
    for start in range(0, high_ref.shape[0], 8):
        places = [ref[start : start + 8, :].astype(F32) for ref in refs]
        value = value_ref[start : start + 8, :]
        coarse = value.astype(BF16).astype(F32)
        fine = value - coarse
        size, zero = sizes[bearer], zeros[bearer]
        coarse_hot, fine_hot, plain_hot = [], [], []
        for j in range(8):
            same = [
                repeated(places[side][j : j + 1], sizes[side]) == iotas[side] for side in range(2)
            ]
            coarse_hot.append(jnp.where(same[bearer], repeated(coarse[j : j + 1], size), zero))
            fine_hot.append(jnp.where(same[bearer], repeated(fine[j : j + 1], size), zero))
            plain_hot.append(jnp.where(same[1 - bearer], one, zeros[1 - bearer]))
        value_hot = jnp.concatenate(
            [jnp.concatenate(coarse_hot, axis=1), jnp.concatenate(fine_hot, axis=1)], axis=0
        )
        plain_hot = jnp.concatenate(plain_hot, axis=1)
        sides = (plain_hot, value_hot) if by_low else (value_hot, plain_hot)
        product = lax.dot_general(
            *sides, (((1,), (1,)), ((), ())), preferred_element_type=F32
        )
        total = product if total is None else total + product
    if by_low:
        return total[:, :low_size] + total[:, low_size:]
    return total[:high_size] + total[high_size:]


def summed_by_columns(row_ref, value_ref, hot_ref):
    row_iota = iota((64, 128), 0).astype(F32).astype(BF16)
    zero = jnp.zeros((64, 128), BF16)
    total = jnp.zeros((128, 256), F32)
    for start in range(0, 64, 8):
        rows = row_ref[start : start + 8, :].astype(F32)
        value = value_ref[start : start + 8, :]
        coarse = value.astype(BF16).astype(F32)
        fine = value - coarse
        coarse_hot, fine_hot = [], []
        for j in range(8):
            same = repeated(rows[j : j + 1], 64) == row_iota
            coarse_hot.append(jnp.where(same, repeated(coarse[j : j + 1], 64), zero))
            fine_hot.append(jnp.where(same, repeated(fine[j : j + 1], 64), zero))
        value_hot = jnp.concatenate(
            [jnp.concatenate(coarse_hot, axis=1), jnp.concatenate(fine_hot, axis=1)], axis=0
        )
        total = total + jnp.dot(
            value_hot, hot_ref[start * 128 : start * 128 + 1024, :], preferred_element_type=F32
        )
    return total[:64] + total[64:]


def columns_kernel(link_cell, hot):
    cols = jnp.bitwise_and(packed(link_cell[...]), 255).astype(F32).T
    lane = iota((128, 256), 1).astype(F32)
    for j in range(64):
        same = jnp.broadcast_to(cols[:, j : j + 1], (128, 256)) == lane
        hot[j * 128 : j * 128 + 128, :] = jnp.where(same, 1.0, 0.0).astype(BF16)


def cell_place(cell):
    high = jnp.where(
        cell >= 0, jnp.bitwise_and(cell >> 7, 1) * 64 + (cell >> 8), -1
    )
    return high, jnp.bitwise_and(cell, 127)


def node_place(node):
    high = jnp.where(
        node >= 0, jnp.bitwise_and(node >> 7, 1) * 32 + (node >> 8), -1
    )
    return high, jnp.bitwise_and(node, 127)


def pipe_table(state):
    return jnp.concatenate([state[:, :128], state[:, 128:]], axis=0)


def strips(blocks, start):
    return jnp.concatenate([block[start : start + HALO_ROWS] for block in blocks], axis=0)


def row_col():
    return lax.axis_index("row"), lax.axis_index("col")


def even(dim):
    return jnp.bitwise_and(row_col()[dim], 1) == 0


def start_kernel(
    surface, cond_x, cond_y, porosity, rainfall, pipes, fields, near, far, tips, arrived
):
    copies = [
        pltpu.make_async_copy(source, fields.at[index], arrived.at[index])
        for index, source in enumerate((surface, cond_x, cond_y, porosity, rainfall))
    ]
    copies.append(pltpu.make_async_copy(pipes.at[24:32, :], tips, arrived.at[5]))
    for copy in copies:
        copy.start()
    for copy in copies:
        copy.wait()
    fields[3] = 1.0 / fields[3]
    for index in range(5):
        halves = [fields[index, :, 0:128], fields[index, :, 128:256]]
        top, bottom = strips(halves, 0), strips(halves, 60)
        near[pl.ds(index * 8, 8), :] = jnp.where(even(0), bottom, top)
        far[pl.ds(index * 8, 8), :] = jnp.where(even(0), top, bottom)
    near[40:48, :] = jnp.concatenate(
        [tips[7:8, 0:128], tips[7:8, 128:256], jnp.zeros((6, 128), F32)], axis=0
    )


def tall_block(block, near, far, start):
    near, far = near[start : start + 4, :], far[start : start + 4, :]
    over = jnp.where(even(0), far, near)
    under = jnp.where(even(0), near, far)
    over = jnp.where(row_col()[0] > 0, over, 0.0)
    under = jnp.where(row_col()[0] < 7, under, 0.0)
    return jnp.concatenate([block, under, over], axis=0)


def pack_cols_kernel(near, far, fields, link_cell, tall_out, out):
    lane = iota((72, 128), 1)
    message = jnp.zeros((72, 128), F32)
    for index in range(5):
        tall = [
            tall_block(
                fields[index, :, half * 128 : half * 128 + 128], near, far,
                index * 8 + half * 4,
            )
            for half in range(2)
        ]
        tall_out[index, :, 0:128] = tall[0]
        tall_out[index, :, 128:256] = tall[1]
        edges = jnp.where(
            lane < HALO_COLS, tall[0], jnp.where(lane >= 128 - HALO_COLS, tall[1], 0.0)
        )
        if index:
            edges = pltpu.roll(edges, index * 2 * HALO_COLS, 1)
        message = message + edges
    out[0:72, :] = message
    out[72:136, :] = packed(link_cell[...]).astype(F32)


def owner_start_kernel(
    pipes, link_node, link_coef, kinds, laws, uppers, lowers, table, nodes, node_high, node_low,
    coef, classes, matrices, meets,
):
    meets[...] = jnp.concatenate(
        [uppers[...], lowers[...], jnp.zeros((4, 128), jnp.int32)], axis=0
    )
    classes[...] = kinds[...]
    matrices[...] = laws[...]
    table[...] = pipe_table(pipes[...])
    high, low = node_place(packed(link_node[...]))
    node_high[...] = high
    node_low[...] = low
    coef[...] = packed(link_coef[...])
    nodes[...] = gathered(table, 64, high, low)


def swept(state, gains):
    def once(_, w):
        return (
            gains[0] * w
            + gains[1] * pltpu.roll(w, 1, 0)
            + gains[2] * pltpu.roll(w, 71, 0)
            + gains[3] * pltpu.roll(w, 1, 1)
            + gains[4] * pltpu.roll(w, 383, 1)
            + gains[5]
        )

    for i in range(SWEEPS):
        state = once(i, state)
    return state


def put(out, blocks, index, value):
    out[pl.ds(index, 128, stride=blocks), :] = value


def taken(got, blocks, index):
    return got[pl.ds(index, 128, stride=blocks), :]


def build_message(out, blocks, heads, nodes, own_ends, other_ends):
    put(out, blocks, 0, paired(heads, nodes))
    own_rows = (iota((128, 128), 0) >> 4) == row_col()[0]
    for half in range(2):
        own = jnp.broadcast_to(own_ends[half], (128, 128))
        other = jnp.broadcast_to(other_ends[half], (128, 128))
        put(out, blocks, 1 + half, jnp.where(own_rows, own, other))
    if blocks > 3:
        put(out, blocks, blocks - 1, beside(nodes))


def partner_rows(blocks):
    return pl.multiple_of((row_col()[0] ^ 1) * (16 * blocks), 16)


def zone_heads(edge, zone_place, edge_ref, zone_ref):
    lane = iota((64, 128), 1)
    edge_ref[...] = jnp.where(lane < ZONE, edge, pltpu.roll(edge, 2 * ZONE, 1))
    lane8 = iota((8, 128), 1)
    table = jnp.zeros((8, 128), F32)
    for s in range(8):
        line = edge_ref[pl.ds(s, 8, stride=8), :]
        if s:
            line = pltpu.roll(line, s * 16, 1)
        table = jnp.where((lane8 >> 4) == s, line, table)
    zone_ref[...] = table
    zone_row, zone_col = zone_place
    high = jnp.where(zone_row >= 0, zone_row >> 3, -1)
    low = jnp.bitwise_and(zone_row, 7) * 16 + zone_col
    return gathered(zone_ref, 8, high, low)


def sweep_and_gather(
    state, gains, cell_high, cell_low, zone_place, surface_out, heads_out, zone_out, cell_table,
    edge_ref, zone_ref,
):
    state = swept(state, gains)
    surface_out[...] = state[:64]
    cell_table[0:64, :] = state[:64, 0:128]
    cell_table[64:128, :] = state[:64, 128:256]
    heads = jnp.concatenate(
        [
            gathered_by_product(cell_table[...], cell_high, cell_low, 4),
            gathered(cell_table, 128, cell_high[32:64, :], cell_low[32:64, :]),
        ],
        axis=0,
    )
    heads_out[...] = heads
    if zone_place is not None:
        zone_out[...] = zone_heads(state[:64, 256:384], zone_place, edge_ref, zone_ref)
    return heads


def first_sweep_kernel(
    tall, near_col, far_col, near, link_cell, table, nodes, coef,
    gains_out, inverse_out, cell_high, cell_low, zone_row_out, zone_col_out, surface_out, heads_out,
    zone_out, out, cell_table, edge_ref, zone_ref,
):
    lane = iota((72, 128), 1)
    wide = []
    from_west = jnp.where(even(1), far_col[...], near_col[...])
    from_east = jnp.where(even(1), near_col[...], far_col[...])
    for index in range(5):
        west = jnp.where(row_col()[1] > 0, from_west[0:72, :], 0.0)
        east = jnp.where(row_col()[1] < 15, from_east[0:72, :], 0.0)
        if index:
            west = pltpu.roll(west, 128 - index * 2 * HALO_COLS, 1)
            east = pltpu.roll(east, 128 - index * 2 * HALO_COLS, 1)
        edge = jnp.where(
            lane < HALO_COLS, east, jnp.where(lane >= 128 - HALO_COLS, west, 0.0)
        )
        wide.append(jnp.concatenate([tall[index], edge], axis=1))
    state, cond_x, cond_y, inverse, rainfall = wide
    north = pltpu.roll(cond_x, 1, 0)
    west = pltpu.roll(cond_y, 1, 1)
    gains = [
        1.0 - (north + cond_x + west + cond_y) * inverse,
        north * inverse, cond_x * inverse, west * inverse, cond_y * inverse, rainfall,
    ]
    for index, gain in enumerate(gains):
        gains_out[index] = gain
    inverse_out[...] = inverse[:64]
    cells = paired(from_west[72:136, :], from_east[72:136, :]).astype(jnp.int32)
    col = jnp.bitwise_and(cells, 255)
    is_west = iota((128, 128), 1) < 64
    zone_col = jnp.where(is_west, col - (256 - 2 * ZONE), col)
    inside = (zone_col >= 0) & (zone_col < 2 * ZONE)
    inside = inside & (jnp.where(is_west, zone_col, zone_col + ZONE) >= ZONE)
    zone_row = jnp.where((cells >= 0) & inside & (jnp.where(is_west, 0, zone_col) < ZONE), cells >> 8, -1)
    zone_row_out[...] = zone_row
    zone_col_out[...] = zone_col
    high, low = cell_place(packed(link_cell[...]))
    cell_high[...] = high
    cell_low[...] = low
    heads = sweep_and_gather(
        state, gains, cell_high, cell_low, (zone_row, zone_col), surface_out, heads_out, zone_out,
        cell_table, edge_ref, zone_ref,
    )
    build_message(
        out, 6, heads, nodes[...], (table[0:1, :], table[32:33, :]), (near[40:41, :], near[41:42, :])
    )
    put(out, 6, 3, paired(coef[...], coef[...]))
    put(out, 6, 4, beside(coef[...]))


def sweep_kernel(
    last, surface, near, far, gains_ref, cell_high, cell_low, zone_row, zone_col,
    table, nodes, surface_out, heads_out, zone_out, out, cell_table, edge_ref, zone_ref,
):
    state = jnp.concatenate(
        [
            tall_block(
                surface[:, block * 128 : block * 128 + 128], near, far, block * 4
            )
            for block in range(3)
        ],
        axis=1,
    )
    gains = [gains_ref[index] for index in range(6)]
    zone_place = None if last else (zone_row[...], zone_col[...])
    heads = sweep_and_gather(
        state, gains, cell_high, cell_low, zone_place, surface_out, heads_out, zone_out,
        cell_table, edge_ref, zone_ref,
    )
    build_message(
        out, 3 if last else 4, heads, nodes[...], (table[0:1, :], table[32:33, :]),
        (table[31:32, :], table[63:64, :]),
    )


def relayed(got, blocks):
    return jnp.concatenate(
        [got[pl.ds(partner_rows(blocks) + block, 16, stride=blocks), :] for block in (1, 2)], axis=0
    )


def relay_kernel(got, out):
    out[...] = relayed(got, 3)


def tile_kernel(
    first, last, got, surface, inverse, heads, zone, cell_high, hot, zone_row, zone_col, *rest
):
    rest = list(rest)
    blocks = 6 if first else 3 if last else 4
    if first:
        own_coef = low_halves(taken(got, 6, 3))
        zone_coef = taken(got, 6, 4)
    else:
        own_coef = rest.pop(0)[...]
        zone_coef = rest.pop(0)[...]
    surface_out = rest.pop(0)
    if not last:
        near, far = rest.pop(0), rest.pop(0)
    if first:
        rest.pop(0)[...] = own_coef
        rest.pop(0)[...] = zone_coef
    value_ref, zone_value_ref, row_ref = rest
    value_ref[...] = jnp.where(
        cell_high[...] >= 0, own_coef * (heads[...] - high_halves(taken(got, blocks, 0))), 0.0
    )
    row_ref[...] = jnp.where(cell_high[...] >= 0, jnp.bitwise_and(cell_high[...], 63), -1)
    lost = summed_by_columns(row_ref, value_ref, hot)
    left = surface[:, 0:128] - inverse[:, 0:128] * lost[:, 0:128]
    right = surface[:, 128:256] - inverse[:, 128:256] * lost[:, 128:256]
    surface_out[:, 0:128] = left
    surface_out[:, 128:256] = right
    if last:
        return
    zone_value_ref[...] = jnp.where(
        zone_row[...] >= 0, zone_coef * (zone[...] - taken(got, blocks, blocks - 1)), 0.0
    )
    lost = summed(zone_row, zone_col, zone_value_ref, 64, 2 * ZONE, by_low=True)
    lost = jnp.concatenate([lost, jnp.zeros((64, 128 - 2 * ZONE), F32)], axis=1)
    lane = iota((64, 128), 1)
    lost = jnp.where(
        lane < ZONE, lost,
        jnp.where(lane >= 128 - ZONE, pltpu.roll(lost, 128 - 2 * ZONE, 1), 0.0),
    )
    edge = surface[:, 256:384] - inverse[:, 256:384] * lost
    surface_out[:, 256:384] = edge
    top, bottom = strips([left, right, edge], 0), strips([left, right, edge], 60)
    near[0:12, :] = jnp.where(even(0), bottom, top)
    far[...] = jnp.where(even(0), top, bottom)
    if not first:
        near[16:48, :] = relayed(got, blocks)


def inflow_of(blocks, got, nodes, node_high, node_low, coef, value_ref):
    value_ref[...] = jnp.where(
        node_high[...] >= 0, coef[...] * (low_halves(taken(got, blocks, 0)) - nodes[...]), 0.0
    )
    return summed(node_high, node_low, value_ref, 64, 128)


def inflow_kernel(got, nodes, node_high, node_low, coef, out, value_ref):
    out[...] = inflow_of(4, got, nodes, node_high, node_low, coef, value_ref)


def last_kernel(
    got, surface, inverse, heads, zone, cell_high, hot, zone_row, zone_col, own_coef, zone_coef,
    nodes, node_high, node_low, coef, surface_out, inflow, value_ref, zone_value_ref, row_ref,
    node_value_ref, held, sent,
):
    tile_kernel(
        False, True, got, surface, inverse, heads, zone, cell_high, hot, zone_row, zone_col,
        own_coef, zone_coef, held, value_ref, zone_value_ref, row_ref,
    )
    copy = pltpu.make_async_copy(held, surface_out, sent)
    copy.start()
    inflow[...] = inflow_of(3, got, nodes, node_high, node_low, coef, node_value_ref)
    copy.wait()


def owner_kernel(
    first, last, got, nodes, node_high, node_low, coef, table, meets, classes, matrices, *rest
):
    blocks = 6 if first else 3 if last else 4
    rest = list(rest)
    relay = None if first else rest.pop(0)
    inflow = None if first else rest.pop(0)[...]
    if last:
        pipes_out, value_ref, ends_ref = rest
    else:
        table_out, nodes_out, value_ref, ends_ref = rest
    if inflow is None:
        inflow = inflow_of(blocks, got, nodes, node_high, node_low, coef, value_ref)
    balance = table[...] + inflow
    start = pl.multiple_of(row_col()[0] * (16 * blocks), 16)
    for half in range(2):
        ends_ref[half * 16 : half * 16 + 16, :] = got[
            pl.ds(start + 1 + half, 16, stride=blocks), :
        ]
    if first:
        ends_ref[32:64, :] = relayed(got, blocks)
    else:
        ends_ref[32:64, :] = relay[0:32, :] if last else relay[16:48, :]
    meet = meets[...]
    meet_high = jnp.bitwise_and(meet >> 7, 1) * 16 + (meet >> 8)
    meet_high = jnp.where(iota((8, 128), 0) < 2, meet_high + 32, meet_high)
    met = gathered(ends_ref, 64, meet_high, meet) * boundary_gain
    node_row = iota((32, 128), 0)
    parts = []
    for half in range(2):
        part = balance[half * 32 : half * 32 + 32]
        part = part + jnp.where(
            node_row == 0, met[half : half + 1],
            jnp.where(node_row == 31, met[2 + half : 3 + half], 0.0),
        )
        products = jnp.dot(
            matrices[...], part, precision=lax.Precision.HIGHEST, preferred_element_type=F32
        )
        kind = classes[half : half + 1, :]
        updated = jnp.zeros((32, 128), F32)
        for index in range(CLASSES):
            updated = jnp.where(kind == index, products[index * 32 : index * 32 + 32], updated)
        parts.append(updated)
    if last:
        pipes_out[:, 0:128] = parts[0]
        pipes_out[:, 128:256] = parts[1]
        return
    table_out[0:32, :] = parts[0]
    table_out[32:64, :] = parts[1]
    nodes_out[...] = gathered(table_out, 64, node_high[...], node_low[...])


def shape(*dims, dtype=F32):
    return jax.ShapeDtypeStruct(dims, dtype)


def call(kernel, inputs, outputs, scratch=(), space=pltpu.VMEM, flops=10**9, spaces=None):
    spaces = spaces or [pltpu.VMEM] * len(outputs)
    return pl.pallas_call(
        kernel,
        out_shape=outputs,
        in_specs=[pl.BlockSpec(memory_space=space)] * len(inputs),
        out_specs=[pl.BlockSpec(memory_space=out) for out in spaces],
        scratch_shapes=list(scratch),
        compiler_params=pltpu.CompilerParams(vmem_limit_bytes=16 << 20),
        cost_estimate=pl.CostEstimate(flops=flops, bytes_accessed=1 << 20, transcendentals=0),
    )(*inputs)


def copy_kernel(source, out):
    out[...] = source[...]


def swapped(near, far, dim, copied=None):
    sizes = lax.axis_size("row"), lax.axis_size("col")
    routes = [], []
    for row in range(sizes[0]):
        for col in range(sizes[1]):
            here = [row, col]
            partner = list(here)
            partner[dim] ^= 1
            other = list(here)
            other[dim] += 1 if here[dim] % 2 else -1
            if not 0 <= other[dim] < sizes[dim]:
                other = list(here)
                other[1 - dim] ^= 1
            for route, there in zip(routes, (partner, other)):
                route.append((row * sizes[1] + col, there[0] * sizes[1] + there[1]))
    if far is None:
        return lax.ppermute(near, ("row", "col"), routes[0])
    if copied == "near":
        (near,) = call(copy_kernel, (near,), [shape(*near.shape)])
    if copied == "far":
        (far,) = call(copy_kernel, (far,), [shape(*far.shape)])
    far = lax.ppermute(far, ("row", "col"), routes[1])
    return lax.ppermute(near, ("row", "col"), routes[0]), far


def body(
    surface_head, conduct_x, conduct_y, porosity, rainfall, pipe_head, pipe_class, pipe_up,
    pipe_down, pipe_matrices, link_cell, link_node, link_coef,
):
    link_cell = link_cell[0]
    uppers, lowers = pipe_up.reshape(2, 128), pipe_down.reshape(2, 128)
    classes = pipe_class.reshape(2, 128)
    matrices = pipe_matrices.reshape(CLASSES * 32, 32)
    ints = functools.partial(shape, dtype=jnp.int32)

    fields, near, far = call(
        start_kernel,
        [pltpu.with_memory_space_constraint(x, pltpu.HBM) for x in (
            surface_head, conduct_x, conduct_y, porosity, rainfall, pipe_head
        )],
        [shape(5, 64, 256), shape(48, 128), shape(40, 128)],
        [pltpu.VMEM((8, 256), F32), pltpu.SemaphoreType.DMA((6,))], space=pltpu.HBM,
    )
    near, far = swapped(near, far, 0, "near")
    link_node = link_node[:, 0, :]
    link_coef = link_coef[:, 0, :]
    table, nodes, node_high, node_low, coef, classes, matrices, meets = call(
        owner_start_kernel, (pipe_head, link_node, link_coef, classes, matrices, uppers, lowers),
        [shape(64, 128), shape(64, 128), ints(64, 128), ints(64, 128), shape(64, 128),
         ints(2, 128), shape(128, 32), ints(8, 128)],
    )
    near, far, nodes = lax.optimization_barrier((near, far, nodes))
    tall, sent = call(
        pack_cols_kernel, (near, far, fields, link_cell),
        [shape(5, 72, 256), shape(136, 128)],
    )
    sent, cells = lax.optimization_barrier((sent, link_cell))
    near_col, far_col = swapped(sent, sent, 1)
    (hot,) = call(columns_kernel, (cells,), [shape(8192, 256, dtype=BF16)])
    gather_scratch = [
        pltpu.VMEM((128, 128), F32), pltpu.VMEM((64, 128), F32), pltpu.VMEM((8, 128), F32)
    ]
    swept_shapes = [shape(64, 384), shape(64, 128), shape(128, 128)]
    (gains, inverse, cell_high, cell_low, zone_row, zone_col, surface, heads, zone, sent) = call(
        first_sweep_kernel,
        (tall, near_col, far_col, near, link_cell, table, nodes, coef),
        [shape(6, 72, 384), shape(64, 384), ints(64, 128), ints(64, 128), ints(128, 128),
         ints(128, 128), *swept_shapes, shape(768, 128)],
        gather_scratch,
    )
    sent, hot = lax.optimization_barrier((sent, hot))
    coefs = ()
    for step in range(STEPS):
        first, last = step == 0, step == STEPS - 1
        if step:
            surface, heads, zone, sent = call(
                functools.partial(sweep_kernel, last),
                (surface, near, far, gains, cell_high, cell_low, zone_row, zone_col,
                 table, nodes),
                [*swept_shapes, shape(384 if last else 512, 128)], gather_scratch,
            )
        got = lax.all_to_all(
            sent.reshape(128, 1, -1), ("row", "col"), split_axis=0, concat_axis=0, tiled=True
        ).reshape(-1, 128)
        tile_inputs = (surface, inverse, heads, zone, cell_high, hot, zone_row, zone_col, *coefs)
        owner_inputs = (nodes, node_high, node_low, coef, table, meets, classes, matrices)
        tile_scratch = [
            pltpu.VMEM((64, 128), F32), pltpu.VMEM((128, 128), F32), pltpu.VMEM((64, 128), jnp.int32)
        ]
        owner_scratch = [pltpu.VMEM((64, 128), F32), pltpu.VMEM((64, 128), F32)]
        if last:
            (relay,) = call(relay_kernel, (got,), [shape(32, 128)])
            relay = swapped(relay, None, 0)
            surface_out, inflow = call(
                last_kernel, (got, *tile_inputs, nodes, node_high, node_low, coef),
                [shape(64, 256), shape(64, 128)],
                tile_scratch + [
                    pltpu.VMEM((64, 128), F32), pltpu.VMEM((64, 256), F32), pltpu.SemaphoreType.DMA
                ],
                spaces=[pltpu.HBM, pltpu.VMEM],
            )
            (pipes_out,) = call(
                functools.partial(owner_kernel, False, True), (got, *owner_inputs, relay, inflow),
                [shape(32, 256)], owner_scratch,
            )
            return surface_out, pipes_out
        outputs = [shape(64, 384), shape(12 if first else 48, 128), shape(12, 128)]
        if first:
            outputs += [shape(64, 128), shape(128, 128)]
        surface, near, far, *new_coefs = call(
            functools.partial(tile_kernel, first, False), (got, *tile_inputs), outputs,
            tile_scratch,
        )
        near, far = swapped(near, far, 0, "far" if first else None)
        if not first:
            (inflow,) = call(
                inflow_kernel, (got, nodes, node_high, node_low, coef), [shape(64, 128)],
                owner_scratch[:1], flops=10**6,
            )
            owner_inputs += (near, inflow)
        table, nodes = call(
            functools.partial(owner_kernel, first, False), (got, *owner_inputs),
            [shape(64, 128), shape(64, 128)], owner_scratch,
        )
        if first:
            coefs = tuple(new_coefs)


def solution(mesh):
    placed = (
        P("row", "col"),
        P("row", "col"),
        P("row", "col"),
        P("row", "col"),
        P("row", "col"),
        P(None, ("row", "col")),
        P(("row", "col")),
        P(("row", "col")),
        P(("row", "col")),
        P(),
        P(("row", "col"), None, None),
        P(None, ("row", "col"), None),
        P(None, ("row", "col"), None),
    )
    return jax.shard_map(
        body,
        mesh=mesh,
        in_specs=placed,
        out_specs=(P("row", "col"), P(None, ("row", "col"))),
        check_vma=False,
    )
```

```python
import functools

import jax
import jax.numpy as jnp
from jax import lax
from jax.experimental import pallas as pl
from jax.experimental.pallas import tpu as pltpu
from jax.sharding import PartitionSpec as P

CLASSES = 4
SWEEPS = 4
STEPS = 3
F32 = jnp.float32
BF16 = jnp.bfloat16

boundary_gain = 0.5

HALO_ROWS = 4
HALO_COLS = 12
ZONE = 8
ENDS = (0, 32, 31, 63)


def iota(shape, dim):
    return lax.broadcasted_iota(jnp.int32, shape, dim)


def packed(x):
    return jnp.concatenate([x[:64], x[64:]], axis=1)


def low_halves(block):
    lane = iota((64, 128), 1)
    return jnp.where(lane < 64, block[:64], pltpu.roll(block[64:], 64, 1))


def high_halves(block):
    lane = iota((64, 128), 1)
    return jnp.where(lane < 64, pltpu.roll(block[:64], 64, 1), block[64:])


def paired(low, high):
    lane = iota((64, 128), 1)
    top = jnp.where(lane < 64, low, pltpu.roll(high, 64, 1))
    bottom = jnp.where(lane < 64, pltpu.roll(low, 64, 1), high)
    return jnp.concatenate([top, bottom], axis=0)


def beside(values):
    lane = iota((128, 128), 1)
    both = paired(values, values)
    return jnp.where(lane < 64, pltpu.roll(both, 1, 0), pltpu.roll(both, 127, 0))


def gathered(table_ref, rows, high, low):
    low = jnp.bitwise_and(low, 127)
    tiles = []
    for start in range(0, high.shape[0], 8):
        tile_high, tile_low = high[start : start + 8], low[start : start + 8]
        found = jnp.zeros((8, 128), F32)
        for row in range(rows):
            line = jnp.broadcast_to(table_ref[row : row + 1, :], (8, 128))
            values = jnp.take_along_axis(line, tile_low, axis=1)
            found = jnp.where(tile_high == row, values, found)
        tiles.append(found)
    return jnp.concatenate(tiles, axis=0) if len(tiles) > 1 else tiles[0]


def gathered_by_product(table, high_ref, low_ref, tiles):
    coarse = table.astype(BF16)
    fine = (table - coarse.astype(F32)).astype(BF16)
    parts = jnp.concatenate([coarse, fine], axis=1)
    row_iota = iota((128, 128), 0)
    high_iota = row_iota.astype(F32).astype(BF16)
    one, zero = jnp.ones((128, 128), BF16), jnp.zeros((128, 128), BF16)
    found = []
    for start in range(0, 8 * tiles, 8):
        high = high_ref[start : start + 8, :].astype(F32)
        low = low_ref[start : start + 8, :]
        hot = jnp.concatenate(
            [
                jnp.where(repeated(high[j : j + 1], 128) == high_iota, one, zero)
                for j in range(8)
            ],
            axis=1,
        )
        lines = lax.dot_general(
            parts, hot, (((0,), (0,)), ((), ())), preferred_element_type=F32
        )
        lines = lines[:128] + lines[128:]
        for j in range(8):
            line = jnp.where(
                row_iota == low[j : j + 1], lines[:, j * 128 : j * 128 + 128], 0.0
            )
            found.append(jnp.sum(line, axis=0, keepdims=True))
    return jnp.concatenate(found, axis=0)


def repeated(line, size):
    block = jnp.broadcast_to(line, (16, 128)).astype(BF16)
    return jnp.concatenate([block] * (size // 16), axis=0) if size > 16 else block


def summed(high_ref, low_ref, value_ref, high_size, low_size, by_low=False):
    refs, sizes = (high_ref, low_ref), (high_size, low_size)
    bearer = 1 if by_low else 0
    iotas = [iota((size, 128), 0).astype(F32).astype(BF16) for size in sizes]
    zeros = [jnp.zeros((size, 128), BF16) for size in sizes]
    one = jnp.ones((sizes[1 - bearer], 128), BF16)
    total = None
    for start in range(0, high_ref.shape[0], 8):
        places = [ref[start : start + 8, :].astype(F32) for ref in refs]
        value = value_ref[start : start + 8, :]
        coarse = value.astype(BF16).astype(F32)
        fine = value - coarse
        size, zero = sizes[bearer], zeros[bearer]
        coarse_hot, fine_hot, plain_hot = [], [], []
        for j in range(8):
            same = [
                repeated(places[side][j : j + 1], sizes[side]) == iotas[side] for side in range(2)
            ]
            coarse_hot.append(jnp.where(same[bearer], repeated(coarse[j : j + 1], size), zero))
            fine_hot.append(jnp.where(same[bearer], repeated(fine[j : j + 1], size), zero))
            plain_hot.append(jnp.where(same[1 - bearer], one, zeros[1 - bearer]))
        value_hot = jnp.concatenate(
            [jnp.concatenate(coarse_hot, axis=1), jnp.concatenate(fine_hot, axis=1)], axis=0
        )
        plain_hot = jnp.concatenate(plain_hot, axis=1)
        sides = (plain_hot, value_hot) if by_low else (value_hot, plain_hot)
        product = lax.dot_general(
            *sides, (((1,), (1,)), ((), ())), preferred_element_type=F32
        )
        total = product if total is None else total + product
    if by_low:
        return total[:, :low_size] + total[:, low_size:]
    return total[:high_size] + total[high_size:]


def summed_by_columns(row_ref, value_ref, hot_ref):
    row_iota = iota((64, 128), 0).astype(F32).astype(BF16)
    zero = jnp.zeros((64, 128), BF16)
    total = jnp.zeros((128, 256), F32)
    for start in range(0, 64, 8):
        rows = row_ref[start : start + 8, :].astype(F32)
        value = value_ref[start : start + 8, :]
        coarse = value.astype(BF16).astype(F32)
        fine = value - coarse
        coarse_hot, fine_hot = [], []
        for j in range(8):
            same = repeated(rows[j : j + 1], 64) == row_iota
            coarse_hot.append(jnp.where(same, repeated(coarse[j : j + 1], 64), zero))
            fine_hot.append(jnp.where(same, repeated(fine[j : j + 1], 64), zero))
        value_hot = jnp.concatenate(
            [jnp.concatenate(coarse_hot, axis=1), jnp.concatenate(fine_hot, axis=1)], axis=0
        )
        total = total + jnp.dot(
            value_hot, hot_ref[start * 128 : start * 128 + 1024, :], preferred_element_type=F32
        )
    return total[:64] + total[64:]


def columns_kernel(link_cell, hot):
    cols = jnp.bitwise_and(packed(link_cell[...]), 255).astype(F32).T
    lane = iota((128, 256), 1).astype(F32)
    for j in range(64):
        same = jnp.broadcast_to(cols[:, j : j + 1], (128, 256)) == lane
        hot[j * 128 : j * 128 + 128, :] = jnp.where(same, 1.0, 0.0).astype(BF16)


def cell_place(cell):
    high = jnp.where(
        cell >= 0, jnp.bitwise_and(cell >> 7, 1) * 64 + (cell >> 8), -1
    )
    return high, jnp.bitwise_and(cell, 127)


def node_place(node):
    high = jnp.where(
        node >= 0, jnp.bitwise_and(node >> 7, 1) * 32 + (node >> 8), -1
    )
    return high, jnp.bitwise_and(node, 127)


def pipe_table(state):
    return jnp.concatenate([state[:, :128], state[:, 128:]], axis=0)


def strips(blocks, start):
    return jnp.concatenate([block[start : start + HALO_ROWS] for block in blocks], axis=0)


def row_col():
    return lax.axis_index("row"), lax.axis_index("col")


def even(dim):
    return jnp.bitwise_and(row_col()[dim], 1) == 0


def start_kernel(
    surface, cond_x, cond_y, porosity, rainfall, pipes, fields, near, far, tips, arrived
):
    copies = [
        pltpu.make_async_copy(source, fields.at[index], arrived.at[index])
        for index, source in enumerate((surface, cond_x, cond_y, porosity, rainfall))
    ]
    copies.append(pltpu.make_async_copy(pipes.at[24:32, :], tips, arrived.at[5]))
    for copy in copies:
        copy.start()
    for copy in copies:
        copy.wait()
    fields[3] = 1.0 / fields[3]
    for index in range(5):
        halves = [fields[index, :, 0:128], fields[index, :, 128:256]]
        top, bottom = strips(halves, 0), strips(halves, 60)
        near[pl.ds(index * 8, 8), :] = jnp.where(even(0), bottom, top)
        far[pl.ds(index * 8, 8), :] = jnp.where(even(0), top, bottom)
    near[40:48, :] = jnp.concatenate(
        [tips[7:8, 0:128], tips[7:8, 128:256], jnp.zeros((6, 128), F32)], axis=0
    )


def tall_block(block, near, far, start):
    near, far = near[start : start + 4, :], far[start : start + 4, :]
    over = jnp.where(even(0), far, near)
    under = jnp.where(even(0), near, far)
    over = jnp.where(row_col()[0] > 0, over, 0.0)
    under = jnp.where(row_col()[0] < 7, under, 0.0)
    return jnp.concatenate([block, under, over], axis=0)


def pack_cols_kernel(near, far, fields, link_cell, tall_out, out):
    lane = iota((72, 128), 1)
    message = jnp.zeros((72, 128), F32)
    for index in range(5):
        tall = [
            tall_block(
                fields[index, :, half * 128 : half * 128 + 128], near, far,
                index * 8 + half * 4,
            )
            for half in range(2)
        ]
        tall_out[index, :, 0:128] = tall[0]
        tall_out[index, :, 128:256] = tall[1]
        edges = jnp.where(
            lane < HALO_COLS, tall[0], jnp.where(lane >= 128 - HALO_COLS, tall[1], 0.0)
        )
        if index:
            edges = pltpu.roll(edges, index * 2 * HALO_COLS, 1)
        message = message + edges
    out[0:72, :] = message
    out[72:136, :] = packed(link_cell[...]).astype(F32)


def owner_start_kernel(
    pipes, link_node, link_coef, kinds, laws, uppers, lowers, table, nodes, node_high, node_low,
    coef, classes, matrices, meets,
):
    meets[...] = jnp.concatenate(
        [uppers[...], lowers[...], jnp.zeros((4, 128), jnp.int32)], axis=0
    )
    classes[...] = kinds[...]
    matrices[...] = laws[...]
    table[...] = pipe_table(pipes[...])
    high, low = node_place(packed(link_node[...]))
    node_high[...] = high
    node_low[...] = low
    coef[...] = packed(link_coef[...])
    nodes[...] = gathered(table, 64, high, low)


def swept(state, gains):
    def once(_, w):
        return (
            gains[0] * w
            + gains[1] * pltpu.roll(w, 1, 0)
            + gains[2] * pltpu.roll(w, 71, 0)
            + gains[3] * pltpu.roll(w, 1, 1)
            + gains[4] * pltpu.roll(w, 383, 1)
            + gains[5]
        )

    for i in range(SWEEPS):
        state = once(i, state)
    return state


def put(out, blocks, index, value):
    out[pl.ds(index, 128, stride=blocks), :] = value


def taken(got, blocks, index):
    return got[pl.ds(index, 128, stride=blocks), :]


def build_message(out, blocks, heads, nodes, own_ends, other_ends):
    put(out, blocks, 0, paired(heads, nodes))
    own_rows = (iota((128, 128), 0) >> 4) == row_col()[0]
    for half in range(2):
        own = jnp.broadcast_to(own_ends[half], (128, 128))
        other = jnp.broadcast_to(other_ends[half], (128, 128))
        put(out, blocks, 1 + half, jnp.where(own_rows, own, other))
    if blocks > 3:
        put(out, blocks, blocks - 1, beside(nodes))


def partner_rows(blocks):
    return pl.multiple_of((row_col()[0] ^ 1) * (16 * blocks), 16)


def zone_heads(edge, zone_place, edge_ref, zone_ref):
    lane = iota((64, 128), 1)
    edge_ref[...] = jnp.where(lane < ZONE, edge, pltpu.roll(edge, 2 * ZONE, 1))
    lane8 = iota((8, 128), 1)
    table = jnp.zeros((8, 128), F32)
    for s in range(8):
        line = edge_ref[pl.ds(s, 8, stride=8), :]
        if s:
            line = pltpu.roll(line, s * 16, 1)
        table = jnp.where((lane8 >> 4) == s, line, table)
    zone_ref[...] = table
    zone_row, zone_col = zone_place
    high = jnp.where(zone_row >= 0, zone_row >> 3, -1)
    low = jnp.bitwise_and(zone_row, 7) * 16 + zone_col
    return gathered(zone_ref, 8, high, low)


def sweep_and_gather(
    state, gains, cell_high, cell_low, zone_place, surface_out, heads_out, zone_out, cell_table,
    edge_ref, zone_ref,
):
    state = swept(state, gains)
    surface_out[...] = state[:64]
    cell_table[0:64, :] = state[:64, 0:128]
    cell_table[64:128, :] = state[:64, 128:256]
    tiles = 4 if zone_place is None else 5
    heads = jnp.concatenate(
        [
            gathered_by_product(cell_table[...], cell_high, cell_low, tiles),
            gathered(cell_table, 128, cell_high[8 * tiles :, :], cell_low[8 * tiles :, :]),
        ],
        axis=0,
    )
    heads_out[...] = heads
    if zone_place is not None:
        zone_out[...] = zone_heads(state[:64, 256:384], zone_place, edge_ref, zone_ref)
    return heads


def first_sweep_kernel(
    tall, near_col, far_col, near, link_cell, table, nodes, coef,
    gains_out, inverse_out, cell_high, cell_low, zone_row_out, zone_col_out, surface_out, heads_out,
    zone_out, out, cell_table, edge_ref, zone_ref,
):
    lane = iota((72, 128), 1)
    wide = []
    from_west = jnp.where(even(1), far_col[...], near_col[...])
    from_east = jnp.where(even(1), near_col[...], far_col[...])
    for index in range(5):
        west = jnp.where(row_col()[1] > 0, from_west[0:72, :], 0.0)
        east = jnp.where(row_col()[1] < 15, from_east[0:72, :], 0.0)
        if index:
            west = pltpu.roll(west, 128 - index * 2 * HALO_COLS, 1)
            east = pltpu.roll(east, 128 - index * 2 * HALO_COLS, 1)
        edge = jnp.where(
            lane < HALO_COLS, east, jnp.where(lane >= 128 - HALO_COLS, west, 0.0)
        )
        wide.append(jnp.concatenate([tall[index], edge], axis=1))
    state, cond_x, cond_y, inverse, rainfall = wide
    north = pltpu.roll(cond_x, 1, 0)
    west = pltpu.roll(cond_y, 1, 1)
    gains = [
        1.0 - (north + cond_x + west + cond_y) * inverse,
        north * inverse, cond_x * inverse, west * inverse, cond_y * inverse, rainfall,
    ]
    for index, gain in enumerate(gains):
        gains_out[index] = gain
    inverse_out[...] = inverse[:64]
    cells = paired(from_west[72:136, :], from_east[72:136, :]).astype(jnp.int32)
    col = jnp.bitwise_and(cells, 255)
    is_west = iota((128, 128), 1) < 64
    zone_col = jnp.where(is_west, col - (256 - 2 * ZONE), col)
    inside = (zone_col >= 0) & (zone_col < 2 * ZONE)
    inside = inside & (jnp.where(is_west, zone_col, zone_col + ZONE) >= ZONE)
    zone_row = jnp.where((cells >= 0) & inside & (jnp.where(is_west, 0, zone_col) < ZONE), cells >> 8, -1)
    zone_row_out[...] = zone_row
    zone_col_out[...] = zone_col
    high, low = cell_place(packed(link_cell[...]))
    cell_high[...] = high
    cell_low[...] = low
    heads = sweep_and_gather(
        state, gains, cell_high, cell_low, (zone_row, zone_col), surface_out, heads_out, zone_out,
        cell_table, edge_ref, zone_ref,
    )
    build_message(
        out, 6, heads, nodes[...], (table[0:1, :], table[32:33, :]), (near[40:41, :], near[41:42, :])
    )
    put(out, 6, 3, paired(coef[...], coef[...]))
    put(out, 6, 4, beside(coef[...]))


def sweep_kernel(
    last, surface, near, far, gains_ref, cell_high, cell_low, zone_row, zone_col,
    table, nodes, surface_out, heads_out, zone_out, out, cell_table, edge_ref, zone_ref,
):
    state = jnp.concatenate(
        [
            tall_block(
                surface[:, block * 128 : block * 128 + 128], near, far, block * 4
            )
            for block in range(3)
        ],
        axis=1,
    )
    gains = [gains_ref[index] for index in range(6)]
    zone_place = None if last else (zone_row[...], zone_col[...])
    heads = sweep_and_gather(
        state, gains, cell_high, cell_low, zone_place, surface_out, heads_out, zone_out,
        cell_table, edge_ref, zone_ref,
    )
    build_message(
        out, 3 if last else 4, heads, nodes[...], (table[0:1, :], table[32:33, :]),
        (table[31:32, :], table[63:64, :]),
    )


def relayed(got, blocks):
    return jnp.concatenate(
        [got[pl.ds(partner_rows(blocks) + block, 16, stride=blocks), :] for block in (1, 2)], axis=0
    )


def relay_kernel(got, out):
    out[...] = relayed(got, 3)


def tile_kernel(
    first, last, got, surface, inverse, heads, zone, cell_high, hot, zone_row, zone_col, *rest
):
    rest = list(rest)
    blocks = 6 if first else 3 if last else 4
    if first:
        own_coef = low_halves(taken(got, 6, 3))
        zone_coef = taken(got, 6, 4)
    else:
        own_coef = rest.pop(0)[...]
        zone_coef = rest.pop(0)[...]
    surface_out = rest.pop(0)
    if not last:
        near, far = rest.pop(0), rest.pop(0)
    if first:
        rest.pop(0)[...] = own_coef
        rest.pop(0)[...] = zone_coef
    value_ref, zone_value_ref, row_ref = rest
    value_ref[...] = jnp.where(
        cell_high[...] >= 0, own_coef * (heads[...] - high_halves(taken(got, blocks, 0))), 0.0
    )
    row_ref[...] = jnp.where(cell_high[...] >= 0, jnp.bitwise_and(cell_high[...], 63), -1)
    lost = summed_by_columns(row_ref, value_ref, hot)
    left = surface[:, 0:128] - inverse[:, 0:128] * lost[:, 0:128]
    right = surface[:, 128:256] - inverse[:, 128:256] * lost[:, 128:256]
    surface_out[:, 0:128] = left
    surface_out[:, 128:256] = right
    if last:
        return
    zone_value_ref[...] = jnp.where(
        zone_row[...] >= 0, zone_coef * (zone[...] - taken(got, blocks, blocks - 1)), 0.0
    )
    lost = summed(zone_row, zone_col, zone_value_ref, 64, 2 * ZONE, by_low=True)
    lost = jnp.concatenate([lost, jnp.zeros((64, 128 - 2 * ZONE), F32)], axis=1)
    lane = iota((64, 128), 1)
    lost = jnp.where(
        lane < ZONE, lost,
        jnp.where(lane >= 128 - ZONE, pltpu.roll(lost, 128 - 2 * ZONE, 1), 0.0),
    )
    edge = surface[:, 256:384] - inverse[:, 256:384] * lost
    surface_out[:, 256:384] = edge
    top, bottom = strips([left, right, edge], 0), strips([left, right, edge], 60)
    near[0:12, :] = jnp.where(even(0), bottom, top)
    far[...] = jnp.where(even(0), top, bottom)
    if not first:
        near[16:48, :] = relayed(got, blocks)


def inflow_of(blocks, got, nodes, node_high, node_low, coef, value_ref):
    value_ref[...] = jnp.where(
        node_high[...] >= 0, coef[...] * (low_halves(taken(got, blocks, 0)) - nodes[...]), 0.0
    )
    return summed(node_high, node_low, value_ref, 64, 128)


def inflow_kernel(got, nodes, node_high, node_low, coef, out, value_ref):
    out[...] = inflow_of(4, got, nodes, node_high, node_low, coef, value_ref)


def owner_kernel(
    first, last, got, nodes, node_high, node_low, coef, table, meets, classes, matrices, *rest
):
    blocks = 6 if first else 3 if last else 4
    rest = list(rest)
    relay = None if first else rest.pop(0)
    inflow = None if first or last else rest.pop(0)[...]
    if last:
        pipes_out, value_ref, ends_ref = rest
    else:
        table_out, nodes_out, value_ref, ends_ref = rest
    if inflow is None:
        inflow = inflow_of(blocks, got, nodes, node_high, node_low, coef, value_ref)
    balance = table[...] + inflow
    start = pl.multiple_of(row_col()[0] * (16 * blocks), 16)
    for half in range(2):
        ends_ref[half * 16 : half * 16 + 16, :] = got[
            pl.ds(start + 1 + half, 16, stride=blocks), :
        ]
    if first:
        ends_ref[32:64, :] = relayed(got, blocks)
    else:
        ends_ref[32:64, :] = relay[0:32, :] if last else relay[16:48, :]
    meet = meets[...]
    meet_high = jnp.bitwise_and(meet >> 7, 1) * 16 + (meet >> 8)
    meet_high = jnp.where(iota((8, 128), 0) < 2, meet_high + 32, meet_high)
    met = gathered(ends_ref, 64, meet_high, meet) * boundary_gain
    node_row = iota((32, 128), 0)
    parts = []
    for half in range(2):
        part = balance[half * 32 : half * 32 + 32]
        part = part + jnp.where(
            node_row == 0, met[half : half + 1],
            jnp.where(node_row == 31, met[2 + half : 3 + half], 0.0),
        )
        products = jnp.dot(
            matrices[...], part, precision=lax.Precision.HIGHEST, preferred_element_type=F32
        )
        kind = classes[half : half + 1, :]
        updated = jnp.zeros((32, 128), F32)
        for index in range(CLASSES):
            updated = jnp.where(kind == index, products[index * 32 : index * 32 + 32], updated)
        parts.append(updated)
    if last:
        pipes_out[:, 0:128] = parts[0]
        pipes_out[:, 128:256] = parts[1]
        return
    table_out[0:32, :] = parts[0]
    table_out[32:64, :] = parts[1]
    nodes_out[...] = gathered(table_out, 64, node_high[...], node_low[...])


def shape(*dims, dtype=F32):
    return jax.ShapeDtypeStruct(dims, dtype)


def call(kernel, inputs, outputs, scratch=(), space=pltpu.VMEM, flops=10**9):
    vmem = pl.BlockSpec(memory_space=pltpu.VMEM)
    return pl.pallas_call(
        kernel,
        out_shape=outputs,
        in_specs=[pl.BlockSpec(memory_space=space)] * len(inputs),
        out_specs=[vmem] * len(outputs),
        scratch_shapes=list(scratch),
        compiler_params=pltpu.CompilerParams(vmem_limit_bytes=16 << 20),
        cost_estimate=pl.CostEstimate(flops=flops, bytes_accessed=1 << 20, transcendentals=0),
    )(*inputs)


def copy_kernel(source, out):
    out[...] = source[...]


def swapped(near, far, dim, copied=None):
    sizes = lax.axis_size("row"), lax.axis_size("col")
    routes = [], []
    for row in range(sizes[0]):
        for col in range(sizes[1]):
            here = [row, col]
            partner = list(here)
            partner[dim] ^= 1
            other = list(here)
            other[dim] += 1 if here[dim] % 2 else -1
            if not 0 <= other[dim] < sizes[dim]:
                other = list(here)
                other[1 - dim] ^= 1
            for route, there in zip(routes, (partner, other)):
                route.append((row * sizes[1] + col, there[0] * sizes[1] + there[1]))
    if far is None:
        return lax.ppermute(near, ("row", "col"), routes[0])
    if copied == "near":
        (near,) = call(copy_kernel, (near,), [shape(*near.shape)])
    if copied == "far":
        (far,) = call(copy_kernel, (far,), [shape(*far.shape)])
    far = lax.ppermute(far, ("row", "col"), routes[1])
    return lax.ppermute(near, ("row", "col"), routes[0]), far


def body(
    surface_head, conduct_x, conduct_y, porosity, rainfall, pipe_head, pipe_class, pipe_up,
    pipe_down, pipe_matrices, link_cell, link_node, link_coef,
):
    link_cell = link_cell[0]
    uppers, lowers = pipe_up.reshape(2, 128), pipe_down.reshape(2, 128)
    classes = pipe_class.reshape(2, 128)
    matrices = pipe_matrices.reshape(CLASSES * 32, 32)
    ints = functools.partial(shape, dtype=jnp.int32)

    fields, near, far = call(
        start_kernel,
        [pltpu.with_memory_space_constraint(x, pltpu.HBM) for x in (
            surface_head, conduct_x, conduct_y, porosity, rainfall, pipe_head
        )],
        [shape(5, 64, 256), shape(48, 128), shape(40, 128)],
        [pltpu.VMEM((8, 256), F32), pltpu.SemaphoreType.DMA((6,))], space=pltpu.HBM,
    )
    near, far = swapped(near, far, 0, "near")
    link_node = link_node[:, 0, :]
    link_coef = link_coef[:, 0, :]
    table, nodes, node_high, node_low, coef, classes, matrices, meets = call(
        owner_start_kernel, (pipe_head, link_node, link_coef, classes, matrices, uppers, lowers),
        [shape(64, 128), shape(64, 128), ints(64, 128), ints(64, 128), shape(64, 128),
         ints(2, 128), shape(128, 32), ints(8, 128)],
    )
    near, far, nodes = lax.optimization_barrier((near, far, nodes))
    tall, sent = call(
        pack_cols_kernel, (near, far, fields, link_cell),
        [shape(5, 72, 256), shape(136, 128)],
    )
    sent, cells = lax.optimization_barrier((sent, link_cell))
    near_col, far_col = swapped(sent, sent, 1)
    (hot,) = call(columns_kernel, (cells,), [shape(8192, 256, dtype=BF16)])
    gather_scratch = [
        pltpu.VMEM((128, 128), F32), pltpu.VMEM((64, 128), F32), pltpu.VMEM((8, 128), F32)
    ]
    swept_shapes = [shape(64, 384), shape(64, 128), shape(128, 128)]
    (gains, inverse, cell_high, cell_low, zone_row, zone_col, surface, heads, zone, sent) = call(
        first_sweep_kernel,
        (tall, near_col, far_col, near, link_cell, table, nodes, coef),
        [shape(6, 72, 384), shape(64, 384), ints(64, 128), ints(64, 128), ints(128, 128),
         ints(128, 128), *swept_shapes, shape(768, 128)],
        gather_scratch,
    )
    sent, hot = lax.optimization_barrier((sent, hot))
    coefs = ()
    for step in range(STEPS):
        first, last = step == 0, step == STEPS - 1
        if step:
            surface, heads, zone, sent = call(
                functools.partial(sweep_kernel, last),
                (surface, near, far, gains, cell_high, cell_low, zone_row, zone_col,
                 table, nodes),
                [*swept_shapes, shape(384 if last else 512, 128)], gather_scratch,
            )
        got = lax.all_to_all(
            sent.reshape(128, 1, -1), ("row", "col"), split_axis=0, concat_axis=0, tiled=True
        ).reshape(-1, 128)
        tile_inputs = (surface, inverse, heads, zone, cell_high, hot, zone_row, zone_col, *coefs)
        owner_inputs = (nodes, node_high, node_low, coef, table, meets, classes, matrices)
        tile_scratch = [
            pltpu.VMEM((64, 128), F32), pltpu.VMEM((128, 128), F32), pltpu.VMEM((64, 128), jnp.int32)
        ]
        owner_scratch = [pltpu.VMEM((64, 128), F32), pltpu.VMEM((64, 128), F32)]
        if last:
            (relay,) = call(relay_kernel, (got,), [shape(32, 128)])
            relay = swapped(relay, None, 0)
            (surface_out,) = call(
                functools.partial(tile_kernel, False, True), (got, *tile_inputs), [shape(64, 256)],
                tile_scratch,
            )
            (pipes_out,) = call(
                functools.partial(owner_kernel, False, True), (got, *owner_inputs, relay),
                [shape(32, 256)], owner_scratch,
            )
            return surface_out, pipes_out
        outputs = [shape(64, 384), shape(12 if first else 48, 128), shape(12, 128)]
        if first:
            outputs += [shape(64, 128), shape(128, 128)]
        surface, near, far, *new_coefs = call(
            functools.partial(tile_kernel, first, False), (got, *tile_inputs), outputs,
            tile_scratch,
        )
        near, far = swapped(near, far, 0, "far" if first else None)
        if not first:
            (inflow,) = call(
                inflow_kernel, (got, nodes, node_high, node_low, coef), [shape(64, 128)],
                owner_scratch[:1], flops=10**6,
            )
            owner_inputs += (near, inflow)
        table, nodes = call(
            functools.partial(owner_kernel, first, False), (got, *owner_inputs),
            [shape(64, 128), shape(64, 128)], owner_scratch,
        )
        if first:
            coefs = tuple(new_coefs)


def solution(mesh):
    placed = (
        P("row", "col"),
        P("row", "col"),
        P("row", "col"),
        P("row", "col"),
        P("row", "col"),
        P(None, ("row", "col")),
        P(("row", "col")),
        P(("row", "col")),
        P(("row", "col")),
        P(),
        P(("row", "col"), None, None),
        P(None, ("row", "col"), None),
        P(None, ("row", "col"), None),
    )
    return jax.shard_map(
        body,
        mesh=mesh,
        in_specs=placed,
        out_specs=(P("row", "col"), P(None, ("row", "col"))),
        check_vma=False,
    )
```
